512 devices in a mesh: region: 16 (over z), slab: 32 (over x, y, core).
Axes of the slice: x: 4, y: 4, z: 16, core: 2. Of those that a mesh axis runs over, the one named last changes fastest.
Arguments:
- records: bfloat16 [16384, 4096], P('region', 'slab'), may hold values from -6 to 6
- first_station: int32 [65536], P(('region', 'slab')), may hold values from 0 to 1023
- second_region: int32 [65536, 1], P(('region', 'slab')), may hold values from 0 to 15; in each aligned block of 128 rows (0 to 127, 128 to 255, ...) at most 16 rows name the same one
- second_station: int32 [65536], P(('region', 'slab')), may hold values from 0 to 1023
Outputs:
- stacks: bfloat16 [65536, 2048], P(('region', 'slab'))
The draws below stay inside these ranges and needn't reach their ends.
Inputs may be any that keep to these rules, and one draw needn't show every extreme that they name: `second_region`: no region is named by more than 16 pairs of one device.
All inputs are finite; a program needn't handle non-finite values.
Results may differ from the reference program's by a relative error of at most 0.0077.
Values may be sent and summed in bfloat16 or wider, within the bound.
A program may use at most 64 MiB of HBM per device.

```python
import math
import jax
import jax.numpy as jnp
import numpy as np
from jax import lax

NFFT = 2048
BINS = 1024
SEG = 2
HALF = 4
PAIR_DEV = 128
CAP = 16
STA_REG = 1024
STATIONS = 16384
PAIRS = 65536
N_REGION = 16
N_SLAB = 32


def plant(drawn, key, least, high):
    longest = drawn.shape.index(max(drawn.shape))
    spots = []
    for shift in (0, 1):
        where = [jax.random.randint(jax.random.fold_in(key, axis), (), 0, length) for axis, length in enumerate(drawn.shape)]
        where[longest] = (where[longest] + shift) % drawn.shape[longest]
        spots.append(tuple(where))
    return drawn.at[spots[0]].set(least).at[spots[1]].set(high)


def level_of(own_key, dims, pieces, smallest, top_value):
    loudness, own = 1.0, jax.random.fold_in(own_key, 6)
    for dim, parts in pieces:
        steps = jnp.exp(jax.random.uniform(jax.random.fold_in(own, dim), (parts,), jnp.float32, smallest / len(pieces), top_value / len(pieces)))
        loudness = loudness * jnp.repeat(steps, dims[dim] // parts).reshape([-1 if axis == dim else 1 for axis in range(len(dims))])
    return loudness


def routed_block(stream_key, own, number, rows, count, top, most, skew):
    order = jax.random.permutation(stream_key, count)
    heavy_load, common = load_shares(count, rows * top, most, skew, True), load_shares(count, rows * top, most, skew, False)
    places = jnp.arange(count)

    def named(tallies, rotation):
        used = int((tallies > 0).sum())
        fixed = max(1, used // 4)
        passed = fixed + (places - fixed + rotation * (used - fixed)) % max(1, count - fixed)
        return jnp.zeros((count,), jnp.int32).at[order[jnp.where(places < fixed, places, passed)]].set(jnp.asarray(tallies, jnp.int32))

    tallies = jnp.where(number % 4 == 0, named(heavy_load, number // 4), named(common, number - number // 4 - 1))
    mixed = jax.random.permutation(jax.random.fold_in(own, 3), count)
    donor, sink = mixed[0:count // 2 * 2:2], mixed[1:count // 2 * 2:2]
    slack = jnp.minimum(tallies[donor] - 1, most - tallies[sink]) // 2
    slack = jnp.where((donor == order[0]) | (sink == order[0]) | (tallies[sink] == 0), 0, jnp.maximum(slack, 0))
    passed = jax.random.randint(jax.random.fold_in(own, 4), (count // 2,), 0, 1 << 20) % (slack + 1)
    tallies = tallies.at[donor].add(-passed).at[sink].add(passed)
    labels = jnp.searchsorted(jnp.cumsum(tallies), jnp.arange(rows * top), side="right").astype(jnp.int32)
    grid = labels.reshape(top, rows).T
    grid = grid[jax.random.permutation(jax.random.fold_in(own, 1), rows)]
    rotation = jax.random.randint(jax.random.fold_in(own, 2), (rows, 1), 0, top)
    return jnp.take_along_axis(grid, (jnp.arange(top)[None, :] + rotation) % top, axis=1)


def load_shares(amount, total, bound, lean, full):
    portions = [(1 << 20) // math.isqrt(standing ** lean) + 1 for standing in range(1, amount + 1)]
    largest = bound if full else min(bound, max(-(-total // amount), total * portions[0] // sum(portions)))
    least = 1 if total - largest >= amount - 1 else 0
    holding, rest = [largest] + [least] * (amount - 1), total - largest - least * (amount - 1)
    while rest > 0:
        free = [i for i in range(1, amount) if holding[i] < largest] or [i for i in range(1, amount) if holding[i] < bound]
        whole, remaining = sum([portions[i] for i in free]), rest
        for i in free:
            extra = min(bound - holding[i], max(1, remaining * portions[i] // whole), rest)
            holding[i] = holding[i] + extra
            rest = rest - extra
    return np.array(holding)


def bell_draw(key, extent, width, limit, split=(), kind=jnp.bfloat16):
    result = jax.random.normal(key, extent, jnp.float32) * width
    if len(split) > 0:
        result = level_of(key, extent, split, -0.22, 0.18) * result
    return jnp.clip(result, min=-limit, max=limit).astype(kind)


def setup_inputs(seed: int = 0) -> dict:
    streams_of = jax.random.split(jax.random.key(seed), 5)
    records = bell_draw(streams_of[0], (STATIONS, SEG * NFFT), 1.0, 6.0, ((0, 16), (1, 32)))
    first_station = plant(jax.random.randint(streams_of[1], (PAIRS,), 0, STA_REG), jax.random.fold_in(streams_of[1], 1), 0, STA_REG - 1).astype(jnp.int32)
    second_region_keys = jax.random.split(jax.random.fold_in(streams_of[2], 1), PAIRS // PAIR_DEV)
    second_region_turns = jax.random.permutation(jax.random.fold_in(streams_of[2], 3), PAIRS // PAIR_DEV)
    second_region = jax.vmap(lambda own, number: routed_block(jax.random.fold_in(streams_of[2], 2), own, number, PAIR_DEV, N_REGION, 1, CAP, 2))(second_region_keys, second_region_turns).reshape((PAIRS, 1))
    second_station = plant(jax.random.randint(streams_of[3], (PAIRS,), 0, STA_REG), jax.random.fold_in(streams_of[3], 1), 0, STA_REG - 1).astype(jnp.int32)
    return dict(records=records, first_station=first_station, second_region=second_region, second_station=second_station)


def dft_table():
    sample = jnp.arange(NFFT, dtype=jnp.int32)[:, None]
    frequency = jnp.arange(BINS, dtype=jnp.int32)[None, :]
    phase = (sample * frequency % NFFT).astype(jnp.float32) * (2.0 * math.pi / NFFT)
    return jnp.concatenate([jnp.cos(phase), -jnp.sin(phase)], axis=1).astype(jnp.bfloat16)

def whitened(traces):
    count = traces.shape[0]
    signal = traces.astype(jnp.float32).reshape(count * SEG, NFFT)
    signal = signal - lax.optimization_barrier(jnp.mean(signal, axis=1, keepdims=True))
    position = jnp.arange(NFFT, dtype=jnp.int32).astype(jnp.float32)
    taper = 0.5 - 0.5 * jnp.cos(position * (2.0 * math.pi / NFFT))
    tapered = (signal * taper[None, :]).astype(jnp.bfloat16)
    spectrum = jnp.dot(tapered, dft_table(), preferred_element_type=jnp.float32)
    real_part = spectrum[:, :BINS]
    imag_part = spectrum[:, BINS:]
    amplitude = jnp.sqrt(real_part * real_part + imag_part * imag_part + 1e-06)
    padded = jnp.pad(amplitude, ((0, 0), (HALF, HALF)))
    smooth = jnp.zeros_like(amplitude)
    for offset in range(2 * HALF + 1):
        smooth = smooth + padded[:, offset:offset + BINS]
    smooth = smooth / (2 * HALF + 1)
    level = lax.optimization_barrier(jnp.mean(amplitude, axis=1, keepdims=True))
    divisor = smooth + level + 1e-06
    white = spectrum / jnp.concatenate([divisor, divisor], axis=1)
    return white.astype(jnp.bfloat16).reshape(count, SEG * NFFT)

def cross(first_rows, second_rows):
    left = first_rows.astype(jnp.float32).reshape(first_rows.shape[:-1] + (SEG, 2, BINS))
    right = second_rows.astype(jnp.float32).reshape(second_rows.shape[:-1] + (SEG, 2, BINS))
    real_sum = lax.optimization_barrier(jnp.mean(left[..., 0, :] * right[..., 0, :] + left[..., 1, :] * right[..., 1, :], axis=-2))
    imag_sum = lax.optimization_barrier(jnp.mean(left[..., 0, :] * right[..., 1, :] - left[..., 1, :] * right[..., 0, :], axis=-2))
    return jnp.concatenate([real_sum, imag_sum], axis=-1).astype(jnp.bfloat16)

def reference(records, first_station, second_region, second_station):
    white = whitened(records)
    blocks = N_REGION * N_SLAB
    owner = jnp.arange(blocks, dtype=jnp.int32) // N_SLAB
    firsts = first_station.reshape(blocks, PAIR_DEV)
    seconds = (second_region[:, 0] * STA_REG + second_station).reshape(blocks, PAIR_DEV)

    def one_block(item):
        owner_region, first_ids, second_ids = item
        first_rows = jnp.take(white, owner_region * STA_REG + first_ids, axis=0)
        second_rows = jnp.take(white, second_ids, axis=0)
        return cross(first_rows, second_rows)
    stacked = lax.map(one_block, (owner, firsts, seconds))
    return stacked.reshape(PAIRS, NFFT)
```

```python
import math

import jax
import jax.numpy as jnp
from jax import lax
from jax.sharding import PartitionSpec as P

NFFT = 2048
BINS = 1024
SEG = 2
HALF = 4


def dft_table():
    low = 64
    high = NFFT // low
    frequency = jnp.arange(BINS, dtype=jnp.int32)[None, :]
    coarse = jnp.arange(high, dtype=jnp.int32)[:, None]
    fine = jnp.arange(low, dtype=jnp.int32)[:, None]
    angle_a = ((coarse * frequency) % high).astype(jnp.float32) * (2.0 * math.pi / high)
    angle_b = ((fine * frequency) % NFFT).astype(jnp.float32) * (2.0 * math.pi / NFFT)
    ca, sa = jnp.cos(angle_a)[:, None, :], jnp.sin(angle_a)[:, None, :]
    cb, sb = jnp.cos(angle_b)[None, :, :], jnp.sin(angle_b)[None, :, :]
    cos_part = (ca * cb - sa * sb).reshape(NFFT, BINS)
    sin_part = (sa * cb + ca * sb).reshape(NFFT, BINS)
    return jnp.concatenate([cos_part, -sin_part], axis=1).astype(jnp.bfloat16)


def whitened(traces):
    count = traces.shape[0]
    signal = traces.astype(jnp.float32).reshape(count * SEG, NFFT)
    signal = signal - jnp.mean(signal, axis=1, keepdims=True)
    position = jnp.arange(NFFT, dtype=jnp.int32).astype(jnp.float32)
    taper = 0.5 - 0.5 * jnp.cos(position * (2.0 * math.pi / NFFT))
    tapered = (signal * taper[None, :]).astype(jnp.bfloat16)
    spectrum = jnp.dot(tapered, dft_table(), preferred_element_type=jnp.float32)
    real_part = spectrum[:, :BINS]
    imag_part = spectrum[:, BINS:]
    amplitude = jnp.sqrt(real_part * real_part + imag_part * imag_part + 1e-06)
    padded = jnp.pad(amplitude, ((0, 0), (HALF, HALF)))
    smooth = jnp.zeros_like(amplitude)
    for offset in range(2 * HALF + 1):
        smooth = smooth + padded[:, offset : offset + BINS]
    smooth = smooth / (2 * HALF + 1)
    level = jnp.mean(amplitude, axis=1, keepdims=True)
    divisor = smooth + level + 1e-06
    white = spectrum / jnp.concatenate([divisor, divisor], axis=1)
    return white.astype(jnp.bfloat16).reshape(count, SEG * NFFT)


def cross(first_rows, second_rows):
    left = first_rows.astype(jnp.float32).reshape(first_rows.shape[:-1] + (SEG, 2, BINS))
    right = second_rows.astype(jnp.float32).reshape(second_rows.shape[:-1] + (SEG, 2, BINS))
    real_sum = jnp.mean(
        left[..., 0, :] * right[..., 0, :] + left[..., 1, :] * right[..., 1, :], axis=-2
    )
    imag_sum = jnp.mean(
        left[..., 0, :] * right[..., 1, :] - left[..., 1, :] * right[..., 0, :], axis=-2
    )
    return jnp.concatenate([real_sum, imag_sum], axis=-1).astype(jnp.bfloat16)


def to_rows(parts):
    slabs, rows, width = parts.shape
    return jnp.transpose(parts, (1, 0, 2)).reshape(rows, slabs * width)


def local(records, first_station, second_region, second_station):
    regions = lax.axis_size("region")
    slabs = lax.axis_size("slab")
    pair_count = first_station.shape[0]
    width = records.shape[1]
    capacity = max(2, pair_count // regions + pair_count // 16)

    firsts = lax.all_gather(first_station, "slab", axis=0, tiled=False)
    first_parts = jnp.take(records, firsts.reshape(-1), axis=0).reshape(slabs, pair_count, width)
    first_arrived = lax.all_to_all(first_parts, "slab", split_axis=0, concat_axis=0, tiled=True)
    first_rows = whitened(to_rows(first_arrived))

    target = second_region[:, 0]
    onehot = (target[:, None] == jnp.arange(regions, dtype=jnp.int32)[None, :]).astype(jnp.int32)
    ranking = jnp.sum((jnp.cumsum(onehot, axis=0) - onehot) * onehot, axis=1)
    slot_index = target * capacity + ranking
    requests = (
        jnp.zeros((regions * capacity,), jnp.int32)
        .at[slot_index]
        .set(second_station)
        .reshape(regions, capacity)
    )
    plane_requests = lax.all_gather(requests, "slab", axis=0, tiled=False)
    asked = lax.all_to_all(plane_requests, "region", split_axis=1, concat_axis=1, tiled=True)
    served = jnp.take(records, jnp.transpose(asked, (1, 0, 2)).reshape(-1), axis=0)
    served = served.reshape(regions, slabs * capacity, width)
    arrived = lax.all_to_all(served, "region", split_axis=0, concat_axis=0, tiled=True)
    slots = lax.all_gather(slot_index, "slab", axis=0, tiled=False)
    flat = (slots // capacity) * (slabs * capacity) + jnp.arange(slabs, dtype=jnp.int32)[:, None] * capacity + slots % capacity
    second_parts = jnp.take(arrived.reshape(regions * slabs * capacity, width), flat.reshape(-1), axis=0)
    second_parts = second_parts.reshape(slabs, pair_count, width)
    second_arrived = lax.all_to_all(second_parts, "slab", split_axis=0, concat_axis=0, tiled=True)
    second_rows = whitened(to_rows(second_arrived))
    return cross(first_rows, second_rows)


def solution(mesh):
    placed = (
        P("region", "slab"),
        P(("region", "slab")),
        P(("region", "slab"), None),
        P(("region", "slab")),
    )
    return jax.shard_map(
        local, mesh=mesh, in_specs=placed, out_specs=P(("region", "slab"), None), check_vma=False
    )
```

```python
import math

import jax
import jax.numpy as jnp
from jax import lax
from jax.experimental import pallas as pl
from jax.experimental.pallas import tpu as pltpu
from jax.sharding import PartitionSpec as P

NFFT = 2048
BINS = 1024
SEG = 2
HALF = 4


def dft_table():
    low = 64
    high = NFFT // low
    frequency = jnp.arange(BINS, dtype=jnp.int32)[None, :]
    coarse = jnp.arange(high, dtype=jnp.int32)[:, None]
    fine = jnp.arange(low, dtype=jnp.int32)[:, None]
    angle_a = ((coarse * frequency) % high).astype(jnp.float32) * (2.0 * math.pi / high)
    angle_b = ((fine * frequency) % NFFT).astype(jnp.float32) * (2.0 * math.pi / NFFT)
    ca, sa = jnp.cos(angle_a)[:, None, :], jnp.sin(angle_a)[:, None, :]
    cb, sb = jnp.cos(angle_b)[None, :, :], jnp.sin(angle_b)[None, :, :]
    cos_part = (ca * cb - sa * sb).reshape(NFFT, BINS)
    sin_part = (sa * cb + ca * sb).reshape(NFFT, BINS)
    return jnp.concatenate([cos_part, -sin_part], axis=1).astype(jnp.bfloat16)


def whitened(traces):
    count = traces.shape[0]
    signal = traces.astype(jnp.float32).reshape(count * SEG, NFFT)
    signal = signal - jnp.mean(signal, axis=1, keepdims=True)
    position = jnp.arange(NFFT, dtype=jnp.int32).astype(jnp.float32)
    taper = 0.5 - 0.5 * jnp.cos(position * (2.0 * math.pi / NFFT))
    tapered = (signal * taper[None, :]).astype(jnp.bfloat16)
    spectrum = jnp.dot(tapered, dft_table(), preferred_element_type=jnp.float32)
    real_part = spectrum[:, :BINS]
    imag_part = spectrum[:, BINS:]
    amplitude = jnp.sqrt(real_part * real_part + imag_part * imag_part + 1e-06)
    padded = jnp.pad(amplitude, ((0, 0), (HALF, HALF)))
    smooth = jnp.zeros_like(amplitude)
    for offset in range(2 * HALF + 1):
        smooth = smooth + padded[:, offset : offset + BINS]
    smooth = smooth / (2 * HALF + 1)
    level = jnp.mean(amplitude, axis=1, keepdims=True)
    divisor = smooth + level + 1e-06
    white = spectrum / jnp.concatenate([divisor, divisor], axis=1)
    return white.astype(jnp.bfloat16).reshape(count, SEG * NFFT)


def cross(first_rows, second_rows):
    left = first_rows.astype(jnp.float32).reshape(first_rows.shape[:-1] + (SEG, 2, BINS))
    right = second_rows.astype(jnp.float32).reshape(second_rows.shape[:-1] + (SEG, 2, BINS))
    real_sum = jnp.mean(
        left[..., 0, :] * right[..., 0, :] + left[..., 1, :] * right[..., 1, :], axis=-2
    )
    imag_sum = jnp.mean(
        left[..., 0, :] * right[..., 1, :] - left[..., 1, :] * right[..., 0, :], axis=-2
    )
    return jnp.concatenate([real_sum, imag_sum], axis=-1).astype(jnp.bfloat16)


def _pick_kernel(ids_ref, table_ref, out_ref):
    ids = ids_ref[...]
    rows = table_ref.shape[0]
    onehot = (lax.broadcasted_iota(jnp.int32, (ids.shape[0], rows), 1) == ids).astype(table_ref.dtype)
    out_ref[...] = jnp.dot(onehot, table_ref[...], preferred_element_type=jnp.float32).astype(out_ref.dtype)


def pick_rows(table, ids, block=512):
    rows, width = table.shape
    count = ids.shape[0]
    block = min(block, count)
    return pl.pallas_call(
        _pick_kernel,
        out_shape=jax.ShapeDtypeStruct((count, width), table.dtype),
        grid=(count // block,),
        in_specs=[
            pl.BlockSpec((block, 1), lambda i: (i, 0)),
            pl.BlockSpec((rows, width), lambda i: (0, 0)),
        ],
        out_specs=pl.BlockSpec((block, width), lambda i: (i, 0)),
        cost_estimate=pl.CostEstimate(
            flops=2 * count * rows * width, transcendentals=0, bytes_accessed=2 * (rows + count) * width
        ),
    )(ids.reshape(count, 1), table)


def _compact_kernel(ids_ref, table_ref, out_ref):
    ids = ids_ref[0]
    buckets, capacity, width = table_ref.shape
    table = table_ref[...].reshape(buckets * capacity, width)
    onehot = (lax.broadcasted_iota(jnp.int32, (ids.shape[0], buckets * capacity), 1) == ids).astype(table.dtype)
    out_ref[0] = jnp.dot(onehot, table, preferred_element_type=jnp.float32).astype(out_ref.dtype)


def compact_rows(arrived, slots):
    buckets, slabs, capacity, width = arrived.shape
    pairs = slots.shape[1]
    return pl.pallas_call(
        _compact_kernel,
        out_shape=jax.ShapeDtypeStruct((slabs, pairs, width), arrived.dtype),
        grid=(slabs,),
        in_specs=[
            pl.BlockSpec((1, pairs, 1), lambda s: (s, 0, 0)),
            pl.BlockSpec((buckets, None, capacity, width), lambda s: (0, s, 0, 0)),
        ],
        out_specs=pl.BlockSpec((1, pairs, width), lambda s: (s, 0, 0)),
        cost_estimate=pl.CostEstimate(
            flops=2 * slabs * pairs * buckets * capacity * width,
            transcendentals=0,
            bytes_accessed=2 * (buckets * capacity + pairs) * slabs * width,
        ),
    )(slots.reshape(slabs, pairs, 1), arrived)


def to_rows(parts):
    slabs, rows, width = parts.shape
    return jnp.transpose(parts, (1, 0, 2)).reshape(rows, slabs * width)


def local(records, first_station, second_region, second_station):
    regions = lax.axis_size("region")
    slabs = lax.axis_size("slab")
    pair_count = first_station.shape[0]
    width = records.shape[1]
    capacity = max(2, pair_count // regions + pair_count // 16)

    target = second_region[:, 0]
    onehot = (target[:, None] == jnp.arange(regions, dtype=jnp.int32)[None, :]).astype(jnp.int32)
    ranking = jnp.sum((jnp.cumsum(onehot, axis=0) - onehot) * onehot, axis=1)
    slot_index = target * capacity + ranking
    requests = (
        jnp.zeros((regions * capacity,), jnp.int32)
        .at[slot_index]
        .set(second_station)
    )
    packed = jnp.concatenate([first_station, slot_index, requests])
    plane = lax.all_gather(packed, "slab", axis=0, tiled=False)
    firsts = plane[:, :pair_count]
    slots = plane[:, pair_count : 2 * pair_count]
    plane_requests = plane[:, 2 * pair_count :].reshape(slabs, regions, capacity)

    first_parts = pick_rows(records, firsts.reshape(-1)).reshape(slabs, pair_count, width)
    first_arrived = lax.all_to_all(first_parts, "slab", split_axis=0, concat_axis=0, tiled=True)
    first_rows = whitened(to_rows(first_arrived))

    asked = lax.all_to_all(plane_requests, "region", split_axis=1, concat_axis=1, tiled=True)
    served = pick_rows(records, jnp.transpose(asked, (1, 0, 2)).reshape(-1))
    served = served.reshape(regions, slabs * capacity, width)
    arrived = lax.all_to_all(served, "region", split_axis=0, concat_axis=0, tiled=True)
    second_parts = compact_rows(arrived.reshape(regions, slabs, capacity, width), slots)
    second_arrived = lax.all_to_all(second_parts, "slab", split_axis=0, concat_axis=0, tiled=True)
    second_rows = whitened(to_rows(second_arrived))
    return cross(first_rows, second_rows)


def solution(mesh):
    placed = (
        P("region", "slab"),
        P(("region", "slab")),
        P(("region", "slab"), None),
        P(("region", "slab")),
    )
    return jax.shard_map(
        local, mesh=mesh, in_specs=placed, out_specs=P(("region", "slab"), None), check_vma=False
    )
```

```python
import math

import jax
import jax.numpy as jnp
from jax import lax
from jax.experimental import pallas as pl
from jax.experimental.pallas import tpu as pltpu
from jax.sharding import PartitionSpec as P

NFFT = 2048
BINS = 1024
SEG = 2
HALF = 4


def dft_table():
    low = 64
    high = NFFT // low
    frequency = jnp.arange(BINS, dtype=jnp.int32)[None, :]
    coarse = jnp.arange(high, dtype=jnp.int32)[:, None]
    fine = jnp.arange(low, dtype=jnp.int32)[:, None]
    angle_a = ((coarse * frequency) % high).astype(jnp.float32) * (2.0 * math.pi / high)
    angle_b = ((fine * frequency) % NFFT).astype(jnp.float32) * (2.0 * math.pi / NFFT)
    ca, sa = jnp.cos(angle_a)[:, None, :], jnp.sin(angle_a)[:, None, :]
    cb, sb = jnp.cos(angle_b)[None, :, :], jnp.sin(angle_b)[None, :, :]
    cos_part = (ca * cb - sa * sb).reshape(NFFT, BINS)
    sin_part = (sa * cb + ca * sb).reshape(NFFT, BINS)
    return jnp.concatenate([cos_part, -sin_part], axis=1).astype(jnp.bfloat16)


def whitened(traces):
    count = traces.shape[0]
    signal = traces.astype(jnp.float32).reshape(count * SEG, NFFT)
    signal = signal - jnp.mean(signal, axis=1, keepdims=True)
    position = jnp.arange(NFFT, dtype=jnp.int32).astype(jnp.float32)
    taper = 0.5 - 0.5 * jnp.cos(position * (2.0 * math.pi / NFFT))
    tapered = (signal * taper[None, :]).astype(jnp.bfloat16)
    spectrum = jnp.dot(tapered, dft_table(), preferred_element_type=jnp.float32)
    real_part = spectrum[:, :BINS]
    imag_part = spectrum[:, BINS:]
    amplitude = jnp.sqrt(real_part * real_part + imag_part * imag_part + 1e-06)
    padded = jnp.pad(amplitude, ((0, 0), (HALF, HALF)))
    smooth = jnp.zeros_like(amplitude)
    for offset in range(2 * HALF + 1):
        smooth = smooth + padded[:, offset : offset + BINS]
    smooth = smooth / (2 * HALF + 1)
    level = jnp.mean(amplitude, axis=1, keepdims=True)
    divisor = smooth + level + 1e-06
    white = spectrum / jnp.concatenate([divisor, divisor], axis=1)
    return white.astype(jnp.bfloat16).reshape(count, SEG * NFFT)


def cross(first_rows, second_rows):
    left = first_rows.astype(jnp.float32).reshape(first_rows.shape[:-1] + (SEG, 2, BINS))
    right = second_rows.astype(jnp.float32).reshape(second_rows.shape[:-1] + (SEG, 2, BINS))
    real_sum = jnp.mean(
        left[..., 0, :] * right[..., 0, :] + left[..., 1, :] * right[..., 1, :], axis=-2
    )
    imag_sum = jnp.mean(
        left[..., 0, :] * right[..., 1, :] - left[..., 1, :] * right[..., 0, :], axis=-2
    )
    return jnp.concatenate([real_sum, imag_sum], axis=-1).astype(jnp.bfloat16)


def _pick_kernel(ids_ref, table_ref, out_ref):
    ids = ids_ref[...]
    rows = table_ref.shape[0]
    onehot = (lax.broadcasted_iota(jnp.int32, (ids.shape[0], rows), 1) == ids).astype(table_ref.dtype)
    out_ref[...] = jnp.dot(onehot, table_ref[...], preferred_element_type=jnp.float32).astype(out_ref.dtype)


def pick_rows(table, ids, block=512):
    rows, width = table.shape
    count = ids.shape[0]
    block = min(block, count)
    return pl.pallas_call(
        _pick_kernel,
        out_shape=jax.ShapeDtypeStruct((count, width), table.dtype),
        grid=(count // block,),
        in_specs=[
            pl.BlockSpec((block, 1), lambda i: (i, 0)),
            pl.BlockSpec((rows, width), lambda i: (0, 0)),
        ],
        out_specs=pl.BlockSpec((block, width), lambda i: (i, 0)),
        cost_estimate=pl.CostEstimate(
            flops=2 * count * rows * width, transcendentals=0, bytes_accessed=2 * (rows + count) * width
        ),
    )(ids.reshape(count, 1), table)


def _compact_kernel(ids_ref, table_ref, out_ref):
    buckets, slabs, capacity, width = table_ref.shape
    for s in range(slabs):
        ids = ids_ref[s]
        table = table_ref[:, s].reshape(buckets * capacity, width)
        onehot = (lax.broadcasted_iota(jnp.int32, (ids.shape[0], buckets * capacity), 1) == ids).astype(table.dtype)
        out_ref[s] = jnp.dot(onehot, table, preferred_element_type=jnp.float32).astype(out_ref.dtype)


def compact_rows(arrived, slots):
    buckets, slabs, capacity, width = arrived.shape
    pairs = slots.shape[1]
    return pl.pallas_call(
        _compact_kernel,
        out_shape=jax.ShapeDtypeStruct((slabs, pairs, width), arrived.dtype),
        cost_estimate=pl.CostEstimate(
            flops=2 * slabs * pairs * buckets * capacity * width,
            transcendentals=0,
            bytes_accessed=2 * (buckets * capacity + pairs) * slabs * width,
        ),
    )(slots.reshape(slabs, pairs, 1), arrived)


def _white_block(x, table, taper):
    slabs, rows, width = x.shape
    per_segment = slabs // SEG
    signal = x.astype(jnp.float32)
    tapered = []
    for segment in range(SEG):
        part = signal[segment * per_segment : (segment + 1) * per_segment]
        mean = jnp.sum(jnp.sum(part, axis=2, keepdims=True), axis=0) / NFFT
        pieces = [((part[i] - mean) * taper[i : i + 1, :]).astype(jnp.bfloat16) for i in range(per_segment)]
        tapered.append(jnp.concatenate(pieces, axis=1))
    spectrum = jnp.dot(jnp.concatenate(tapered, axis=0), table, preferred_element_type=jnp.float32)
    real_part = spectrum[:, :BINS]
    imag_part = spectrum[:, BINS:]
    amplitude = jnp.sqrt(real_part * real_part + imag_part * imag_part + 1e-06)
    lane = lax.broadcasted_iota(jnp.int32, amplitude.shape, 1)
    smooth = jnp.zeros_like(amplitude)
    for offset in range(-HALF, HALF + 1):
        moved = amplitude if offset == 0 else pltpu.roll(amplitude, (-offset) % BINS, 1)
        inside = (lane + offset >= 0) & (lane + offset < BINS)
        smooth = smooth + jnp.where(inside, moved, 0.0)
    smooth = smooth / (2 * HALF + 1)
    level = jnp.sum(amplitude, axis=1, keepdims=True) / BINS
    divisor = smooth + level + 1e-06
    white_real = (real_part / divisor).astype(jnp.bfloat16)
    white_imag = (imag_part / divisor).astype(jnp.bfloat16)
    return white_real, white_imag


def _white_kernel(x_ref, table_ref, taper_ref, out_ref):
    rows = x_ref.shape[1]
    white_real, white_imag = _white_block(x_ref[...], table_ref[...], taper_ref[...])
    for segment in range(SEG):
        out_ref[2 * segment] = white_real[segment * rows : (segment + 1) * rows]
        out_ref[2 * segment + 1] = white_imag[segment * rows : (segment + 1) * rows]


def _cross_kernel(x_ref, first_ref, table_ref, taper_ref, out_ref):
    rows = x_ref.shape[1]
    white_real, white_imag = _white_block(x_ref[...], table_ref[...], taper_ref[...])
    real_sum = None
    imag_sum = None
    for segment in range(SEG):
        left_real = first_ref[2 * segment].astype(jnp.float32)
        left_imag = first_ref[2 * segment + 1].astype(jnp.float32)
        right_real = white_real[segment * rows : (segment + 1) * rows].astype(jnp.float32)
        right_imag = white_imag[segment * rows : (segment + 1) * rows].astype(jnp.float32)
        real_term = left_real * right_real + left_imag * right_imag
        imag_term = left_real * right_imag - left_imag * right_real
        real_sum = real_term if real_sum is None else real_sum + real_term
        imag_sum = imag_term if imag_sum is None else imag_sum + imag_term
    out_ref[:, :BINS] = (real_sum / SEG).astype(out_ref.dtype)
    out_ref[:, BINS:] = (imag_sum / SEG).astype(out_ref.dtype)


def taper_table(slabs_per_segment, width):
    position = jnp.arange(NFFT, dtype=jnp.int32).astype(jnp.float32)
    taper = 0.5 - 0.5 * jnp.cos(position * (2.0 * math.pi / NFFT))
    return taper.reshape(slabs_per_segment, width)


def _white_specs(slabs, block, width, per_segment):
    return [
        pl.BlockSpec((slabs, block, width), lambda i: (0, i, 0)),
        pl.BlockSpec((NFFT, 2 * BINS), lambda i: (0, 0), pipeline_mode=pl.Buffered(1)),
        pl.BlockSpec((per_segment, width), lambda i: (0, 0)),
    ]


def white_rows(parts, table, taper, block=32):
    slabs, rows, width = parts.shape
    specs = _white_specs(slabs, block, width, slabs // SEG)
    return pl.pallas_call(
        _white_kernel,
        out_shape=jax.ShapeDtypeStruct((2 * SEG, rows, BINS), jnp.bfloat16),
        grid=(rows // block,),
        in_specs=specs,
        out_specs=pl.BlockSpec((2 * SEG, block, BINS), lambda i: (0, i, 0)),
        compiler_params=pltpu.CompilerParams(vmem_limit_bytes=48 * 1024 * 1024),
        cost_estimate=pl.CostEstimate(
            flops=2 * SEG * rows * NFFT * 2 * BINS, transcendentals=SEG * rows * BINS,
            bytes_accessed=NFFT * 2 * BINS * 2 + 4 * slabs * rows * width,
        ),
    )(parts, table, taper)


def cross_rows(parts, first_white, table, taper, block=32):
    slabs, rows, width = parts.shape
    specs = _white_specs(slabs, block, width, slabs // SEG)
    specs.insert(1, pl.BlockSpec((2 * SEG, block, BINS), lambda i: (0, i, 0)))
    return pl.pallas_call(
        _cross_kernel,
        out_shape=jax.ShapeDtypeStruct((rows, 2 * BINS), jnp.bfloat16),
        grid=(rows // block,),
        in_specs=specs,
        out_specs=pl.BlockSpec((block, 2 * BINS), lambda i: (i, 0)),
        compiler_params=pltpu.CompilerParams(vmem_limit_bytes=48 * 1024 * 1024),
        cost_estimate=pl.CostEstimate(
            flops=2 * SEG * rows * NFFT * 2 * BINS, transcendentals=SEG * rows * BINS,
            bytes_accessed=NFFT * 2 * BINS * 2 + 8 * slabs * rows * width,
        ),
    )(parts, first_white, table, taper)


def to_rows(parts):
    slabs, rows, width = parts.shape
    return jnp.transpose(parts, (1, 0, 2)).reshape(rows, slabs * width)


def local(records, first_station, second_region, second_station):
    regions = lax.axis_size("region")
    slabs = lax.axis_size("slab")
    pair_count = first_station.shape[0]
    width = records.shape[1]
    capacity = max(2, pair_count // regions + pair_count // 16)

    target = second_region[:, 0]
    onehot = (target[:, None] == jnp.arange(regions, dtype=jnp.int32)[None, :]).astype(jnp.int32)
    ranking = jnp.sum((jnp.cumsum(onehot, axis=0) - onehot) * onehot, axis=1)
    slot_index = target * capacity + ranking
    requests = (
        jnp.zeros((regions * capacity,), jnp.int32)
        .at[slot_index]
        .set(second_station)
    )
    packed = jnp.concatenate([first_station, slot_index, requests])
    plane = lax.all_gather(packed, "slab", axis=0, tiled=False)
    firsts = plane[:, :pair_count]
    slots = plane[:, pair_count : 2 * pair_count]
    plane_requests = plane[:, 2 * pair_count :].reshape(slabs, regions, capacity)

    first_parts = pick_rows(records, firsts.reshape(-1)).reshape(slabs, pair_count, width)
    first_arrived = lax.all_to_all(first_parts, "slab", split_axis=0, concat_axis=0, tiled=True)
    table = dft_table()
    taper = taper_table(slabs // SEG, width)
    first_white = white_rows(first_arrived, table, taper)

    asked = lax.all_to_all(plane_requests, "region", split_axis=1, concat_axis=1, tiled=True)
    served = pick_rows(records, jnp.transpose(asked, (1, 0, 2)).reshape(-1))
    served = served.reshape(regions, slabs * capacity, width)
    arrived = lax.all_to_all(served, "region", split_axis=0, concat_axis=0, tiled=True)
    second_parts = compact_rows(arrived.reshape(regions, slabs, capacity, width), slots)
    second_arrived = lax.all_to_all(second_parts, "slab", split_axis=0, concat_axis=0, tiled=True)
    return cross_rows(second_arrived, first_white, table, taper)


def solution(mesh):
    placed = (
        P("region", "slab"),
        P(("region", "slab")),
        P(("region", "slab"), None),
        P(("region", "slab")),
    )
    return jax.shard_map(
        local, mesh=mesh, in_specs=placed, out_specs=P(("region", "slab"), None), check_vma=False
    )
```

```python
import math

import jax
import jax.numpy as jnp
from jax import lax
from jax.experimental import pallas as pl
from jax.experimental.pallas import tpu as pltpu
from jax.sharding import PartitionSpec as P

NFFT = 2048
BINS = 1024
SEG = 2
HALF = 4


def dft_table():
    low = 64
    high = NFFT // low
    frequency = jnp.arange(BINS, dtype=jnp.int32)[None, :]
    coarse = jnp.arange(high, dtype=jnp.int32)[:, None]
    fine = jnp.arange(low, dtype=jnp.int32)[:, None]
    angle_a = ((coarse * frequency) % high).astype(jnp.float32) * (2.0 * math.pi / high)
    angle_b = ((fine * frequency) % NFFT).astype(jnp.float32) * (2.0 * math.pi / NFFT)
    ca, sa = jnp.cos(angle_a)[:, None, :], jnp.sin(angle_a)[:, None, :]
    cb, sb = jnp.cos(angle_b)[None, :, :], jnp.sin(angle_b)[None, :, :]
    cos_part = (ca * cb - sa * sb).reshape(NFFT, BINS)
    sin_part = (sa * cb + ca * sb).reshape(NFFT, BINS)
    return jnp.concatenate([cos_part, -sin_part], axis=1).astype(jnp.bfloat16)


def whitened(traces):
    count = traces.shape[0]
    signal = traces.astype(jnp.float32).reshape(count * SEG, NFFT)
    signal = signal - jnp.mean(signal, axis=1, keepdims=True)
    position = jnp.arange(NFFT, dtype=jnp.int32).astype(jnp.float32)
    taper = 0.5 - 0.5 * jnp.cos(position * (2.0 * math.pi / NFFT))
    tapered = (signal * taper[None, :]).astype(jnp.bfloat16)
    spectrum = jnp.dot(tapered, dft_table(), preferred_element_type=jnp.float32)
    real_part = spectrum[:, :BINS]
    imag_part = spectrum[:, BINS:]
    amplitude = jnp.sqrt(real_part * real_part + imag_part * imag_part + 1e-06)
    padded = jnp.pad(amplitude, ((0, 0), (HALF, HALF)))
    smooth = jnp.zeros_like(amplitude)
    for offset in range(2 * HALF + 1):
        smooth = smooth + padded[:, offset : offset + BINS]
    smooth = smooth / (2 * HALF + 1)
    level = jnp.mean(amplitude, axis=1, keepdims=True)
    divisor = smooth + level + 1e-06
    white = spectrum / jnp.concatenate([divisor, divisor], axis=1)
    return white.astype(jnp.bfloat16).reshape(count, SEG * NFFT)


def cross(first_rows, second_rows):
    left = first_rows.astype(jnp.float32).reshape(first_rows.shape[:-1] + (SEG, 2, BINS))
    right = second_rows.astype(jnp.float32).reshape(second_rows.shape[:-1] + (SEG, 2, BINS))
    real_sum = jnp.mean(
        left[..., 0, :] * right[..., 0, :] + left[..., 1, :] * right[..., 1, :], axis=-2
    )
    imag_sum = jnp.mean(
        left[..., 0, :] * right[..., 1, :] - left[..., 1, :] * right[..., 0, :], axis=-2
    )
    return jnp.concatenate([real_sum, imag_sum], axis=-1).astype(jnp.bfloat16)


def _pick_kernel(ids_ref, table_ref, out_ref):
    ids = ids_ref[...]
    rows = table_ref.shape[0]
    onehot = (lax.broadcasted_iota(jnp.int32, (ids.shape[0], rows), 1) == ids).astype(table_ref.dtype)
    out_ref[...] = jnp.dot(onehot, table_ref[...], preferred_element_type=jnp.float32).astype(out_ref.dtype)


def pick_rows(table, ids, block=512):
    rows, width = table.shape
    count = ids.shape[0]
    block = min(block, count)
    return pl.pallas_call(
        _pick_kernel,
        out_shape=jax.ShapeDtypeStruct((count, width), table.dtype),
        grid=(count // block,),
        in_specs=[
            pl.BlockSpec((block, 1), lambda i: (i, 0)),
            pl.BlockSpec((rows, width), lambda i: (0, 0)),
        ],
        out_specs=pl.BlockSpec((block, width), lambda i: (i, 0)),
        cost_estimate=pl.CostEstimate(
            flops=2 * count * rows * width, transcendentals=0, bytes_accessed=2 * (rows + count) * width
        ),
    )(ids.reshape(count, 1), table)


def _compact_kernel(ids_ref, table_ref, out_ref):
    buckets, slabs, capacity, width = table_ref.shape
    for s in range(slabs):
        ids = ids_ref[s]
        table = table_ref[:, s].reshape(buckets * capacity, width)
        onehot = (lax.broadcasted_iota(jnp.int32, (ids.shape[0], buckets * capacity), 1) == ids).astype(table.dtype)
        out_ref[s] = jnp.dot(onehot, table, preferred_element_type=jnp.float32).astype(out_ref.dtype)


def compact_rows(arrived, slots):
    buckets, slabs, capacity, width = arrived.shape
    pairs = slots.shape[1]
    return pl.pallas_call(
        _compact_kernel,
        out_shape=jax.ShapeDtypeStruct((slabs, pairs, width), arrived.dtype),
        cost_estimate=pl.CostEstimate(
            flops=2 * slabs * pairs * buckets * capacity * width,
            transcendentals=0,
            bytes_accessed=2 * (buckets * capacity + pairs) * slabs * width,
        ),
    )(slots.reshape(slabs, pairs, 1), arrived)


def _white_block(x, table, taper):
    slabs, rows, width = x.shape
    per_segment = slabs // SEG
    signal = x.astype(jnp.float32)
    tapered = []
    for segment in range(SEG):
        part = signal[segment * per_segment : (segment + 1) * per_segment]
        mean = jnp.sum(jnp.sum(part, axis=2, keepdims=True), axis=0) / NFFT
        pieces = [((part[i] - mean) * taper[i : i + 1, :]).astype(jnp.bfloat16) for i in range(per_segment)]
        tapered.append(jnp.concatenate(pieces, axis=1))
    spectrum = jnp.dot(jnp.concatenate(tapered, axis=0), table, preferred_element_type=jnp.float32)
    real_part = spectrum[:, :BINS]
    imag_part = spectrum[:, BINS:]
    amplitude = jnp.sqrt(real_part * real_part + imag_part * imag_part + 1e-06)
    lane = lax.broadcasted_iota(jnp.int32, amplitude.shape, 1)
    smooth = jnp.zeros_like(amplitude)
    for offset in range(-HALF, HALF + 1):
        moved = amplitude if offset == 0 else pltpu.roll(amplitude, (-offset) % BINS, 1)
        inside = (lane + offset >= 0) & (lane + offset < BINS)
        smooth = smooth + jnp.where(inside, moved, 0.0)
    smooth = smooth / (2 * HALF + 1)
    level = jnp.sum(amplitude, axis=1, keepdims=True) / BINS
    divisor = smooth + level + 1e-06
    white_real = (real_part / divisor).astype(jnp.bfloat16)
    white_imag = (imag_part / divisor).astype(jnp.bfloat16)
    return white_real, white_imag


def _white_kernel(x_ref, table_ref, taper_ref, out_ref):
    rows = x_ref.shape[1]
    white_real, white_imag = _white_block(x_ref[...], table_ref[...], taper_ref[...])
    for segment in range(SEG):
        out_ref[2 * segment] = white_real[segment * rows : (segment + 1) * rows]
        out_ref[2 * segment + 1] = white_imag[segment * rows : (segment + 1) * rows]


def _cross_kernel(x_ref, first_ref, table_ref, taper_ref, out_ref):
    rows = x_ref.shape[1]
    white_real, white_imag = _white_block(x_ref[...], table_ref[...], taper_ref[...])
    real_sum = None
    imag_sum = None
    for segment in range(SEG):
        left_real = first_ref[2 * segment].astype(jnp.float32)
        left_imag = first_ref[2 * segment + 1].astype(jnp.float32)
        right_real = white_real[segment * rows : (segment + 1) * rows].astype(jnp.float32)
        right_imag = white_imag[segment * rows : (segment + 1) * rows].astype(jnp.float32)
        real_term = left_real * right_real + left_imag * right_imag
        imag_term = left_real * right_imag - left_imag * right_real
        real_sum = real_term if real_sum is None else real_sum + real_term
        imag_sum = imag_term if imag_sum is None else imag_sum + imag_term
    out_ref[:, :BINS] = (real_sum / SEG).astype(out_ref.dtype)
    out_ref[:, BINS:] = (imag_sum / SEG).astype(out_ref.dtype)


def taper_table(slabs_per_segment, width):
    position = jnp.arange(NFFT, dtype=jnp.int32).astype(jnp.float32)
    taper = 0.5 - 0.5 * jnp.cos(position * (2.0 * math.pi / NFFT))
    return taper.reshape(slabs_per_segment, width)


def _white_specs(slabs, block, width, per_segment):
    return [
        pl.BlockSpec((slabs, block, width), lambda i: (0, i, 0)),
        pl.BlockSpec((NFFT, 2 * BINS), lambda i: (0, 0), pipeline_mode=pl.Buffered(1)),
        pl.BlockSpec((per_segment, width), lambda i: (0, 0)),
    ]


def white_rows(parts, table, taper, block=32):
    slabs, rows, width = parts.shape
    specs = _white_specs(slabs, block, width, slabs // SEG)
    return pl.pallas_call(
        _white_kernel,
        out_shape=jax.ShapeDtypeStruct((2 * SEG, rows, BINS), jnp.bfloat16),
        grid=(rows // block,),
        in_specs=specs,
        out_specs=pl.BlockSpec((2 * SEG, block, BINS), lambda i: (0, i, 0)),
        compiler_params=pltpu.CompilerParams(vmem_limit_bytes=48 * 1024 * 1024),
        cost_estimate=pl.CostEstimate(
            flops=2 * SEG * rows * NFFT * 2 * BINS, transcendentals=SEG * rows * BINS,
            bytes_accessed=NFFT * 2 * BINS * 2 + 4 * slabs * rows * width,
        ),
    )(parts, table, taper)


def cross_rows(parts, first_white, table, taper, block=32):
    slabs, rows, width = parts.shape
    specs = _white_specs(slabs, block, width, slabs // SEG)
    specs.insert(1, pl.BlockSpec((2 * SEG, block, BINS), lambda i: (0, i, 0)))
    return pl.pallas_call(
        _cross_kernel,
        out_shape=jax.ShapeDtypeStruct((rows, 2 * BINS), jnp.bfloat16),
        grid=(rows // block,),
        in_specs=specs,
        out_specs=pl.BlockSpec((block, 2 * BINS), lambda i: (i, 0)),
        compiler_params=pltpu.CompilerParams(vmem_limit_bytes=48 * 1024 * 1024),
        cost_estimate=pl.CostEstimate(
            flops=2 * SEG * rows * NFFT * 2 * BINS, transcendentals=SEG * rows * BINS,
            bytes_accessed=NFFT * 2 * BINS * 2 + 8 * slabs * rows * width,
        ),
    )(parts, first_white, table, taper)


def _slab_exchange_kernel(x_ref, out_ref, landed, send_sems, recv_sems):
    slabs = x_ref.shape[0]
    region = lax.axis_index("region")
    me = lax.axis_index("slab")
    barrier = pltpu.get_barrier_semaphore()
    for step in range(1, slabs):
        pl.semaphore_signal(
            barrier, inc=1, device_id=(region, lax.rem(me + step, slabs)), device_id_type=pl.DeviceIdType.MESH
        )
    pl.semaphore_wait(barrier, slabs - 1)
    copies = []
    for step in range(1, slabs):
        peer = lax.rem(me + step, slabs)
        copy = pltpu.make_async_remote_copy(
            src_ref=x_ref.at[peer],
            dst_ref=landed.at[me],
            send_sem=send_sems.at[step],
            recv_sem=recv_sems.at[step],
            device_id=(region, peer),
            device_id_type=pl.DeviceIdType.MESH,
        )
        copy.start()
        copies.append(copy)
    landed[me] = x_ref[me]
    for copy in copies:
        copy.wait_send()
        copy.wait_recv()
    out_ref[...] = landed[...]


def slab_exchange(parts, collective):
    slabs = parts.shape[0]
    return pl.pallas_call(
        _slab_exchange_kernel,
        out_shape=jax.ShapeDtypeStruct(parts.shape, parts.dtype),
        scratch_shapes=[
            pltpu.VMEM(parts.shape, parts.dtype),
            pltpu.SemaphoreType.DMA((slabs,)),
            pltpu.SemaphoreType.DMA((slabs,)),
        ],
        compiler_params=pltpu.CompilerParams(collective_id=collective, has_side_effects=True),
        cost_estimate=pl.CostEstimate(flops=0, transcendentals=0, bytes_accessed=4 * parts.size),
    )(parts)


def to_rows(parts):
    slabs, rows, width = parts.shape
    return jnp.transpose(parts, (1, 0, 2)).reshape(rows, slabs * width)


def local(records, first_station, second_region, second_station):
    regions = lax.axis_size("region")
    slabs = lax.axis_size("slab")
    pair_count = first_station.shape[0]
    width = records.shape[1]
    capacity = max(2, pair_count // regions + pair_count // 16)

    target = second_region[:, 0]
    onehot = (target[:, None] == jnp.arange(regions, dtype=jnp.int32)[None, :]).astype(jnp.int32)
    ranking = jnp.sum((jnp.cumsum(onehot, axis=0) - onehot) * onehot, axis=1)
    slot_index = target * capacity + ranking
    requests = (
        jnp.zeros((regions * capacity,), jnp.int32)
        .at[slot_index]
        .set(second_station)
    )
    packed = jnp.concatenate([first_station, slot_index, requests])
    plane = lax.all_gather(packed, "slab", axis=0, tiled=False)
    firsts = plane[:, :pair_count]
    slots = plane[:, pair_count : 2 * pair_count]
    plane_requests = plane[:, 2 * pair_count :].reshape(slabs, regions, capacity)

    first_parts = pick_rows(records, firsts.reshape(-1)).reshape(slabs, pair_count, width)
    first_arrived = slab_exchange(first_parts, 0)
    table = dft_table()
    taper = taper_table(slabs // SEG, width)
    first_white = white_rows(first_arrived, table, taper)

    asked = lax.all_to_all(plane_requests, "region", split_axis=1, concat_axis=1, tiled=True)
    served = pick_rows(records, jnp.transpose(asked, (1, 0, 2)).reshape(-1))
    served = served.reshape(regions, slabs * capacity, width)
    arrived = lax.all_to_all(served, "region", split_axis=0, concat_axis=0, tiled=True)
    second_parts = compact_rows(arrived.reshape(regions, slabs, capacity, width), slots)
    second_arrived = slab_exchange(second_parts, 1)
    return cross_rows(second_arrived, first_white, table, taper)


def solution(mesh):
    placed = (
        P("region", "slab"),
        P(("region", "slab")),
        P(("region", "slab"), None),
        P(("region", "slab")),
    )
    return jax.shard_map(
        local, mesh=mesh, in_specs=placed, out_specs=P(("region", "slab"), None), check_vma=False
    )
```

```python
import functools
import math

import jax
import jax.numpy as jnp
from jax import lax
from jax.experimental import pallas as pl
from jax.experimental.pallas import tpu as pltpu
from jax.sharding import PartitionSpec as P

NFFT = 2048
BINS = 1024
SEG = 2
HALF = 4


def dft_table():
    low = 64
    high = NFFT // low
    frequency = jnp.arange(BINS, dtype=jnp.int32)[None, :]
    coarse = jnp.arange(high, dtype=jnp.int32)[:, None]
    fine = jnp.arange(low, dtype=jnp.int32)[:, None]
    angle_a = ((coarse * frequency) % high).astype(jnp.float32) * (2.0 * math.pi / high)
    angle_b = ((fine * frequency) % NFFT).astype(jnp.float32) * (2.0 * math.pi / NFFT)
    ca, sa = jnp.cos(angle_a)[:, None, :], jnp.sin(angle_a)[:, None, :]
    cb, sb = jnp.cos(angle_b)[None, :, :], jnp.sin(angle_b)[None, :, :]
    cos_part = (ca * cb - sa * sb).reshape(NFFT, BINS)
    sin_part = (sa * cb + ca * sb).reshape(NFFT, BINS)
    return jnp.concatenate([cos_part, -sin_part], axis=1).astype(jnp.bfloat16)


def whitened(traces):
    count = traces.shape[0]
    signal = traces.astype(jnp.float32).reshape(count * SEG, NFFT)
    signal = signal - jnp.mean(signal, axis=1, keepdims=True)
    position = jnp.arange(NFFT, dtype=jnp.int32).astype(jnp.float32)
    taper = 0.5 - 0.5 * jnp.cos(position * (2.0 * math.pi / NFFT))
    tapered = (signal * taper[None, :]).astype(jnp.bfloat16)
    spectrum = jnp.dot(tapered, dft_table(), preferred_element_type=jnp.float32)
    real_part = spectrum[:, :BINS]
    imag_part = spectrum[:, BINS:]
    amplitude = jnp.sqrt(real_part * real_part + imag_part * imag_part + 1e-06)
    padded = jnp.pad(amplitude, ((0, 0), (HALF, HALF)))
    smooth = jnp.zeros_like(amplitude)
    for offset in range(2 * HALF + 1):
        smooth = smooth + padded[:, offset : offset + BINS]
    smooth = smooth / (2 * HALF + 1)
    level = jnp.mean(amplitude, axis=1, keepdims=True)
    divisor = smooth + level + 1e-06
    white = spectrum / jnp.concatenate([divisor, divisor], axis=1)
    return white.astype(jnp.bfloat16).reshape(count, SEG * NFFT)


def cross(first_rows, second_rows):
    left = first_rows.astype(jnp.float32).reshape(first_rows.shape[:-1] + (SEG, 2, BINS))
    right = second_rows.astype(jnp.float32).reshape(second_rows.shape[:-1] + (SEG, 2, BINS))
    real_sum = jnp.mean(
        left[..., 0, :] * right[..., 0, :] + left[..., 1, :] * right[..., 1, :], axis=-2
    )
    imag_sum = jnp.mean(
        left[..., 0, :] * right[..., 1, :] - left[..., 1, :] * right[..., 0, :], axis=-2
    )
    return jnp.concatenate([real_sum, imag_sum], axis=-1).astype(jnp.bfloat16)


def _pick_kernel(ids_ref, table_ref, out_ref):
    ids = ids_ref[...]
    rows = table_ref.shape[0]
    onehot = (lax.broadcasted_iota(jnp.int32, (ids.shape[0], rows), 1) == ids).astype(table_ref.dtype)
    out_ref[...] = jnp.dot(onehot, table_ref[...], preferred_element_type=jnp.float32).astype(out_ref.dtype)


def pick_rows(table, ids, block=512):
    rows, width = table.shape
    count = ids.shape[0]
    block = min(block, count)
    return pl.pallas_call(
        _pick_kernel,
        out_shape=jax.ShapeDtypeStruct((count, width), table.dtype),
        grid=(count // block,),
        in_specs=[
            pl.BlockSpec((block, 1), lambda i: (i, 0)),
            pl.BlockSpec((rows, width), lambda i: (0, 0)),
        ],
        out_specs=pl.BlockSpec((block, width), lambda i: (i, 0)),
        cost_estimate=pl.CostEstimate(
            flops=2 * count * rows * width, transcendentals=0, bytes_accessed=2 * (rows + count) * width
        ),
    )(ids.reshape(count, 1), table)


def _compact_kernel(ids_ref, table_ref, out_ref):
    buckets, slabs, capacity, width = table_ref.shape
    for s in range(slabs):
        ids = ids_ref[s]
        table = table_ref[:, s].reshape(buckets * capacity, width)
        onehot = (lax.broadcasted_iota(jnp.int32, (ids.shape[0], buckets * capacity), 1) == ids).astype(table.dtype)
        out_ref[s] = jnp.dot(onehot, table, preferred_element_type=jnp.float32).astype(out_ref.dtype)


def compact_rows(arrived, slots):
    buckets, slabs, capacity, width = arrived.shape
    pairs = slots.shape[1]
    return pl.pallas_call(
        _compact_kernel,
        out_shape=jax.ShapeDtypeStruct((slabs, pairs, width), arrived.dtype),
        cost_estimate=pl.CostEstimate(
            flops=2 * slabs * pairs * buckets * capacity * width,
            transcendentals=0,
            bytes_accessed=2 * (buckets * capacity + pairs) * slabs * width,
        ),
    )(slots.reshape(slabs, pairs, 1), arrived)


def _white_block(x, table, taper):
    slabs, rows, width = x.shape
    per_segment = slabs // SEG
    signal = x.astype(jnp.float32)
    tapered = []
    for segment in range(SEG):
        part = signal[segment * per_segment : (segment + 1) * per_segment]
        mean = jnp.sum(jnp.sum(part, axis=2, keepdims=True), axis=0) / NFFT
        pieces = [((part[i] - mean) * taper[i : i + 1, :]).astype(jnp.bfloat16) for i in range(per_segment)]
        tapered.append(jnp.concatenate(pieces, axis=1))
    spectrum = jnp.dot(jnp.concatenate(tapered, axis=0), table, preferred_element_type=jnp.float32)
    real_part = spectrum[:, :BINS]
    imag_part = spectrum[:, BINS:]
    amplitude = jnp.sqrt(real_part * real_part + imag_part * imag_part + 1e-06)
    lane = lax.broadcasted_iota(jnp.int32, amplitude.shape, 1)
    smooth = jnp.zeros_like(amplitude)
    for offset in range(-HALF, HALF + 1):
        moved = amplitude if offset == 0 else pltpu.roll(amplitude, (-offset) % BINS, 1)
        inside = (lane + offset >= 0) & (lane + offset < BINS)
        smooth = smooth + jnp.where(inside, moved, 0.0)
    smooth = smooth / (2 * HALF + 1)
    level = jnp.sum(amplitude, axis=1, keepdims=True) / BINS
    divisor = smooth + level + 1e-06
    white_real = (real_part / divisor).astype(jnp.bfloat16)
    white_imag = (imag_part / divisor).astype(jnp.bfloat16)
    return white_real, white_imag


def _white_kernel(x_ref, table_ref, taper_ref, out_ref):
    rows = x_ref.shape[1]
    white_real, white_imag = _white_block(x_ref[...], table_ref[...], taper_ref[...])
    for segment in range(SEG):
        out_ref[2 * segment] = white_real[segment * rows : (segment + 1) * rows]
        out_ref[2 * segment + 1] = white_imag[segment * rows : (segment + 1) * rows]


def _cross_kernel(x_ref, first_ref, table_ref, taper_ref, out_ref):
    rows = x_ref.shape[1]
    white_real, white_imag = _white_block(x_ref[...], table_ref[...], taper_ref[...])
    real_sum = None
    imag_sum = None
    for segment in range(SEG):
        left_real = first_ref[2 * segment].astype(jnp.float32)
        left_imag = first_ref[2 * segment + 1].astype(jnp.float32)
        right_real = white_real[segment * rows : (segment + 1) * rows].astype(jnp.float32)
        right_imag = white_imag[segment * rows : (segment + 1) * rows].astype(jnp.float32)
        real_term = left_real * right_real + left_imag * right_imag
        imag_term = left_real * right_imag - left_imag * right_real
        real_sum = real_term if real_sum is None else real_sum + real_term
        imag_sum = imag_term if imag_sum is None else imag_sum + imag_term
    out_ref[:, :BINS] = (real_sum / SEG).astype(out_ref.dtype)
    out_ref[:, BINS:] = (imag_sum / SEG).astype(out_ref.dtype)


def taper_table(slabs_per_segment, width):
    position = jnp.arange(NFFT, dtype=jnp.int32).astype(jnp.float32)
    taper = 0.5 - 0.5 * jnp.cos(position * (2.0 * math.pi / NFFT))
    return taper.reshape(slabs_per_segment, width)


def _white_specs(slabs, block, width, per_segment):
    return [
        pl.BlockSpec((slabs, block, width), lambda i: (0, i, 0)),
        pl.BlockSpec((NFFT, 2 * BINS), lambda i: (0, 0), pipeline_mode=pl.Buffered(1)),
        pl.BlockSpec((per_segment, width), lambda i: (0, 0)),
    ]


def white_rows(parts, table, taper, block=32):
    slabs, rows, width = parts.shape
    specs = _white_specs(slabs, block, width, slabs // SEG)
    return pl.pallas_call(
        _white_kernel,
        out_shape=jax.ShapeDtypeStruct((2 * SEG, rows, BINS), jnp.bfloat16),
        grid=(rows // block,),
        in_specs=specs,
        out_specs=pl.BlockSpec((2 * SEG, block, BINS), lambda i: (0, i, 0)),
        compiler_params=pltpu.CompilerParams(vmem_limit_bytes=48 * 1024 * 1024),
        cost_estimate=pl.CostEstimate(
            flops=2 * SEG * rows * NFFT * 2 * BINS, transcendentals=SEG * rows * BINS,
            bytes_accessed=NFFT * 2 * BINS * 2 + 4 * slabs * rows * width,
        ),
    )(parts, table, taper)


def cross_rows(parts, first_white, table, taper, block=32):
    slabs, rows, width = parts.shape
    specs = _white_specs(slabs, block, width, slabs // SEG)
    specs.insert(1, pl.BlockSpec((2 * SEG, block, BINS), lambda i: (0, i, 0)))
    return pl.pallas_call(
        _cross_kernel,
        out_shape=jax.ShapeDtypeStruct((rows, 2 * BINS), jnp.bfloat16),
        grid=(rows // block,),
        in_specs=specs,
        out_specs=pl.BlockSpec((block, 2 * BINS), lambda i: (i, 0)),
        compiler_params=pltpu.CompilerParams(vmem_limit_bytes=48 * 1024 * 1024),
        cost_estimate=pl.CostEstimate(
            flops=2 * SEG * rows * NFFT * 2 * BINS, transcendentals=SEG * rows * BINS,
            bytes_accessed=NFFT * 2 * BINS * 2 + 8 * slabs * rows * width,
        ),
    )(parts, first_white, table, taper)


def _exchange_kernel(axis, x_ref, out_ref, landed, send_sems, recv_sems):
    count = x_ref.shape[0]
    me = lax.axis_index(axis)

    def peer_id(peer):
        return {axis: peer}

    barrier = pltpu.get_barrier_semaphore()
    for step in range(1, count):
        pl.semaphore_signal(
            barrier, inc=1, device_id=peer_id(lax.rem(me + step, count)), device_id_type=pl.DeviceIdType.MESH
        )
    pl.semaphore_wait(barrier, count - 1)
    copies = []
    for step in range(1, count):
        peer = lax.rem(me + step, count)
        copy = pltpu.make_async_remote_copy(
            src_ref=x_ref.at[peer],
            dst_ref=landed.at[me],
            send_sem=send_sems.at[step],
            recv_sem=recv_sems.at[step],
            device_id=peer_id(peer),
            device_id_type=pl.DeviceIdType.MESH,
        )
        copy.start()
        copies.append(copy)
    landed[me] = x_ref[me]
    for copy in copies:
        copy.wait_send()
        copy.wait_recv()
    out_ref[...] = landed[...]


def exchange(parts, axis, collective):
    count = parts.shape[0]
    return pl.pallas_call(
        functools.partial(_exchange_kernel, axis),
        out_shape=jax.ShapeDtypeStruct(parts.shape, parts.dtype),
        scratch_shapes=[
            pltpu.VMEM(parts.shape, parts.dtype),
            pltpu.SemaphoreType.DMA((count,)),
            pltpu.SemaphoreType.DMA((count,)),
        ],
        compiler_params=pltpu.CompilerParams(collective_id=collective, has_side_effects=True),
        cost_estimate=pl.CostEstimate(flops=0, transcendentals=0, bytes_accessed=4 * parts.size),
    )(parts)


def to_rows(parts):
    slabs, rows, width = parts.shape
    return jnp.transpose(parts, (1, 0, 2)).reshape(rows, slabs * width)


def local(records, first_station, second_region, second_station):
    regions = lax.axis_size("region")
    slabs = lax.axis_size("slab")
    pair_count = first_station.shape[0]
    width = records.shape[1]
    capacity = max(2, pair_count // regions + pair_count // 16)

    target = second_region[:, 0]
    onehot = (target[:, None] == jnp.arange(regions, dtype=jnp.int32)[None, :]).astype(jnp.int32)
    ranking = jnp.sum((jnp.cumsum(onehot, axis=0) - onehot) * onehot, axis=1)
    slot_index = target * capacity + ranking
    requests = (
        jnp.zeros((regions * capacity,), jnp.int32)
        .at[slot_index]
        .set(second_station)
    )
    packed = jnp.concatenate([first_station, slot_index, requests])
    plane = lax.all_gather(packed, "slab", axis=0, tiled=False)
    firsts = plane[:, :pair_count]
    slots = plane[:, pair_count : 2 * pair_count]
    plane_requests = plane[:, 2 * pair_count :].reshape(slabs, regions, capacity)

    first_parts = pick_rows(records, firsts.reshape(-1)).reshape(slabs, pair_count, width)
    first_arrived = exchange(first_parts, "slab", 0)
    table = dft_table()
    taper = taper_table(slabs // SEG, width)
    first_white = white_rows(first_arrived, table, taper)

    outgoing = jnp.transpose(plane_requests, (1, 0, 2)).reshape(regions, -1, 128)
    outgoing = jnp.pad(outgoing, ((0, 0), (0, (-outgoing.shape[1]) % 8), (0, 0)))
    asked = exchange(outgoing, "region", 1)[:, : slabs * capacity // 128].reshape(-1)
    served = pick_rows(records, asked)
    served = served.reshape(regions, slabs * capacity, width)
    arrived = lax.all_to_all(served, "region", split_axis=0, concat_axis=0, tiled=True)
    second_parts = compact_rows(arrived.reshape(regions, slabs, capacity, width), slots)
    second_arrived = lax.all_to_all(second_parts, "slab", split_axis=0, concat_axis=0, tiled=True)
    return cross_rows(second_arrived, first_white, table, taper)


def solution(mesh):
    placed = (
        P("region", "slab"),
        P(("region", "slab")),
        P(("region", "slab"), None),
        P(("region", "slab")),
    )
    return jax.shard_map(
        local, mesh=mesh, in_specs=placed, out_specs=P(("region", "slab"), None), check_vma=False
    )
```

```python
import functools
import math

import jax
import jax.numpy as jnp
from jax import lax
from jax.experimental import pallas as pl
from jax.experimental.pallas import tpu as pltpu
from jax.sharding import PartitionSpec as P

NFFT = 2048
BINS = 1024
SEG = 2
HALF = 4


def dft_table():
    low = 64
    high = NFFT // low
    frequency = jnp.arange(BINS, dtype=jnp.int32)[None, :]
    coarse = jnp.arange(high, dtype=jnp.int32)[:, None]
    fine = jnp.arange(low, dtype=jnp.int32)[:, None]
    angle_a = ((coarse * frequency) % high).astype(jnp.float32) * (2.0 * math.pi / high)
    angle_b = ((fine * frequency) % NFFT).astype(jnp.float32) * (2.0 * math.pi / NFFT)
    ca, sa = jnp.cos(angle_a)[:, None, :], jnp.sin(angle_a)[:, None, :]
    cb, sb = jnp.cos(angle_b)[None, :, :], jnp.sin(angle_b)[None, :, :]
    cos_part = (ca * cb - sa * sb).reshape(NFFT, BINS)
    sin_part = (sa * cb + ca * sb).reshape(NFFT, BINS)
    return jnp.concatenate([cos_part, -sin_part], axis=1).astype(jnp.bfloat16)


def whitened(traces):
    count = traces.shape[0]
    signal = traces.astype(jnp.float32).reshape(count * SEG, NFFT)
    signal = signal - jnp.mean(signal, axis=1, keepdims=True)
    position = jnp.arange(NFFT, dtype=jnp.int32).astype(jnp.float32)
    taper = 0.5 - 0.5 * jnp.cos(position * (2.0 * math.pi / NFFT))
    tapered = (signal * taper[None, :]).astype(jnp.bfloat16)
    spectrum = jnp.dot(tapered, dft_table(), preferred_element_type=jnp.float32)
    real_part = spectrum[:, :BINS]
    imag_part = spectrum[:, BINS:]
    amplitude = jnp.sqrt(real_part * real_part + imag_part * imag_part + 1e-06)
    padded = jnp.pad(amplitude, ((0, 0), (HALF, HALF)))
    smooth = jnp.zeros_like(amplitude)
    for offset in range(2 * HALF + 1):
        smooth = smooth + padded[:, offset : offset + BINS]
    smooth = smooth / (2 * HALF + 1)
    level = jnp.mean(amplitude, axis=1, keepdims=True)
    divisor = smooth + level + 1e-06
    white = spectrum / jnp.concatenate([divisor, divisor], axis=1)
    return white.astype(jnp.bfloat16).reshape(count, SEG * NFFT)


def cross(first_rows, second_rows):
    left = first_rows.astype(jnp.float32).reshape(first_rows.shape[:-1] + (SEG, 2, BINS))
    right = second_rows.astype(jnp.float32).reshape(second_rows.shape[:-1] + (SEG, 2, BINS))
    real_sum = jnp.mean(
        left[..., 0, :] * right[..., 0, :] + left[..., 1, :] * right[..., 1, :], axis=-2
    )
    imag_sum = jnp.mean(
        left[..., 0, :] * right[..., 1, :] - left[..., 1, :] * right[..., 0, :], axis=-2
    )
    return jnp.concatenate([real_sum, imag_sum], axis=-1).astype(jnp.bfloat16)


def _pick_kernel(ids_ref, table_ref, out_ref):
    ids = ids_ref[...]
    rows = table_ref.shape[0]
    onehot = (lax.broadcasted_iota(jnp.int32, (ids.shape[0], rows), 1) == ids).astype(table_ref.dtype)
    out_ref[...] = jnp.dot(onehot, table_ref[...], preferred_element_type=jnp.float32).astype(out_ref.dtype)


def pick_rows(table, ids, block=512):
    rows, width = table.shape
    count = ids.shape[0]
    block = min(block, count)
    return pl.pallas_call(
        _pick_kernel,
        out_shape=jax.ShapeDtypeStruct((count, width), table.dtype),
        grid=(count // block,),
        in_specs=[
            pl.BlockSpec((block, 1), lambda i: (i, 0)),
            pl.BlockSpec((rows, width), lambda i: (0, 0)),
        ],
        out_specs=pl.BlockSpec((block, width), lambda i: (i, 0)),
        cost_estimate=pl.CostEstimate(
            flops=2 * count * rows * width, transcendentals=0, bytes_accessed=2 * (rows + count) * width
        ),
    )(ids.reshape(count, 1), table)


def _compact_kernel(ids_ref, table_ref, out_ref):
    buckets, slabs, capacity, width = table_ref.shape
    for s in range(slabs):
        ids = ids_ref[s]
        table = table_ref[:, s].reshape(buckets * capacity, width)
        onehot = (lax.broadcasted_iota(jnp.int32, (ids.shape[0], buckets * capacity), 1) == ids).astype(table.dtype)
        out_ref[s] = jnp.dot(onehot, table, preferred_element_type=jnp.float32).astype(out_ref.dtype)


def compact_rows(arrived, slots):
    buckets, slabs, capacity, width = arrived.shape
    pairs = slots.shape[1]
    return pl.pallas_call(
        _compact_kernel,
        out_shape=jax.ShapeDtypeStruct((slabs, pairs, width), arrived.dtype),
        cost_estimate=pl.CostEstimate(
            flops=2 * slabs * pairs * buckets * capacity * width,
            transcendentals=0,
            bytes_accessed=2 * (buckets * capacity + pairs) * slabs * width,
        ),
    )(slots.reshape(slabs, pairs, 1), arrived)


def _white_block(x, table, taper):
    slabs, rows, width = x.shape
    per_segment = slabs // SEG
    signal = x.astype(jnp.float32)
    tapered = []
    for segment in range(SEG):
        part = signal[segment * per_segment : (segment + 1) * per_segment]
        mean = jnp.sum(jnp.sum(part, axis=2, keepdims=True), axis=0) / NFFT
        pieces = [((part[i] - mean) * taper[i : i + 1, :]).astype(jnp.bfloat16) for i in range(per_segment)]
        tapered.append(jnp.concatenate(pieces, axis=1))
    spectrum = jnp.dot(jnp.concatenate(tapered, axis=0), table, preferred_element_type=jnp.float32)
    real_part = spectrum[:, :BINS]
    imag_part = spectrum[:, BINS:]
    amplitude = jnp.sqrt(real_part * real_part + imag_part * imag_part + 1e-06)
    lane = lax.broadcasted_iota(jnp.int32, amplitude.shape, 1)
    smooth = jnp.zeros_like(amplitude)
    for offset in range(-HALF, HALF + 1):
        moved = amplitude if offset == 0 else pltpu.roll(amplitude, (-offset) % BINS, 1)
        inside = (lane + offset >= 0) & (lane + offset < BINS)
        smooth = smooth + jnp.where(inside, moved, 0.0)
    smooth = smooth / (2 * HALF + 1)
    level = jnp.sum(amplitude, axis=1, keepdims=True) / BINS
    divisor = smooth + level + 1e-06
    white_real = (real_part / divisor).astype(jnp.bfloat16)
    white_imag = (imag_part / divisor).astype(jnp.bfloat16)
    return white_real, white_imag


def _white_kernel(x_ref, table_ref, taper_ref, out_ref):
    rows = x_ref.shape[1]
    white_real, white_imag = _white_block(x_ref[...], table_ref[...], taper_ref[...])
    for segment in range(SEG):
        out_ref[2 * segment] = white_real[segment * rows : (segment + 1) * rows]
        out_ref[2 * segment + 1] = white_imag[segment * rows : (segment + 1) * rows]


def _cross_kernel(x_ref, first_ref, table_ref, taper_ref, out_ref):
    rows = x_ref.shape[1]
    white_real, white_imag = _white_block(x_ref[...], table_ref[...], taper_ref[...])
    real_sum = None
    imag_sum = None
    for segment in range(SEG):
        left_real = first_ref[2 * segment].astype(jnp.float32)
        left_imag = first_ref[2 * segment + 1].astype(jnp.float32)
        right_real = white_real[segment * rows : (segment + 1) * rows].astype(jnp.float32)
        right_imag = white_imag[segment * rows : (segment + 1) * rows].astype(jnp.float32)
        real_term = left_real * right_real + left_imag * right_imag
        imag_term = left_real * right_imag - left_imag * right_real
        real_sum = real_term if real_sum is None else real_sum + real_term
        imag_sum = imag_term if imag_sum is None else imag_sum + imag_term
    out_ref[:, :BINS] = (real_sum / SEG).astype(out_ref.dtype)
    out_ref[:, BINS:] = (imag_sum / SEG).astype(out_ref.dtype)


def taper_table(slabs_per_segment, width):
    position = jnp.arange(NFFT, dtype=jnp.int32).astype(jnp.float32)
    taper = 0.5 - 0.5 * jnp.cos(position * (2.0 * math.pi / NFFT))
    return taper.reshape(slabs_per_segment, width)


def _white_specs(slabs, block, width, per_segment):
    return [
        pl.BlockSpec((slabs, block, width), lambda i: (0, i, 0)),
        pl.BlockSpec((NFFT, 2 * BINS), lambda i: (0, 0), pipeline_mode=pl.Buffered(1)),
        pl.BlockSpec((per_segment, width), lambda i: (0, 0)),
    ]


def white_rows(parts, table, taper, block=32):
    slabs, rows, width = parts.shape
    specs = _white_specs(slabs, block, width, slabs // SEG)
    return pl.pallas_call(
        _white_kernel,
        out_shape=jax.ShapeDtypeStruct((2 * SEG, rows, BINS), jnp.bfloat16),
        grid=(rows // block,),
        in_specs=specs,
        out_specs=pl.BlockSpec((2 * SEG, block, BINS), lambda i: (0, i, 0)),
        compiler_params=pltpu.CompilerParams(vmem_limit_bytes=48 * 1024 * 1024),
        cost_estimate=pl.CostEstimate(
            flops=2 * SEG * rows * NFFT * 2 * BINS, transcendentals=SEG * rows * BINS,
            bytes_accessed=NFFT * 2 * BINS * 2 + 4 * slabs * rows * width,
        ),
    )(parts, table, taper)


def cross_rows(parts, first_white, table, taper, block=32):
    slabs, rows, width = parts.shape
    specs = _white_specs(slabs, block, width, slabs // SEG)
    specs.insert(1, pl.BlockSpec((2 * SEG, block, BINS), lambda i: (0, i, 0)))
    return pl.pallas_call(
        _cross_kernel,
        out_shape=jax.ShapeDtypeStruct((rows, 2 * BINS), jnp.bfloat16),
        grid=(rows // block,),
        in_specs=specs,
        out_specs=pl.BlockSpec((block, 2 * BINS), lambda i: (i, 0)),
        compiler_params=pltpu.CompilerParams(vmem_limit_bytes=48 * 1024 * 1024),
        cost_estimate=pl.CostEstimate(
            flops=2 * SEG * rows * NFFT * 2 * BINS, transcendentals=SEG * rows * BINS,
            bytes_accessed=NFFT * 2 * BINS * 2 + 8 * slabs * rows * width,
        ),
    )(parts, first_white, table, taper)


def _exchange_kernel(axis, x_ref, out_ref, landed, send_sems, recv_sems):
    count = x_ref.shape[0]
    me = lax.axis_index(axis)

    def peer_id(peer):
        return {axis: peer}

    barrier = pltpu.get_barrier_semaphore()
    for step in range(1, count):
        pl.semaphore_signal(
            barrier, inc=1, device_id=peer_id(lax.rem(me + step, count)), device_id_type=pl.DeviceIdType.MESH
        )
    pl.semaphore_wait(barrier, count - 1)
    copies = []
    for step in range(1, count):
        peer = lax.rem(me + step, count)
        copy = pltpu.make_async_remote_copy(
            src_ref=x_ref.at[peer],
            dst_ref=landed.at[me],
            send_sem=send_sems.at[step],
            recv_sem=recv_sems.at[step],
            device_id=peer_id(peer),
            device_id_type=pl.DeviceIdType.MESH,
        )
        copy.start()
        copies.append(copy)
    landed[me] = x_ref[me]
    for copy in copies:
        copy.wait_send()
        copy.wait_recv()
    out_ref[...] = landed[...]


def exchange(parts, axis, collective):
    count = parts.shape[0]
    return pl.pallas_call(
        functools.partial(_exchange_kernel, axis),
        out_shape=jax.ShapeDtypeStruct(parts.shape, parts.dtype),
        scratch_shapes=[
            pltpu.VMEM(parts.shape, parts.dtype),
            pltpu.SemaphoreType.DMA((count,)),
            pltpu.SemaphoreType.DMA((count,)),
        ],
        compiler_params=pltpu.CompilerParams(collective_id=collective, has_side_effects=True),
        cost_estimate=pl.CostEstimate(flops=0, transcendentals=0, bytes_accessed=4 * parts.size),
    )(parts)


def to_rows(parts):
    slabs, rows, width = parts.shape
    return jnp.transpose(parts, (1, 0, 2)).reshape(rows, slabs * width)


def local(records, first_station, second_region, second_station):
    regions = lax.axis_size("region")
    slabs = lax.axis_size("slab")
    pair_count = first_station.shape[0]
    width = records.shape[1]
    capacity = max(2, pair_count // regions + pair_count // 16)

    target = second_region[:, 0]
    onehot = (target[:, None] == jnp.arange(regions, dtype=jnp.int32)[None, :]).astype(jnp.int32)
    ranking = jnp.sum((jnp.cumsum(onehot, axis=0) - onehot) * onehot, axis=1)
    slot_index = target * capacity + ranking
    requests = (
        jnp.zeros((regions * capacity,), jnp.int32)
        .at[slot_index]
        .set(second_station)
    )
    packed = jnp.concatenate([first_station, slot_index, requests])
    plane = lax.all_gather(packed, "slab", axis=0, tiled=False)
    firsts = plane[:, :pair_count]
    slots = plane[:, pair_count : 2 * pair_count]
    plane_requests = plane[:, 2 * pair_count :].reshape(slabs, regions, capacity)

    first_parts = pick_rows(records, firsts.reshape(-1)).reshape(slabs, pair_count, width)
    first_arrived = exchange(first_parts, "slab", 0)
    table = dft_table()
    taper = taper_table(slabs // SEG, width)
    first_white = white_rows(first_arrived, table, taper)

    outgoing = jnp.transpose(plane_requests, (1, 0, 2)).reshape(regions, -1, 128)
    outgoing = jnp.pad(outgoing, ((0, 0), (0, (-outgoing.shape[1]) % 8), (0, 0)))
    asked = exchange(outgoing, "region", 1)[:, : slabs * capacity // 128].reshape(-1)
    served = pick_rows(records, asked)
    served = served.reshape(regions, slabs * capacity, width)
    arrived = lax.all_to_all(served, "region", split_axis=0, concat_axis=0, tiled=True)
    arrived, first_white = lax.optimization_barrier((arrived, first_white))
    second_parts = compact_rows(arrived.reshape(regions, slabs, capacity, width), slots)
    second_arrived = lax.all_to_all(second_parts, "slab", split_axis=0, concat_axis=0, tiled=True)
    return cross_rows(second_arrived, first_white, table, taper)


def solution(mesh):
    placed = (
        P("region", "slab"),
        P(("region", "slab")),
        P(("region", "slab"), None),
        P(("region", "slab")),
    )
    return jax.shard_map(
        local, mesh=mesh, in_specs=placed, out_specs=P(("region", "slab"), None), check_vma=False
    )
```

```python
import functools
import math

import jax
import jax.numpy as jnp
from jax import lax
from jax.experimental import pallas as pl
from jax.experimental.pallas import tpu as pltpu
from jax.sharding import PartitionSpec as P

NFFT = 2048
BINS = 1024
SEG = 2
HALF = 4


def dft_table():
    low = 64
    high = NFFT // low
    frequency = jnp.arange(BINS, dtype=jnp.int32)[None, :]
    coarse = jnp.arange(high, dtype=jnp.int32)[:, None]
    fine = jnp.arange(low, dtype=jnp.int32)[:, None]
    angle_a = ((coarse * frequency) % high).astype(jnp.float32) * (2.0 * math.pi / high)
    angle_b = ((fine * frequency) % NFFT).astype(jnp.float32) * (2.0 * math.pi / NFFT)
    ca, sa = jnp.cos(angle_a)[:, None, :], jnp.sin(angle_a)[:, None, :]
    cb, sb = jnp.cos(angle_b)[None, :, :], jnp.sin(angle_b)[None, :, :]
    cos_part = (ca * cb - sa * sb).reshape(NFFT, BINS)
    sin_part = (sa * cb + ca * sb).reshape(NFFT, BINS)
    return jnp.concatenate([cos_part, -sin_part], axis=1).astype(jnp.bfloat16)


def whitened(traces):
    count = traces.shape[0]
    signal = traces.astype(jnp.float32).reshape(count * SEG, NFFT)
    signal = signal - jnp.mean(signal, axis=1, keepdims=True)
    position = jnp.arange(NFFT, dtype=jnp.int32).astype(jnp.float32)
    taper = 0.5 - 0.5 * jnp.cos(position * (2.0 * math.pi / NFFT))
    tapered = (signal * taper[None, :]).astype(jnp.bfloat16)
    spectrum = jnp.dot(tapered, dft_table(), preferred_element_type=jnp.float32)
    real_part = spectrum[:, :BINS]
    imag_part = spectrum[:, BINS:]
    amplitude = jnp.sqrt(real_part * real_part + imag_part * imag_part + 1e-06)
    padded = jnp.pad(amplitude, ((0, 0), (HALF, HALF)))
    smooth = jnp.zeros_like(amplitude)
    for offset in range(2 * HALF + 1):
        smooth = smooth + padded[:, offset : offset + BINS]
    smooth = smooth / (2 * HALF + 1)
    level = jnp.mean(amplitude, axis=1, keepdims=True)
    divisor = smooth + level + 1e-06
    white = spectrum / jnp.concatenate([divisor, divisor], axis=1)
    return white.astype(jnp.bfloat16).reshape(count, SEG * NFFT)


def cross(first_rows, second_rows):
    left = first_rows.astype(jnp.float32).reshape(first_rows.shape[:-1] + (SEG, 2, BINS))
    right = second_rows.astype(jnp.float32).reshape(second_rows.shape[:-1] + (SEG, 2, BINS))
    real_sum = jnp.mean(
        left[..., 0, :] * right[..., 0, :] + left[..., 1, :] * right[..., 1, :], axis=-2
    )
    imag_sum = jnp.mean(
        left[..., 0, :] * right[..., 1, :] - left[..., 1, :] * right[..., 0, :], axis=-2
    )
    return jnp.concatenate([real_sum, imag_sum], axis=-1).astype(jnp.bfloat16)


def _pick_kernel(ids_ref, table_ref, out_ref):
    ids = ids_ref[...]
    rows = table_ref.shape[0]
    onehot = (lax.broadcasted_iota(jnp.int32, (ids.shape[0], rows), 1) == ids).astype(table_ref.dtype)
    out_ref[...] = jnp.dot(onehot, table_ref[...], preferred_element_type=jnp.float32).astype(out_ref.dtype)


def pick_rows(table, ids, block=512):
    rows, width = table.shape
    count = ids.shape[0]
    block = min(block, count)
    return pl.pallas_call(
        _pick_kernel,
        out_shape=jax.ShapeDtypeStruct((count, width), table.dtype),
        grid=(count // block,),
        in_specs=[
            pl.BlockSpec((block, 1), lambda i: (i, 0)),
            pl.BlockSpec((rows, width), lambda i: (0, 0)),
        ],
        out_specs=pl.BlockSpec((block, width), lambda i: (i, 0)),
        cost_estimate=pl.CostEstimate(
            flops=2 * count * rows * width, transcendentals=0, bytes_accessed=2 * (rows + count) * width
        ),
    )(ids.reshape(count, 1), table)


def _compact_kernel(ids_ref, table_ref, out_ref):
    buckets, slabs, capacity, width = table_ref.shape
    for s in range(slabs):
        ids = ids_ref[s]
        table = table_ref[:, s].reshape(buckets * capacity, width)
        onehot = (lax.broadcasted_iota(jnp.int32, (ids.shape[0], buckets * capacity), 1) == ids).astype(table.dtype)
        out_ref[s] = jnp.dot(onehot, table, preferred_element_type=jnp.float32).astype(out_ref.dtype)


def compact_rows(arrived, slots):
    buckets, slabs, capacity, width = arrived.shape
    pairs = slots.shape[1]
    return pl.pallas_call(
        _compact_kernel,
        out_shape=jax.ShapeDtypeStruct((slabs, pairs, width), arrived.dtype),
        cost_estimate=pl.CostEstimate(
            flops=2 * slabs * pairs * buckets * capacity * width,
            transcendentals=0,
            bytes_accessed=2 * (buckets * capacity + pairs) * slabs * width,
        ),
    )(slots.reshape(slabs, pairs, 1), arrived)


def _white_block(x, table, taper):
    slabs, rows, width = x.shape
    per_segment = slabs // SEG
    signal = x.astype(jnp.float32)
    tapered = []
    for segment in range(SEG):
        part = signal[segment * per_segment : (segment + 1) * per_segment]
        mean = jnp.sum(jnp.sum(part, axis=2, keepdims=True), axis=0) / NFFT
        pieces = [((part[i] - mean) * taper[i : i + 1, :]).astype(jnp.bfloat16) for i in range(per_segment)]
        tapered.append(jnp.concatenate(pieces, axis=1))
    spectrum = jnp.dot(jnp.concatenate(tapered, axis=0), table, preferred_element_type=jnp.float32)
    real_part = spectrum[:, :BINS]
    imag_part = spectrum[:, BINS:]
    amplitude = jnp.sqrt(real_part * real_part + imag_part * imag_part + 1e-06)
    lane = lax.broadcasted_iota(jnp.int32, amplitude.shape, 1)
    smooth = jnp.zeros_like(amplitude)
    for offset in range(-HALF, HALF + 1):
        moved = amplitude if offset == 0 else pltpu.roll(amplitude, (-offset) % BINS, 1)
        inside = (lane + offset >= 0) & (lane + offset < BINS)
        smooth = smooth + jnp.where(inside, moved, 0.0)
    smooth = smooth / (2 * HALF + 1)
    level = jnp.sum(amplitude, axis=1, keepdims=True) / BINS
    divisor = smooth + level + 1e-06
    white_real = (real_part / divisor).astype(jnp.bfloat16)
    white_imag = (imag_part / divisor).astype(jnp.bfloat16)
    return white_real, white_imag


def _white_kernel(x_ref, table_ref, taper_ref, out_ref):
    rows = x_ref.shape[1]
    white_real, white_imag = _white_block(x_ref[...], table_ref[...], taper_ref[...])
    for segment in range(SEG):
        out_ref[2 * segment] = white_real[segment * rows : (segment + 1) * rows]
        out_ref[2 * segment + 1] = white_imag[segment * rows : (segment + 1) * rows]


def _cross_kernel(x_ref, first_ref, table_ref, taper_ref, out_ref):
    rows = x_ref.shape[1]
    white_real, white_imag = _white_block(x_ref[...], table_ref[...], taper_ref[...])
    real_sum = None
    imag_sum = None
    for segment in range(SEG):
        left_real = first_ref[2 * segment].astype(jnp.float32)
        left_imag = first_ref[2 * segment + 1].astype(jnp.float32)
        right_real = white_real[segment * rows : (segment + 1) * rows].astype(jnp.float32)
        right_imag = white_imag[segment * rows : (segment + 1) * rows].astype(jnp.float32)
        real_term = left_real * right_real + left_imag * right_imag
        imag_term = left_real * right_imag - left_imag * right_real
        real_sum = real_term if real_sum is None else real_sum + real_term
        imag_sum = imag_term if imag_sum is None else imag_sum + imag_term
    out_ref[:, :BINS] = (real_sum / SEG).astype(out_ref.dtype)
    out_ref[:, BINS:] = (imag_sum / SEG).astype(out_ref.dtype)


def taper_table(slabs_per_segment, width):
    position = jnp.arange(NFFT, dtype=jnp.int32).astype(jnp.float32)
    taper = 0.5 - 0.5 * jnp.cos(position * (2.0 * math.pi / NFFT))
    return taper.reshape(slabs_per_segment, width)


def _white_specs(slabs, block, width, per_segment):
    return [
        pl.BlockSpec((slabs, block, width), lambda i: (0, i, 0)),
        pl.BlockSpec((NFFT, 2 * BINS), lambda i: (0, 0), pipeline_mode=pl.Buffered(1)),
        pl.BlockSpec((per_segment, width), lambda i: (0, 0)),
    ]


def white_rows(parts, table, taper, block=32):
    slabs, rows, width = parts.shape
    specs = _white_specs(slabs, block, width, slabs // SEG)
    return pl.pallas_call(
        _white_kernel,
        out_shape=jax.ShapeDtypeStruct((2 * SEG, rows, BINS), jnp.bfloat16),
        grid=(rows // block,),
        in_specs=specs,
        out_specs=pl.BlockSpec((2 * SEG, block, BINS), lambda i: (0, i, 0)),
        compiler_params=pltpu.CompilerParams(vmem_limit_bytes=48 * 1024 * 1024),
        cost_estimate=pl.CostEstimate(
            flops=2 * SEG * rows * NFFT * 2 * BINS, transcendentals=SEG * rows * BINS,
            bytes_accessed=NFFT * 2 * BINS * 2 + 4 * slabs * rows * width,
        ),
    )(parts, table, taper)


def cross_rows(parts, first_white, table, taper, block=32):
    slabs, rows, width = parts.shape
    specs = _white_specs(slabs, block, width, slabs // SEG)
    specs.insert(1, pl.BlockSpec((2 * SEG, block, BINS), lambda i: (0, i, 0)))
    return pl.pallas_call(
        _cross_kernel,
        out_shape=jax.ShapeDtypeStruct((rows, 2 * BINS), jnp.bfloat16),
        grid=(rows // block,),
        in_specs=specs,
        out_specs=pl.BlockSpec((block, 2 * BINS), lambda i: (i, 0)),
        compiler_params=pltpu.CompilerParams(vmem_limit_bytes=48 * 1024 * 1024),
        cost_estimate=pl.CostEstimate(
            flops=2 * SEG * rows * NFFT * 2 * BINS, transcendentals=SEG * rows * BINS,
            bytes_accessed=NFFT * 2 * BINS * 2 + 8 * slabs * rows * width,
        ),
    )(parts, first_white, table, taper)


def _exchange_kernel(axis, x_ref, out_ref, landed, send_sems, recv_sems):
    count = x_ref.shape[0]
    me = lax.axis_index(axis)

    def peer_id(peer):
        return {axis: peer}

    barrier = pltpu.get_barrier_semaphore()
    for step in range(1, count):
        pl.semaphore_signal(
            barrier, inc=1, device_id=peer_id(lax.rem(me + step, count)), device_id_type=pl.DeviceIdType.MESH
        )
    pl.semaphore_wait(barrier, count - 1)
    copies = []
    for step in range(1, count):
        peer = lax.rem(me + step, count)
        copy = pltpu.make_async_remote_copy(
            src_ref=x_ref.at[peer],
            dst_ref=landed.at[me],
            send_sem=send_sems.at[step],
            recv_sem=recv_sems.at[step],
            device_id=peer_id(peer),
            device_id_type=pl.DeviceIdType.MESH,
        )
        copy.start()
        copies.append(copy)
    landed[me] = x_ref[me]
    for copy in copies:
        copy.wait_send()
        copy.wait_recv()
    out_ref[...] = landed[...]


def exchange(parts, axis, collective):
    count = parts.shape[0]
    return pl.pallas_call(
        functools.partial(_exchange_kernel, axis),
        out_shape=jax.ShapeDtypeStruct(parts.shape, parts.dtype),
        scratch_shapes=[
            pltpu.VMEM(parts.shape, parts.dtype),
            pltpu.SemaphoreType.DMA((count,)),
            pltpu.SemaphoreType.DMA((count,)),
        ],
        compiler_params=pltpu.CompilerParams(collective_id=collective, has_side_effects=True),
        cost_estimate=pl.CostEstimate(flops=0, transcendentals=0, bytes_accessed=4 * parts.size),
    )(parts)


def to_rows(parts):
    slabs, rows, width = parts.shape
    return jnp.transpose(parts, (1, 0, 2)).reshape(rows, slabs * width)


def local(records, first_station, second_region, second_station):
    regions = lax.axis_size("region")
    slabs = lax.axis_size("slab")
    pair_count = first_station.shape[0]
    width = records.shape[1]
    capacity = max(2, pair_count // regions + pair_count // 16)

    target = second_region[:, 0]
    onehot = (target[:, None] == jnp.arange(regions, dtype=jnp.int32)[None, :]).astype(jnp.int32)
    ranking = jnp.sum((jnp.cumsum(onehot, axis=0) - onehot) * onehot, axis=1)
    slot_index = target * capacity + ranking
    requests = (
        jnp.zeros((regions * capacity,), jnp.int32)
        .at[slot_index]
        .set(second_station)
    )
    packed = jnp.concatenate([first_station, slot_index, requests])
    plane = lax.all_gather(packed, "slab", axis=0, tiled=False)
    firsts = plane[:, :pair_count]
    slots = plane[:, pair_count : 2 * pair_count]
    plane_requests = plane[:, 2 * pair_count :].reshape(slabs, regions, capacity)

    first_parts = pick_rows(records, firsts.reshape(-1)).reshape(slabs, pair_count, width)
    first_arrived = exchange(first_parts, "slab", 0)
    table = dft_table()
    taper = taper_table(slabs // SEG, width)
    first_white = white_rows(first_arrived, table, taper)

    outgoing = jnp.transpose(plane_requests, (1, 0, 2)).reshape(regions, -1, 128)
    outgoing = jnp.pad(outgoing, ((0, 0), (0, (-outgoing.shape[1]) % 8), (0, 0)))
    asked = exchange(outgoing, "region", 1)[:, : slabs * capacity // 128].reshape(-1)
    served = pick_rows(records, asked)
    served = served.reshape(regions * slabs, capacity, width)
    arrived = lax.all_to_all(served, ("region", "slab"), split_axis=0, concat_axis=0, tiled=True)
    arrived, first_white = lax.optimization_barrier((arrived, first_white))
    own_slots = jnp.broadcast_to(slot_index[None, :], (slabs, pair_count))
    second_arrived = compact_rows(arrived.reshape(regions, slabs, capacity, width), own_slots)
    return cross_rows(second_arrived, first_white, table, taper)


def solution(mesh):
    placed = (
        P("region", "slab"),
        P(("region", "slab")),
        P(("region", "slab"), None),
        P(("region", "slab")),
    )
    return jax.shard_map(
        local, mesh=mesh, in_specs=placed, out_specs=P(("region", "slab"), None), check_vma=False
    )
```

```python
import functools
import math

import jax
import jax.numpy as jnp
from jax import lax
from jax.experimental import pallas as pl
from jax.experimental.pallas import tpu as pltpu
from jax.sharding import PartitionSpec as P

NFFT = 2048
BINS = 1024
SEG = 2
HALF = 4


def dft_table():
    low = 64
    high = NFFT // low
    frequency = jnp.arange(BINS, dtype=jnp.int32)[None, :]
    coarse = jnp.arange(high, dtype=jnp.int32)[:, None]
    fine = jnp.arange(low, dtype=jnp.int32)[:, None]
    angle_a = ((coarse * frequency) % high).astype(jnp.float32) * (2.0 * math.pi / high)
    angle_b = ((fine * frequency) % NFFT).astype(jnp.float32) * (2.0 * math.pi / NFFT)
    ca, sa = jnp.cos(angle_a)[:, None, :], jnp.sin(angle_a)[:, None, :]
    cb, sb = jnp.cos(angle_b)[None, :, :], jnp.sin(angle_b)[None, :, :]
    cos_part = (ca * cb - sa * sb).reshape(NFFT, BINS)
    sin_part = (sa * cb + ca * sb).reshape(NFFT, BINS)
    return jnp.concatenate([cos_part, -sin_part], axis=1).astype(jnp.bfloat16)


def whitened(traces):
    count = traces.shape[0]
    signal = traces.astype(jnp.float32).reshape(count * SEG, NFFT)
    signal = signal - jnp.mean(signal, axis=1, keepdims=True)
    position = jnp.arange(NFFT, dtype=jnp.int32).astype(jnp.float32)
    taper = 0.5 - 0.5 * jnp.cos(position * (2.0 * math.pi / NFFT))
    tapered = (signal * taper[None, :]).astype(jnp.bfloat16)
    spectrum = jnp.dot(tapered, dft_table(), preferred_element_type=jnp.float32)
    real_part = spectrum[:, :BINS]
    imag_part = spectrum[:, BINS:]
    amplitude = jnp.sqrt(real_part * real_part + imag_part * imag_part + 1e-06)
    padded = jnp.pad(amplitude, ((0, 0), (HALF, HALF)))
    smooth = jnp.zeros_like(amplitude)
    for offset in range(2 * HALF + 1):
        smooth = smooth + padded[:, offset : offset + BINS]
    smooth = smooth / (2 * HALF + 1)
    level = jnp.mean(amplitude, axis=1, keepdims=True)
    divisor = smooth + level + 1e-06
    white = spectrum / jnp.concatenate([divisor, divisor], axis=1)
    return white.astype(jnp.bfloat16).reshape(count, SEG * NFFT)


def cross(first_rows, second_rows):
    left = first_rows.astype(jnp.float32).reshape(first_rows.shape[:-1] + (SEG, 2, BINS))
    right = second_rows.astype(jnp.float32).reshape(second_rows.shape[:-1] + (SEG, 2, BINS))
    real_sum = jnp.mean(
        left[..., 0, :] * right[..., 0, :] + left[..., 1, :] * right[..., 1, :], axis=-2
    )
    imag_sum = jnp.mean(
        left[..., 0, :] * right[..., 1, :] - left[..., 1, :] * right[..., 0, :], axis=-2
    )
    return jnp.concatenate([real_sum, imag_sum], axis=-1).astype(jnp.bfloat16)


def _pick_kernel(ids_ref, table_ref, out_ref):
    ids = ids_ref[...]
    rows = table_ref.shape[0]
    onehot = (lax.broadcasted_iota(jnp.int32, (ids.shape[0], rows), 1) == ids).astype(table_ref.dtype)
    out_ref[...] = jnp.dot(onehot, table_ref[...], preferred_element_type=jnp.float32).astype(out_ref.dtype)


def pick_rows(table, ids, block=512):
    rows, width = table.shape
    count = ids.shape[0]
    block = min(block, count)
    return pl.pallas_call(
        _pick_kernel,
        out_shape=jax.ShapeDtypeStruct((count, width), table.dtype),
        grid=(count // block,),
        in_specs=[
            pl.BlockSpec((block, 1), lambda i: (i, 0)),
            pl.BlockSpec((rows, width), lambda i: (0, 0)),
        ],
        out_specs=pl.BlockSpec((block, width), lambda i: (i, 0)),
        cost_estimate=pl.CostEstimate(
            flops=2 * count * rows * width, transcendentals=0, bytes_accessed=2 * (rows + count) * width
        ),
    )(ids.reshape(count, 1), table)


def _compact_kernel(ids_ref, table_ref, out_ref):
    buckets, slabs, capacity, width = table_ref.shape
    for s in range(slabs):
        ids = ids_ref[s]
        table = table_ref[:, s].reshape(buckets * capacity, width)
        onehot = (lax.broadcasted_iota(jnp.int32, (ids.shape[0], buckets * capacity), 1) == ids).astype(table.dtype)
        out_ref[s] = jnp.dot(onehot, table, preferred_element_type=jnp.float32).astype(out_ref.dtype)


def compact_rows(arrived, slots):
    buckets, slabs, capacity, width = arrived.shape
    pairs = slots.shape[1]
    return pl.pallas_call(
        _compact_kernel,
        out_shape=jax.ShapeDtypeStruct((slabs, pairs, width), arrived.dtype),
        cost_estimate=pl.CostEstimate(
            flops=2 * slabs * pairs * buckets * capacity * width,
            transcendentals=0,
            bytes_accessed=2 * (buckets * capacity + pairs) * slabs * width,
        ),
    )(slots.reshape(slabs, pairs, 1), arrived)


def _white_block(x, table, taper):
    slabs, rows, width = x.shape
    per_segment = slabs // SEG
    signal = x.astype(jnp.float32)
    tapered = []
    for segment in range(SEG):
        part = signal[segment * per_segment : (segment + 1) * per_segment]
        mean = jnp.sum(jnp.sum(part, axis=2, keepdims=True), axis=0) / NFFT
        pieces = [((part[i] - mean) * taper[i : i + 1, :]).astype(jnp.bfloat16) for i in range(per_segment)]
        tapered.append(jnp.concatenate(pieces, axis=1))
    spectrum = jnp.dot(jnp.concatenate(tapered, axis=0), table, preferred_element_type=jnp.float32)
    real_part = spectrum[:, :BINS]
    imag_part = spectrum[:, BINS:]
    amplitude = jnp.sqrt(real_part * real_part + imag_part * imag_part + 1e-06)
    lane = lax.broadcasted_iota(jnp.int32, amplitude.shape, 1)
    smooth = jnp.zeros_like(amplitude)
    for offset in range(-HALF, HALF + 1):
        moved = amplitude if offset == 0 else pltpu.roll(amplitude, (-offset) % BINS, 1)
        inside = (lane + offset >= 0) & (lane + offset < BINS)
        smooth = smooth + jnp.where(inside, moved, 0.0)
    smooth = smooth / (2 * HALF + 1)
    level = jnp.sum(amplitude, axis=1, keepdims=True) / BINS
    divisor = smooth + level + 1e-06
    white_real = (real_part / divisor).astype(jnp.bfloat16)
    white_imag = (imag_part / divisor).astype(jnp.bfloat16)
    return white_real, white_imag


def _white_kernel(x_ref, table_ref, taper_ref, out_ref):
    rows = x_ref.shape[1]
    white_real, white_imag = _white_block(x_ref[...], table_ref[...], taper_ref[...])
    for segment in range(SEG):
        out_ref[2 * segment] = white_real[segment * rows : (segment + 1) * rows]
        out_ref[2 * segment + 1] = white_imag[segment * rows : (segment + 1) * rows]


def _cross_kernel(x_ref, first_ref, table_ref, taper_ref, out_ref):
    rows = x_ref.shape[1]
    white_real, white_imag = _white_block(x_ref[...], table_ref[...], taper_ref[...])
    real_sum = None
    imag_sum = None
    for segment in range(SEG):
        left_real = first_ref[2 * segment].astype(jnp.float32)
        left_imag = first_ref[2 * segment + 1].astype(jnp.float32)
        right_real = white_real[segment * rows : (segment + 1) * rows].astype(jnp.float32)
        right_imag = white_imag[segment * rows : (segment + 1) * rows].astype(jnp.float32)
        real_term = left_real * right_real + left_imag * right_imag
        imag_term = left_real * right_imag - left_imag * right_real
        real_sum = real_term if real_sum is None else real_sum + real_term
        imag_sum = imag_term if imag_sum is None else imag_sum + imag_term
    out_ref[:, :BINS] = (real_sum / SEG).astype(out_ref.dtype)
    out_ref[:, BINS:] = (imag_sum / SEG).astype(out_ref.dtype)


def taper_table(slabs_per_segment, width):
    position = jnp.arange(NFFT, dtype=jnp.int32).astype(jnp.float32)
    taper = 0.5 - 0.5 * jnp.cos(position * (2.0 * math.pi / NFFT))
    return taper.reshape(slabs_per_segment, width)


def _white_specs(slabs, block, width, per_segment):
    return [
        pl.BlockSpec((slabs, block, width), lambda i: (0, i, 0)),
        pl.BlockSpec((NFFT, 2 * BINS), lambda i: (0, 0), pipeline_mode=pl.Buffered(1)),
        pl.BlockSpec((per_segment, width), lambda i: (0, 0)),
    ]


def white_rows(parts, table, taper, block=32):
    slabs, rows, width = parts.shape
    specs = _white_specs(slabs, block, width, slabs // SEG)
    return pl.pallas_call(
        _white_kernel,
        out_shape=jax.ShapeDtypeStruct((2 * SEG, rows, BINS), jnp.bfloat16),
        grid=(rows // block,),
        in_specs=specs,
        out_specs=pl.BlockSpec((2 * SEG, block, BINS), lambda i: (0, i, 0)),
        compiler_params=pltpu.CompilerParams(vmem_limit_bytes=48 * 1024 * 1024),
        cost_estimate=pl.CostEstimate(
            flops=2 * SEG * rows * NFFT * 2 * BINS, transcendentals=SEG * rows * BINS,
            bytes_accessed=NFFT * 2 * BINS * 2 + 4 * slabs * rows * width,
        ),
    )(parts, table, taper)


def cross_rows(parts, first_white, table, taper, block=32):
    slabs, rows, width = parts.shape
    specs = _white_specs(slabs, block, width, slabs // SEG)
    specs.insert(1, pl.BlockSpec((2 * SEG, block, BINS), lambda i: (0, i, 0)))
    return pl.pallas_call(
        _cross_kernel,
        out_shape=jax.ShapeDtypeStruct((rows, 2 * BINS), jnp.bfloat16),
        grid=(rows // block,),
        in_specs=specs,
        out_specs=pl.BlockSpec((block, 2 * BINS), lambda i: (i, 0)),
        compiler_params=pltpu.CompilerParams(vmem_limit_bytes=48 * 1024 * 1024),
        cost_estimate=pl.CostEstimate(
            flops=2 * SEG * rows * NFFT * 2 * BINS, transcendentals=SEG * rows * BINS,
            bytes_accessed=NFFT * 2 * BINS * 2 + 8 * slabs * rows * width,
        ),
    )(parts, first_white, table, taper)


def _exchange_kernel(axis, x_ref, out_ref, landed, send_sems, recv_sems):
    count = x_ref.shape[0]
    me = lax.axis_index(axis)

    def peer_id(peer):
        return {axis: peer}

    barrier = pltpu.get_barrier_semaphore()
    for step in range(1, count):
        pl.semaphore_signal(
            barrier, inc=1, device_id=peer_id(lax.rem(me + step, count)), device_id_type=pl.DeviceIdType.MESH
        )
    pl.semaphore_wait(barrier, count - 1)
    copies = []
    for step in range(1, count):
        peer = lax.rem(me + step, count)
        copy = pltpu.make_async_remote_copy(
            src_ref=x_ref.at[peer],
            dst_ref=landed.at[me],
            send_sem=send_sems.at[step],
            recv_sem=recv_sems.at[step],
            device_id=peer_id(peer),
            device_id_type=pl.DeviceIdType.MESH,
        )
        copy.start()
        copies.append(copy)
    landed[me] = x_ref[me]
    for copy in copies:
        copy.wait_send()
        copy.wait_recv()
    out_ref[...] = landed[...]


def exchange(parts, axis, collective):
    count = parts.shape[0]
    return pl.pallas_call(
        functools.partial(_exchange_kernel, axis),
        out_shape=jax.ShapeDtypeStruct(parts.shape, parts.dtype),
        scratch_shapes=[
            pltpu.VMEM(parts.shape, parts.dtype),
            pltpu.SemaphoreType.DMA((count,)),
            pltpu.SemaphoreType.DMA((count,)),
        ],
        compiler_params=pltpu.CompilerParams(collective_id=collective, has_side_effects=True),
        cost_estimate=pl.CostEstimate(flops=0, transcendentals=0, bytes_accessed=4 * parts.size),
    )(parts)


def to_rows(parts):
    slabs, rows, width = parts.shape
    return jnp.transpose(parts, (1, 0, 2)).reshape(rows, slabs * width)


def local(records, first_station, second_region, second_station):
    regions = lax.axis_size("region")
    slabs = lax.axis_size("slab")
    pair_count = first_station.shape[0]
    width = records.shape[1]
    capacity = max(2, pair_count // regions + pair_count // 16)

    target = second_region[:, 0]
    onehot = (target[:, None] == jnp.arange(regions, dtype=jnp.int32)[None, :]).astype(jnp.int32)
    ranking = jnp.sum((jnp.cumsum(onehot, axis=0) - onehot) * onehot, axis=1)
    slot_index = target * capacity + ranking
    requests = (
        jnp.zeros((regions * capacity,), jnp.int32)
        .at[slot_index]
        .set(second_station)
    )
    outgoing = jnp.broadcast_to(requests.reshape(regions, 1, capacity), (regions, slabs, capacity))
    asked = lax.all_to_all(outgoing.reshape(regions * slabs, capacity), ("region", "slab"), split_axis=0, concat_axis=0, tiled=True)
    asked = asked.reshape(-1)

    firsts = lax.all_gather(first_station, "slab", axis=0, tiled=False)
    first_parts = pick_rows(records, firsts.reshape(-1)).reshape(slabs, pair_count, width)
    first_arrived = exchange(first_parts, "slab", 0)
    table = dft_table()
    taper = taper_table(slabs // SEG, width)
    first_white = white_rows(first_arrived, table, taper)

    served = pick_rows(records, asked)
    served = served.reshape(regions * slabs, capacity, width)
    arrived = lax.all_to_all(served, ("region", "slab"), split_axis=0, concat_axis=0, tiled=True)
    arrived, first_white = lax.optimization_barrier((arrived, first_white))
    own_slots = jnp.broadcast_to(slot_index[None, :], (slabs, pair_count))
    second_arrived = compact_rows(arrived.reshape(regions, slabs, capacity, width), own_slots)
    return cross_rows(second_arrived, first_white, table, taper)


def solution(mesh):
    placed = (
        P("region", "slab"),
        P(("region", "slab")),
        P(("region", "slab"), None),
        P(("region", "slab")),
    )
    return jax.shard_map(
        local, mesh=mesh, in_specs=placed, out_specs=P(("region", "slab"), None), check_vma=False
    )
```

```python
import functools
import math

import jax
import jax.numpy as jnp
from jax import lax
from jax.experimental import pallas as pl
from jax.experimental.pallas import tpu as pltpu
from jax.sharding import PartitionSpec as P

NFFT = 2048
BINS = 1024
SEG = 2
HALF = 4


def dft_table():
    low = 64
    high = NFFT // low
    frequency = jnp.arange(BINS, dtype=jnp.int32)[None, :]
    coarse = jnp.arange(high, dtype=jnp.int32)[:, None]
    fine = jnp.arange(low, dtype=jnp.int32)[:, None]
    angle_a = ((coarse * frequency) % high).astype(jnp.float32) * (2.0 * math.pi / high)
    angle_b = ((fine * frequency) % NFFT).astype(jnp.float32) * (2.0 * math.pi / NFFT)
    ca, sa = jnp.cos(angle_a)[:, None, :], jnp.sin(angle_a)[:, None, :]
    cb, sb = jnp.cos(angle_b)[None, :, :], jnp.sin(angle_b)[None, :, :]
    cos_part = (ca * cb - sa * sb).reshape(NFFT, BINS)
    sin_part = (sa * cb + ca * sb).reshape(NFFT, BINS)
    return jnp.concatenate([cos_part, -sin_part], axis=1).astype(jnp.bfloat16)


def whitened(traces):
    count = traces.shape[0]
    signal = traces.astype(jnp.float32).reshape(count * SEG, NFFT)
    signal = signal - jnp.mean(signal, axis=1, keepdims=True)
    position = jnp.arange(NFFT, dtype=jnp.int32).astype(jnp.float32)
    taper = 0.5 - 0.5 * jnp.cos(position * (2.0 * math.pi / NFFT))
    tapered = (signal * taper[None, :]).astype(jnp.bfloat16)
    spectrum = jnp.dot(tapered, dft_table(), preferred_element_type=jnp.float32)
    real_part = spectrum[:, :BINS]
    imag_part = spectrum[:, BINS:]
    amplitude = jnp.sqrt(real_part * real_part + imag_part * imag_part + 1e-06)
    padded = jnp.pad(amplitude, ((0, 0), (HALF, HALF)))
    smooth = jnp.zeros_like(amplitude)
    for offset in range(2 * HALF + 1):
        smooth = smooth + padded[:, offset : offset + BINS]
    smooth = smooth / (2 * HALF + 1)
    level = jnp.mean(amplitude, axis=1, keepdims=True)
    divisor = smooth + level + 1e-06
    white = spectrum / jnp.concatenate([divisor, divisor], axis=1)
    return white.astype(jnp.bfloat16).reshape(count, SEG * NFFT)


def cross(first_rows, second_rows):
    left = first_rows.astype(jnp.float32).reshape(first_rows.shape[:-1] + (SEG, 2, BINS))
    right = second_rows.astype(jnp.float32).reshape(second_rows.shape[:-1] + (SEG, 2, BINS))
    real_sum = jnp.mean(
        left[..., 0, :] * right[..., 0, :] + left[..., 1, :] * right[..., 1, :], axis=-2
    )
    imag_sum = jnp.mean(
        left[..., 0, :] * right[..., 1, :] - left[..., 1, :] * right[..., 0, :], axis=-2
    )
    return jnp.concatenate([real_sum, imag_sum], axis=-1).astype(jnp.bfloat16)


def _pick_kernel(ids_ref, table_ref, out_ref):
    ids = ids_ref[...]
    rows = table_ref.shape[0]
    onehot = (lax.broadcasted_iota(jnp.int32, (ids.shape[0], rows), 1) == ids).astype(table_ref.dtype)
    out_ref[...] = jnp.dot(onehot, table_ref[...], preferred_element_type=jnp.float32).astype(out_ref.dtype)


def pick_rows(table, ids, block=512):
    rows, width = table.shape
    count = ids.shape[0]
    block = min(block, count)
    return pl.pallas_call(
        _pick_kernel,
        out_shape=jax.ShapeDtypeStruct((count, width), table.dtype),
        grid=(count // block,),
        in_specs=[
            pl.BlockSpec((block, 1), lambda i: (i, 0)),
            pl.BlockSpec((rows, width), lambda i: (0, 0)),
        ],
        out_specs=pl.BlockSpec((block, width), lambda i: (i, 0)),
        cost_estimate=pl.CostEstimate(
            flops=2 * count * rows * width, transcendentals=0, bytes_accessed=2 * (rows + count) * width
        ),
    )(ids.reshape(count, 1), table)


def _compact_kernel(ids_ref, table_ref, out_ref):
    buckets, slabs, capacity, width = table_ref.shape
    for s in range(slabs):
        ids = ids_ref[s]
        table = table_ref[:, s].reshape(buckets * capacity, width)
        onehot = (lax.broadcasted_iota(jnp.int32, (ids.shape[0], buckets * capacity), 1) == ids).astype(table.dtype)
        out_ref[s] = jnp.dot(onehot, table, preferred_element_type=jnp.float32).astype(out_ref.dtype)


def compact_rows(arrived, slots):
    buckets, slabs, capacity, width = arrived.shape
    pairs = slots.shape[1]
    return pl.pallas_call(
        _compact_kernel,
        out_shape=jax.ShapeDtypeStruct((slabs, pairs, width), arrived.dtype),
        cost_estimate=pl.CostEstimate(
            flops=2 * slabs * pairs * buckets * capacity * width,
            transcendentals=0,
            bytes_accessed=2 * (buckets * capacity + pairs) * slabs * width,
        ),
    )(slots.reshape(slabs, pairs, 1), arrived)


def _white_block(slices, table, taper):
    per_segment = len(slices) // SEG
    tapered = []
    for segment in range(SEG):
        part = [piece.astype(jnp.float32) for piece in slices[segment * per_segment : (segment + 1) * per_segment]]
        total = jnp.sum(part[0], axis=1, keepdims=True)
        for piece in part[1:]:
            total = total + jnp.sum(piece, axis=1, keepdims=True)
        mean = total / NFFT
        pieces = [((part[i] - mean) * taper[i : i + 1, :]).astype(jnp.bfloat16) for i in range(per_segment)]
        tapered.append(jnp.concatenate(pieces, axis=1))
    spectrum = jnp.dot(jnp.concatenate(tapered, axis=0), table, preferred_element_type=jnp.float32)
    real_part = spectrum[:, :BINS]
    imag_part = spectrum[:, BINS:]
    amplitude = jnp.sqrt(real_part * real_part + imag_part * imag_part + 1e-06)
    lane = lax.broadcasted_iota(jnp.int32, amplitude.shape, 1)
    smooth = jnp.zeros_like(amplitude)
    for offset in range(-HALF, HALF + 1):
        moved = amplitude if offset == 0 else pltpu.roll(amplitude, (-offset) % BINS, 1)
        inside = (lane + offset >= 0) & (lane + offset < BINS)
        smooth = smooth + jnp.where(inside, moved, 0.0)
    smooth = smooth / (2 * HALF + 1)
    level = jnp.sum(amplitude, axis=1, keepdims=True) / BINS
    divisor = smooth + level + 1e-06
    white_real = (real_part / divisor).astype(jnp.bfloat16)
    white_imag = (imag_part / divisor).astype(jnp.bfloat16)
    return white_real, white_imag


def _white_kernel(x_ref, table_ref, taper_ref, out_ref):
    rows = x_ref.shape[1]
    slices = [x_ref[i] for i in range(x_ref.shape[0])]
    white_real, white_imag = _white_block(slices, table_ref[...], taper_ref[...])
    for segment in range(SEG):
        out_ref[2 * segment] = white_real[segment * rows : (segment + 1) * rows]
        out_ref[2 * segment + 1] = white_imag[segment * rows : (segment + 1) * rows]


def _cross_kernel(ids_ref, arrived_ref, first_ref, table_ref, taper_ref, out_ref):
    buckets, slabs, capacity, width = arrived_ref.shape
    ids = ids_ref[...]
    rows = ids.shape[0]
    onehot = (lax.broadcasted_iota(jnp.int32, (rows, buckets * capacity), 1) == ids).astype(arrived_ref.dtype)
    slices = [
        jnp.dot(onehot, arrived_ref[:, s].reshape(buckets * capacity, width), preferred_element_type=jnp.float32).astype(
            arrived_ref.dtype
        )
        for s in range(slabs)
    ]
    white_real, white_imag = _white_block(slices, table_ref[...], taper_ref[...])
    real_sum = None
    imag_sum = None
    for segment in range(SEG):
        left_real = first_ref[2 * segment].astype(jnp.float32)
        left_imag = first_ref[2 * segment + 1].astype(jnp.float32)
        right_real = white_real[segment * rows : (segment + 1) * rows].astype(jnp.float32)
        right_imag = white_imag[segment * rows : (segment + 1) * rows].astype(jnp.float32)
        real_term = left_real * right_real + left_imag * right_imag
        imag_term = left_real * right_imag - left_imag * right_real
        real_sum = real_term if real_sum is None else real_sum + real_term
        imag_sum = imag_term if imag_sum is None else imag_sum + imag_term
    out_ref[:, :BINS] = (real_sum / SEG).astype(out_ref.dtype)
    out_ref[:, BINS:] = (imag_sum / SEG).astype(out_ref.dtype)


def taper_table(slabs_per_segment, width):
    position = jnp.arange(NFFT, dtype=jnp.int32).astype(jnp.float32)
    taper = 0.5 - 0.5 * jnp.cos(position * (2.0 * math.pi / NFFT))
    return taper.reshape(slabs_per_segment, width)


def _white_specs(slabs, block, width, per_segment):
    return [
        pl.BlockSpec((slabs, block, width), lambda i: (0, i, 0)),
        pl.BlockSpec((NFFT, 2 * BINS), lambda i: (0, 0), pipeline_mode=pl.Buffered(1)),
        pl.BlockSpec((per_segment, width), lambda i: (0, 0)),
    ]


def white_rows(parts, table, taper, block=32):
    slabs, rows, width = parts.shape
    specs = _white_specs(slabs, block, width, slabs // SEG)
    return pl.pallas_call(
        _white_kernel,
        out_shape=jax.ShapeDtypeStruct((2 * SEG, rows, BINS), jnp.bfloat16),
        grid=(rows // block,),
        in_specs=specs,
        out_specs=pl.BlockSpec((2 * SEG, block, BINS), lambda i: (0, i, 0)),
        compiler_params=pltpu.CompilerParams(vmem_limit_bytes=48 * 1024 * 1024),
        cost_estimate=pl.CostEstimate(
            flops=2 * SEG * rows * NFFT * 2 * BINS, transcendentals=SEG * rows * BINS,
            bytes_accessed=NFFT * 2 * BINS * 2 + 4 * slabs * rows * width,
        ),
    )(parts, table, taper)


def cross_rows(arrived, slots, first_white, table, taper, block=32):
    buckets, slabs, capacity, width = arrived.shape
    rows = slots.shape[0]
    return pl.pallas_call(
        _cross_kernel,
        out_shape=jax.ShapeDtypeStruct((rows, 2 * BINS), jnp.bfloat16),
        grid=(rows // block,),
        in_specs=[
            pl.BlockSpec((block, 1), lambda i: (i, 0)),
            pl.BlockSpec(arrived.shape, lambda i: (0, 0, 0, 0), pipeline_mode=pl.Buffered(1)),
            pl.BlockSpec((2 * SEG, block, BINS), lambda i: (0, i, 0)),
            pl.BlockSpec((NFFT, 2 * BINS), lambda i: (0, 0), pipeline_mode=pl.Buffered(1)),
            pl.BlockSpec((slabs // SEG, width), lambda i: (0, 0)),
        ],
        out_specs=pl.BlockSpec((block, 2 * BINS), lambda i: (i, 0)),
        compiler_params=pltpu.CompilerParams(vmem_limit_bytes=48 * 1024 * 1024),
        cost_estimate=pl.CostEstimate(
            flops=2 * SEG * rows * NFFT * 2 * BINS, transcendentals=SEG * rows * BINS,
            bytes_accessed=NFFT * 2 * BINS * 2 + 2 * arrived.size,
        ),
    )(slots.reshape(rows, 1), arrived, first_white, table, taper)


def _exchange_kernel(axis, x_ref, out_ref, landed, send_sems, recv_sems):
    count = x_ref.shape[0]
    me = lax.axis_index(axis)

    def peer_id(peer):
        return {axis: peer}

    barrier = pltpu.get_barrier_semaphore()
    for step in range(1, count):
        pl.semaphore_signal(
            barrier, inc=1, device_id=peer_id(lax.rem(me + step, count)), device_id_type=pl.DeviceIdType.MESH
        )
    pl.semaphore_wait(barrier, count - 1)
    copies = []
    for step in range(1, count):
        peer = lax.rem(me + step, count)
        copy = pltpu.make_async_remote_copy(
            src_ref=x_ref.at[peer],
            dst_ref=landed.at[me],
            send_sem=send_sems.at[step],
            recv_sem=recv_sems.at[step],
            device_id=peer_id(peer),
            device_id_type=pl.DeviceIdType.MESH,
        )
        copy.start()
        copies.append(copy)
    landed[me] = x_ref[me]
    for copy in copies:
        copy.wait_send()
        copy.wait_recv()
    out_ref[...] = landed[...]


def exchange(parts, axis, collective):
    count = parts.shape[0]
    return pl.pallas_call(
        functools.partial(_exchange_kernel, axis),
        out_shape=jax.ShapeDtypeStruct(parts.shape, parts.dtype),
        scratch_shapes=[
            pltpu.VMEM(parts.shape, parts.dtype),
            pltpu.SemaphoreType.DMA((count,)),
            pltpu.SemaphoreType.DMA((count,)),
        ],
        compiler_params=pltpu.CompilerParams(collective_id=collective, has_side_effects=True),
        cost_estimate=pl.CostEstimate(flops=0, transcendentals=0, bytes_accessed=4 * parts.size),
    )(parts)


def to_rows(parts):
    slabs, rows, width = parts.shape
    return jnp.transpose(parts, (1, 0, 2)).reshape(rows, slabs * width)


def local(records, first_station, second_region, second_station):
    regions = lax.axis_size("region")
    slabs = lax.axis_size("slab")
    pair_count = first_station.shape[0]
    width = records.shape[1]
    capacity = max(2, pair_count // regions + pair_count // 16)

    target = second_region[:, 0]
    onehot = (target[:, None] == jnp.arange(regions, dtype=jnp.int32)[None, :]).astype(jnp.int32)
    ranking = jnp.sum((jnp.cumsum(onehot, axis=0) - onehot) * onehot, axis=1)
    slot_index = target * capacity + ranking
    requests = (
        jnp.zeros((regions * capacity,), jnp.int32)
        .at[slot_index]
        .set(second_station)
    )
    outgoing = jnp.broadcast_to(requests.reshape(regions, 1, capacity), (regions, slabs, capacity))
    asked = lax.all_to_all(outgoing.reshape(regions * slabs, capacity), ("region", "slab"), split_axis=0, concat_axis=0, tiled=True)
    asked = asked.reshape(-1)

    firsts = lax.all_gather(first_station, "slab", axis=0, tiled=False)
    first_parts = pick_rows(records, firsts.reshape(-1)).reshape(slabs, pair_count, width)
    first_arrived = exchange(first_parts, "slab", 0)
    table = dft_table()
    taper = taper_table(slabs // SEG, width)
    first_white = white_rows(first_arrived, table, taper)

    served = pick_rows(records, asked)
    served = served.reshape(regions * slabs, capacity, width)
    arrived = lax.all_to_all(served, ("region", "slab"), split_axis=0, concat_axis=0, tiled=True)
    arrived, first_white = lax.optimization_barrier((arrived, first_white))
    return cross_rows(arrived.reshape(regions, slabs, capacity, width), slot_index, first_white, table, taper)

def solution(mesh):
    placed = (
        P("region", "slab"),
        P(("region", "slab")),
        P(("region", "slab"), None),
        P(("region", "slab")),
    )
    return jax.shard_map(
        local, mesh=mesh, in_specs=placed, out_specs=P(("region", "slab"), None), check_vma=False
    )
```

```python
import functools
import math

import jax
import jax.numpy as jnp
from jax import lax
from jax.experimental import pallas as pl
from jax.experimental.pallas import tpu as pltpu
from jax.sharding import PartitionSpec as P

NFFT = 2048
BINS = 1024
SEG = 2
HALF = 4


def dft_table():
    low = 64
    high = NFFT // low
    frequency = jnp.arange(BINS, dtype=jnp.int32)[None, :]
    coarse = jnp.arange(high, dtype=jnp.int32)[:, None]
    fine = jnp.arange(low, dtype=jnp.int32)[:, None]
    angle_a = ((coarse * frequency) % high).astype(jnp.float32) * (2.0 * math.pi / high)
    angle_b = ((fine * frequency) % NFFT).astype(jnp.float32) * (2.0 * math.pi / NFFT)
    ca, sa = jnp.cos(angle_a)[:, None, :], jnp.sin(angle_a)[:, None, :]
    cb, sb = jnp.cos(angle_b)[None, :, :], jnp.sin(angle_b)[None, :, :]
    cos_part = (ca * cb - sa * sb).reshape(NFFT, BINS)
    sin_part = (sa * cb + ca * sb).reshape(NFFT, BINS)
    return jnp.concatenate([cos_part, -sin_part], axis=1).astype(jnp.bfloat16)


def whitened(traces):
    count = traces.shape[0]
    signal = traces.astype(jnp.float32).reshape(count * SEG, NFFT)
    signal = signal - jnp.mean(signal, axis=1, keepdims=True)
    position = jnp.arange(NFFT, dtype=jnp.int32).astype(jnp.float32)
    taper = 0.5 - 0.5 * jnp.cos(position * (2.0 * math.pi / NFFT))
    tapered = (signal * taper[None, :]).astype(jnp.bfloat16)
    spectrum = jnp.dot(tapered, dft_table(), preferred_element_type=jnp.float32)
    real_part = spectrum[:, :BINS]
    imag_part = spectrum[:, BINS:]
    amplitude = jnp.sqrt(real_part * real_part + imag_part * imag_part + 1e-06)
    padded = jnp.pad(amplitude, ((0, 0), (HALF, HALF)))
    smooth = jnp.zeros_like(amplitude)
    for offset in range(2 * HALF + 1):
        smooth = smooth + padded[:, offset : offset + BINS]
    smooth = smooth / (2 * HALF + 1)
    level = jnp.mean(amplitude, axis=1, keepdims=True)
    divisor = smooth + level + 1e-06
    white = spectrum / jnp.concatenate([divisor, divisor], axis=1)
    return white.astype(jnp.bfloat16).reshape(count, SEG * NFFT)


def cross(first_rows, second_rows):
    left = first_rows.astype(jnp.float32).reshape(first_rows.shape[:-1] + (SEG, 2, BINS))
    right = second_rows.astype(jnp.float32).reshape(second_rows.shape[:-1] + (SEG, 2, BINS))
    real_sum = jnp.mean(
        left[..., 0, :] * right[..., 0, :] + left[..., 1, :] * right[..., 1, :], axis=-2
    )
    imag_sum = jnp.mean(
        left[..., 0, :] * right[..., 1, :] - left[..., 1, :] * right[..., 0, :], axis=-2
    )
    return jnp.concatenate([real_sum, imag_sum], axis=-1).astype(jnp.bfloat16)


def _pick_kernel(ids_ref, table_ref, out_ref):
    ids = ids_ref[...]
    rows = table_ref.shape[0]
    onehot = (lax.broadcasted_iota(jnp.int32, (ids.shape[0], rows), 1) == ids).astype(table_ref.dtype)
    out_ref[...] = jnp.dot(onehot, table_ref[...], preferred_element_type=jnp.float32).astype(out_ref.dtype)


def pick_rows(table, ids, block=512):
    rows, width = table.shape
    count = ids.shape[0]
    block = min(block, count)
    return pl.pallas_call(
        _pick_kernel,
        out_shape=jax.ShapeDtypeStruct((count, width), table.dtype),
        grid=(count // block,),
        in_specs=[
            pl.BlockSpec((block, 1), lambda i: (i, 0)),
            pl.BlockSpec((rows, width), lambda i: (0, 0)),
        ],
        out_specs=pl.BlockSpec((block, width), lambda i: (i, 0)),
        cost_estimate=pl.CostEstimate(
            flops=2 * count * rows * width, transcendentals=0, bytes_accessed=2 * (rows + count) * width
        ),
    )(ids.reshape(count, 1), table)


def _compact_kernel(ids_ref, table_ref, out_ref):
    buckets, slabs, capacity, width = table_ref.shape
    for s in range(slabs):
        ids = ids_ref[s]
        table = table_ref[:, s].reshape(buckets * capacity, width)
        onehot = (lax.broadcasted_iota(jnp.int32, (ids.shape[0], buckets * capacity), 1) == ids).astype(table.dtype)
        out_ref[s] = jnp.dot(onehot, table, preferred_element_type=jnp.float32).astype(out_ref.dtype)


def compact_rows(arrived, slots):
    buckets, slabs, capacity, width = arrived.shape
    pairs = slots.shape[1]
    return pl.pallas_call(
        _compact_kernel,
        out_shape=jax.ShapeDtypeStruct((slabs, pairs, width), arrived.dtype),
        cost_estimate=pl.CostEstimate(
            flops=2 * slabs * pairs * buckets * capacity * width,
            transcendentals=0,
            bytes_accessed=2 * (buckets * capacity + pairs) * slabs * width,
        ),
    )(slots.reshape(slabs, pairs, 1), arrived)


def _white_block(slices, table, taper):
    per_segment = len(slices) // SEG
    tapered = []
    for segment in range(SEG):
        part = [piece.astype(jnp.float32) for piece in slices[segment * per_segment : (segment + 1) * per_segment]]
        total = jnp.sum(part[0], axis=1, keepdims=True)
        for piece in part[1:]:
            total = total + jnp.sum(piece, axis=1, keepdims=True)
        mean = total / NFFT
        pieces = [((part[i] - mean) * taper[i : i + 1, :]).astype(jnp.bfloat16) for i in range(per_segment)]
        tapered.append(jnp.concatenate(pieces, axis=1))
    spectrum = jnp.dot(jnp.concatenate(tapered, axis=0), table, preferred_element_type=jnp.float32)
    real_part = spectrum[:, :BINS]
    imag_part = spectrum[:, BINS:]
    amplitude = jnp.sqrt(real_part * real_part + imag_part * imag_part + 1e-06)
    lane = lax.broadcasted_iota(jnp.int32, amplitude.shape, 1)
    smooth = jnp.zeros_like(amplitude)
    for offset in range(-HALF, HALF + 1):
        moved = amplitude if offset == 0 else pltpu.roll(amplitude, (-offset) % BINS, 1)
        inside = (lane + offset >= 0) & (lane + offset < BINS)
        smooth = smooth + jnp.where(inside, moved, 0.0)
    smooth = smooth / (2 * HALF + 1)
    level = jnp.sum(amplitude, axis=1, keepdims=True) / BINS
    divisor = smooth + level + 1e-06
    white_real = (real_part / divisor).astype(jnp.bfloat16)
    white_imag = (imag_part / divisor).astype(jnp.bfloat16)
    return white_real, white_imag


def _white_kernel(x_ref, table_ref, taper_ref, out_ref):
    rows = x_ref.shape[1]
    slices = [x_ref[i] for i in range(x_ref.shape[0])]
    white_real, white_imag = _white_block(slices, table_ref[...], taper_ref[...])
    for segment in range(SEG):
        out_ref[2 * segment] = white_real[segment * rows : (segment + 1) * rows]
        out_ref[2 * segment + 1] = white_imag[segment * rows : (segment + 1) * rows]


def _cross_kernel(ids_ref, arrived_ref, first_ref, table_ref, taper_ref, out_ref):
    buckets, slabs, capacity, width = arrived_ref.shape
    ids = ids_ref[...]
    rows = ids.shape[0]
    onehot = (lax.broadcasted_iota(jnp.int32, (rows, buckets * capacity), 1) == ids).astype(arrived_ref.dtype)
    slices = [
        jnp.dot(onehot, arrived_ref[:, s].reshape(buckets * capacity, width), preferred_element_type=jnp.float32).astype(
            arrived_ref.dtype
        )
        for s in range(slabs)
    ]
    white_real, white_imag = _white_block(slices, table_ref[...], taper_ref[...])
    real_sum = None
    imag_sum = None
    for segment in range(SEG):
        left_real = first_ref[2 * segment].astype(jnp.float32)
        left_imag = first_ref[2 * segment + 1].astype(jnp.float32)
        right_real = white_real[segment * rows : (segment + 1) * rows].astype(jnp.float32)
        right_imag = white_imag[segment * rows : (segment + 1) * rows].astype(jnp.float32)
        real_term = left_real * right_real + left_imag * right_imag
        imag_term = left_real * right_imag - left_imag * right_real
        real_sum = real_term if real_sum is None else real_sum + real_term
        imag_sum = imag_term if imag_sum is None else imag_sum + imag_term
    out_ref[:, :BINS] = (real_sum / SEG).astype(out_ref.dtype)
    out_ref[:, BINS:] = (imag_sum / SEG).astype(out_ref.dtype)


def taper_table(slabs_per_segment, width):
    position = jnp.arange(NFFT, dtype=jnp.int32).astype(jnp.float32)
    taper = 0.5 - 0.5 * jnp.cos(position * (2.0 * math.pi / NFFT))
    return taper.reshape(slabs_per_segment, width)


def _white_specs(slabs, block, width, per_segment):
    return [
        pl.BlockSpec((slabs, block, width), lambda i: (0, i, 0)),
        pl.BlockSpec((NFFT, 2 * BINS), lambda i: (0, 0), pipeline_mode=pl.Buffered(1)),
        pl.BlockSpec((per_segment, width), lambda i: (0, 0)),
    ]


def white_rows(parts, table, taper, block=128):
    slabs, rows, width = parts.shape
    specs = _white_specs(slabs, block, width, slabs // SEG)
    return pl.pallas_call(
        _white_kernel,
        out_shape=jax.ShapeDtypeStruct((2 * SEG, rows, BINS), jnp.bfloat16),
        grid=(rows // block,),
        in_specs=specs,
        out_specs=pl.BlockSpec((2 * SEG, block, BINS), lambda i: (0, i, 0)),
        compiler_params=pltpu.CompilerParams(vmem_limit_bytes=48 * 1024 * 1024),
        cost_estimate=pl.CostEstimate(
            flops=2 * SEG * rows * NFFT * 2 * BINS, transcendentals=SEG * rows * BINS,
            bytes_accessed=NFFT * 2 * BINS * 2 + 4 * slabs * rows * width,
        ),
    )(parts, table, taper)


def cross_rows(arrived, slots, first_white, table, taper, block=128):
    buckets, slabs, capacity, width = arrived.shape
    rows = slots.shape[0]
    return pl.pallas_call(
        _cross_kernel,
        out_shape=jax.ShapeDtypeStruct((rows, 2 * BINS), jnp.bfloat16),
        grid=(rows // block,),
        in_specs=[
            pl.BlockSpec((block, 1), lambda i: (i, 0)),
            pl.BlockSpec(arrived.shape, lambda i: (0, 0, 0, 0), pipeline_mode=pl.Buffered(1)),
            pl.BlockSpec((2 * SEG, block, BINS), lambda i: (0, i, 0)),
            pl.BlockSpec((NFFT, 2 * BINS), lambda i: (0, 0), pipeline_mode=pl.Buffered(1)),
            pl.BlockSpec((slabs // SEG, width), lambda i: (0, 0)),
        ],
        out_specs=pl.BlockSpec((block, 2 * BINS), lambda i: (i, 0)),
        compiler_params=pltpu.CompilerParams(vmem_limit_bytes=48 * 1024 * 1024),
        cost_estimate=pl.CostEstimate(
            flops=2 * SEG * rows * NFFT * 2 * BINS, transcendentals=SEG * rows * BINS,
            bytes_accessed=NFFT * 2 * BINS * 2 + 2 * arrived.size,
        ),
    )(slots.reshape(rows, 1), arrived, first_white, table, taper)


def _exchange_kernel(axis, x_ref, out_ref, landed, send_sems, recv_sems):
    count = x_ref.shape[0]
    me = lax.axis_index(axis)

    def peer_id(peer):
        return {axis: peer}

    barrier = pltpu.get_barrier_semaphore()
    for step in range(1, count):
        pl.semaphore_signal(
            barrier, inc=1, device_id=peer_id(lax.rem(me + step, count)), device_id_type=pl.DeviceIdType.MESH
        )
    pl.semaphore_wait(barrier, count - 1)
    copies = []
    for step in range(1, count):
        peer = lax.rem(me + step, count)
        copy = pltpu.make_async_remote_copy(
            src_ref=x_ref.at[peer],
            dst_ref=landed.at[me],
            send_sem=send_sems.at[step],
            recv_sem=recv_sems.at[step],
            device_id=peer_id(peer),
            device_id_type=pl.DeviceIdType.MESH,
        )
        copy.start()
        copies.append(copy)
    landed[me] = x_ref[me]
    for copy in copies:
        copy.wait_send()
        copy.wait_recv()
    out_ref[...] = landed[...]


def exchange(parts, axis, collective):
    count = parts.shape[0]
    return pl.pallas_call(
        functools.partial(_exchange_kernel, axis),
        out_shape=jax.ShapeDtypeStruct(parts.shape, parts.dtype),
        scratch_shapes=[
            pltpu.VMEM(parts.shape, parts.dtype),
            pltpu.SemaphoreType.DMA((count,)),
            pltpu.SemaphoreType.DMA((count,)),
        ],
        compiler_params=pltpu.CompilerParams(collective_id=collective, has_side_effects=True),
        cost_estimate=pl.CostEstimate(flops=0, transcendentals=0, bytes_accessed=4 * parts.size),
    )(parts)


def to_rows(parts):
    slabs, rows, width = parts.shape
    return jnp.transpose(parts, (1, 0, 2)).reshape(rows, slabs * width)


def local(records, first_station, second_region, second_station):
    regions = lax.axis_size("region")
    slabs = lax.axis_size("slab")
    pair_count = first_station.shape[0]
    width = records.shape[1]
    capacity = max(2, pair_count // regions + pair_count // 16)

    target = second_region[:, 0]
    onehot = (target[:, None] == jnp.arange(regions, dtype=jnp.int32)[None, :]).astype(jnp.int32)
    ranking = jnp.sum((jnp.cumsum(onehot, axis=0) - onehot) * onehot, axis=1)
    slot_index = target * capacity + ranking
    requests = (
        jnp.zeros((regions * capacity,), jnp.int32)
        .at[slot_index]
        .set(second_station)
    )
    outgoing = jnp.broadcast_to(requests.reshape(regions, 1, capacity), (regions, slabs, capacity))
    asked = lax.all_to_all(outgoing.reshape(regions * slabs, capacity), ("region", "slab"), split_axis=0, concat_axis=0, tiled=True)
    asked = asked.reshape(-1)

    firsts = lax.all_gather(first_station, "slab", axis=0, tiled=False)
    first_parts = pick_rows(records, firsts.reshape(-1)).reshape(slabs, pair_count, width)
    first_arrived = exchange(first_parts, "slab", 0)
    table = dft_table()
    taper = taper_table(slabs // SEG, width)
    first_white = white_rows(first_arrived, table, taper)

    served = pick_rows(records, asked)
    served = served.reshape(regions * slabs, capacity, width)
    arrived = lax.all_to_all(served, ("region", "slab"), split_axis=0, concat_axis=0, tiled=True)
    arrived, first_white = lax.optimization_barrier((arrived, first_white))
    return cross_rows(arrived.reshape(regions, slabs, capacity, width), slot_index, first_white, table, taper)

def solution(mesh):
    placed = (
        P("region", "slab"),
        P(("region", "slab")),
        P(("region", "slab"), None),
        P(("region", "slab")),
    )
    return jax.shard_map(
        local, mesh=mesh, in_specs=placed, out_specs=P(("region", "slab"), None), check_vma=False
    )
```

```python
import functools
import math

import jax
import jax.numpy as jnp
from jax import lax
from jax.experimental import pallas as pl
from jax.experimental.pallas import tpu as pltpu
from jax.sharding import PartitionSpec as P

NFFT = 2048
BINS = 1024
SEG = 2
HALF = 4


def dft_table():
    low = 64
    high = NFFT // low
    frequency = jnp.arange(BINS, dtype=jnp.int32)[None, :]
    coarse = jnp.arange(high, dtype=jnp.int32)[:, None]
    fine = jnp.arange(low, dtype=jnp.int32)[:, None]
    angle_a = ((coarse * frequency) % high).astype(jnp.float32) * (2.0 * math.pi / high)
    angle_b = ((fine * frequency) % NFFT).astype(jnp.float32) * (2.0 * math.pi / NFFT)
    ca, sa = jnp.cos(angle_a)[:, None, :], jnp.sin(angle_a)[:, None, :]
    cb, sb = jnp.cos(angle_b)[None, :, :], jnp.sin(angle_b)[None, :, :]
    cos_part = (ca * cb - sa * sb).reshape(NFFT, BINS)
    sin_part = (sa * cb + ca * sb).reshape(NFFT, BINS)
    return jnp.concatenate([cos_part, -sin_part], axis=1).astype(jnp.bfloat16)


def whitened(traces):
    count = traces.shape[0]
    signal = traces.astype(jnp.float32).reshape(count * SEG, NFFT)
    signal = signal - jnp.mean(signal, axis=1, keepdims=True)
    position = jnp.arange(NFFT, dtype=jnp.int32).astype(jnp.float32)
    taper = 0.5 - 0.5 * jnp.cos(position * (2.0 * math.pi / NFFT))
    tapered = (signal * taper[None, :]).astype(jnp.bfloat16)
    spectrum = jnp.dot(tapered, dft_table(), preferred_element_type=jnp.float32)
    real_part = spectrum[:, :BINS]
    imag_part = spectrum[:, BINS:]
    amplitude = jnp.sqrt(real_part * real_part + imag_part * imag_part + 1e-06)
    padded = jnp.pad(amplitude, ((0, 0), (HALF, HALF)))
    smooth = jnp.zeros_like(amplitude)
    for offset in range(2 * HALF + 1):
        smooth = smooth + padded[:, offset : offset + BINS]
    smooth = smooth / (2 * HALF + 1)
    level = jnp.mean(amplitude, axis=1, keepdims=True)
    divisor = smooth + level + 1e-06
    white = spectrum / jnp.concatenate([divisor, divisor], axis=1)
    return white.astype(jnp.bfloat16).reshape(count, SEG * NFFT)


def cross(first_rows, second_rows):
    left = first_rows.astype(jnp.float32).reshape(first_rows.shape[:-1] + (SEG, 2, BINS))
    right = second_rows.astype(jnp.float32).reshape(second_rows.shape[:-1] + (SEG, 2, BINS))
    real_sum = jnp.mean(
        left[..., 0, :] * right[..., 0, :] + left[..., 1, :] * right[..., 1, :], axis=-2
    )
    imag_sum = jnp.mean(
        left[..., 0, :] * right[..., 1, :] - left[..., 1, :] * right[..., 0, :], axis=-2
    )
    return jnp.concatenate([real_sum, imag_sum], axis=-1).astype(jnp.bfloat16)


def _pick_kernel(ids_ref, table_ref, out_ref):
    ids = ids_ref[...]
    rows = table_ref.shape[0]
    onehot = (lax.broadcasted_iota(jnp.int32, (ids.shape[0], rows), 1) == ids).astype(table_ref.dtype)
    out_ref[...] = jnp.dot(onehot, table_ref[...], preferred_element_type=jnp.float32).astype(out_ref.dtype)


def pick_rows(table, ids, block=512):
    rows, width = table.shape
    count = ids.shape[0]
    block = min(block, count)
    return pl.pallas_call(
        _pick_kernel,
        out_shape=jax.ShapeDtypeStruct((count, width), table.dtype),
        grid=(count // block,),
        in_specs=[
            pl.BlockSpec((block, 1), lambda i: (i, 0)),
            pl.BlockSpec((rows, width), lambda i: (0, 0)),
        ],
        out_specs=pl.BlockSpec((block, width), lambda i: (i, 0)),
        cost_estimate=pl.CostEstimate(
            flops=2 * count * rows * width, transcendentals=0, bytes_accessed=2 * (rows + count) * width
        ),
    )(ids.reshape(count, 1), table)


def _compact_kernel(ids_ref, table_ref, out_ref):
    buckets, slabs, capacity, width = table_ref.shape
    for s in range(slabs):
        ids = ids_ref[s]
        table = table_ref[:, s].reshape(buckets * capacity, width)
        onehot = (lax.broadcasted_iota(jnp.int32, (ids.shape[0], buckets * capacity), 1) == ids).astype(table.dtype)
        out_ref[s] = jnp.dot(onehot, table, preferred_element_type=jnp.float32).astype(out_ref.dtype)


def compact_rows(arrived, slots):
    buckets, slabs, capacity, width = arrived.shape
    pairs = slots.shape[1]
    return pl.pallas_call(
        _compact_kernel,
        out_shape=jax.ShapeDtypeStruct((slabs, pairs, width), arrived.dtype),
        cost_estimate=pl.CostEstimate(
            flops=2 * slabs * pairs * buckets * capacity * width,
            transcendentals=0,
            bytes_accessed=2 * (buckets * capacity + pairs) * slabs * width,
        ),
    )(slots.reshape(slabs, pairs, 1), arrived)


def _white_block(slices, table, taper):
    per_segment = len(slices) // SEG
    tapered = []
    for segment in range(SEG):
        part = [piece.astype(jnp.float32) for piece in slices[segment * per_segment : (segment + 1) * per_segment]]
        total = jnp.sum(part[0], axis=1, keepdims=True)
        for piece in part[1:]:
            total = total + jnp.sum(piece, axis=1, keepdims=True)
        mean = total / NFFT
        pieces = [((part[i] - mean) * taper[i : i + 1, :]).astype(jnp.bfloat16) for i in range(per_segment)]
        tapered.append(jnp.concatenate(pieces, axis=1))
    spectrum = jnp.dot(jnp.concatenate(tapered, axis=0), table, preferred_element_type=jnp.float32)
    real_part = spectrum[:, :BINS]
    imag_part = spectrum[:, BINS:]
    amplitude = jnp.sqrt(real_part * real_part + imag_part * imag_part + 1e-06)
    lane = lax.broadcasted_iota(jnp.int32, amplitude.shape, 1)
    smooth = jnp.zeros_like(amplitude)
    for offset in range(-HALF, HALF + 1):
        moved = amplitude if offset == 0 else pltpu.roll(amplitude, (-offset) % BINS, 1)
        inside = (lane + offset >= 0) & (lane + offset < BINS)
        smooth = smooth + jnp.where(inside, moved, 0.0)
    smooth = smooth / (2 * HALF + 1)
    level = jnp.sum(amplitude, axis=1, keepdims=True) / BINS
    divisor = smooth + level + 1e-06
    white_real = (real_part / divisor).astype(jnp.bfloat16)
    white_imag = (imag_part / divisor).astype(jnp.bfloat16)
    return white_real, white_imag


def _white_kernel(x_ref, table_ref, taper_ref, out_ref):
    rows = x_ref.shape[1]
    slices = [x_ref[i] for i in range(x_ref.shape[0])]
    white_real, white_imag = _white_block(slices, table_ref[...], taper_ref[...])
    for segment in range(SEG):
        out_ref[2 * segment] = white_real[segment * rows : (segment + 1) * rows]
        out_ref[2 * segment + 1] = white_imag[segment * rows : (segment + 1) * rows]


def _cross_kernel(ids_ref, arrived_ref, first_ref, table_ref, taper_ref, out_ref):
    buckets, slabs, capacity, width = arrived_ref.shape
    ids = ids_ref[...]
    rows = ids.shape[0]
    onehot = (lax.broadcasted_iota(jnp.int32, (rows, buckets * capacity), 1) == ids).astype(arrived_ref.dtype)
    slices = [
        jnp.dot(onehot, arrived_ref[:, s].reshape(buckets * capacity, width), preferred_element_type=jnp.float32).astype(
            arrived_ref.dtype
        )
        for s in range(slabs)
    ]
    white_real, white_imag = _white_block(slices, table_ref[...], taper_ref[...])
    real_sum = None
    imag_sum = None
    for segment in range(SEG):
        left_real = first_ref[2 * segment].astype(jnp.float32)
        left_imag = first_ref[2 * segment + 1].astype(jnp.float32)
        right_real = white_real[segment * rows : (segment + 1) * rows].astype(jnp.float32)
        right_imag = white_imag[segment * rows : (segment + 1) * rows].astype(jnp.float32)
        real_term = left_real * right_real + left_imag * right_imag
        imag_term = left_real * right_imag - left_imag * right_real
        real_sum = real_term if real_sum is None else real_sum + real_term
        imag_sum = imag_term if imag_sum is None else imag_sum + imag_term
    out_ref[:, :BINS] = (real_sum / SEG).astype(out_ref.dtype)
    out_ref[:, BINS:] = (imag_sum / SEG).astype(out_ref.dtype)


def taper_table(slabs_per_segment, width):
    position = jnp.arange(NFFT, dtype=jnp.int32).astype(jnp.float32)
    taper = 0.5 - 0.5 * jnp.cos(position * (2.0 * math.pi / NFFT))
    return taper.reshape(slabs_per_segment, width)


def _white_specs(slabs, block, width, per_segment):
    return [
        pl.BlockSpec((slabs, block, width), lambda i: (0, i, 0)),
        pl.BlockSpec((NFFT, 2 * BINS), lambda i: (0, 0), pipeline_mode=pl.Buffered(1)),
        pl.BlockSpec((per_segment, width), lambda i: (0, 0)),
    ]


def white_rows(parts, table, taper, block=128):
    slabs, rows, width = parts.shape
    specs = _white_specs(slabs, block, width, slabs // SEG)
    return pl.pallas_call(
        _white_kernel,
        out_shape=jax.ShapeDtypeStruct((2 * SEG, rows, BINS), jnp.bfloat16),
        grid=(rows // block,),
        in_specs=specs,
        out_specs=pl.BlockSpec((2 * SEG, block, BINS), lambda i: (0, i, 0)),
        compiler_params=pltpu.CompilerParams(vmem_limit_bytes=48 * 1024 * 1024),
        cost_estimate=pl.CostEstimate(
            flops=2 * SEG * rows * NFFT * 2 * BINS, transcendentals=SEG * rows * BINS,
            bytes_accessed=NFFT * 2 * BINS * 2 + 4 * slabs * rows * width,
        ),
    )(parts, table, taper)


def cross_rows(arrived, slots, first_white, table, taper, block=128):
    buckets, slabs, capacity, width = arrived.shape
    rows = slots.shape[0]
    return pl.pallas_call(
        _cross_kernel,
        out_shape=jax.ShapeDtypeStruct((rows, 2 * BINS), jnp.bfloat16),
        grid=(rows // block,),
        in_specs=[
            pl.BlockSpec((block, 1), lambda i: (i, 0)),
            pl.BlockSpec(arrived.shape, lambda i: (0, 0, 0, 0), pipeline_mode=pl.Buffered(1)),
            pl.BlockSpec((2 * SEG, block, BINS), lambda i: (0, i, 0)),
            pl.BlockSpec((NFFT, 2 * BINS), lambda i: (0, 0), pipeline_mode=pl.Buffered(1)),
            pl.BlockSpec((slabs // SEG, width), lambda i: (0, 0)),
        ],
        out_specs=pl.BlockSpec((block, 2 * BINS), lambda i: (i, 0)),
        compiler_params=pltpu.CompilerParams(vmem_limit_bytes=48 * 1024 * 1024),
        cost_estimate=pl.CostEstimate(
            flops=2 * SEG * rows * NFFT * 2 * BINS, transcendentals=SEG * rows * BINS,
            bytes_accessed=NFFT * 2 * BINS * 2 + 2 * arrived.size,
        ),
    )(slots.reshape(rows, 1), arrived, first_white, table, taper)


def _exchange_kernel(axis, x_ref, out_ref, landed, send_sems, recv_sems):
    count = x_ref.shape[0]
    me = lax.axis_index(axis)

    def peer_id(peer):
        return {axis: peer}

    barrier = pltpu.get_barrier_semaphore()
    for step in range(1, count):
        pl.semaphore_signal(
            barrier, inc=1, device_id=peer_id(lax.rem(me + step, count)), device_id_type=pl.DeviceIdType.MESH
        )
    pl.semaphore_wait(barrier, count - 1)
    copies = []
    for step in range(1, count):
        peer = lax.rem(me + step, count)
        copy = pltpu.make_async_remote_copy(
            src_ref=x_ref.at[peer],
            dst_ref=landed.at[me],
            send_sem=send_sems.at[step],
            recv_sem=recv_sems.at[step],
            device_id=peer_id(peer),
            device_id_type=pl.DeviceIdType.MESH,
        )
        copy.start()
        copies.append(copy)
    landed[me] = x_ref[me]
    for copy in copies:
        copy.wait_send()
        copy.wait_recv()
    out_ref[...] = landed[...]


def exchange(parts, axis, collective):
    count = parts.shape[0]
    return pl.pallas_call(
        functools.partial(_exchange_kernel, axis),
        out_shape=jax.ShapeDtypeStruct(parts.shape, parts.dtype),
        scratch_shapes=[
            pltpu.VMEM(parts.shape, parts.dtype),
            pltpu.SemaphoreType.DMA((count,)),
            pltpu.SemaphoreType.DMA((count,)),
        ],
        compiler_params=pltpu.CompilerParams(collective_id=collective, has_side_effects=True),
        cost_estimate=pl.CostEstimate(flops=0, transcendentals=0, bytes_accessed=4 * parts.size),
    )(parts)


def to_rows(parts):
    slabs, rows, width = parts.shape
    return jnp.transpose(parts, (1, 0, 2)).reshape(rows, slabs * width)


def local(records, first_station, second_region, second_station):
    regions = lax.axis_size("region")
    slabs = lax.axis_size("slab")
    pair_count = first_station.shape[0]
    width = records.shape[1]
    capacity = max(2, pair_count // regions + pair_count // 16)

    target = second_region[:, 0]
    onehot = (target[:, None] == jnp.arange(regions, dtype=jnp.int32)[None, :]).astype(jnp.int32)
    ranking = jnp.sum((jnp.cumsum(onehot, axis=0) - onehot) * onehot, axis=1)
    slot_index = target * capacity + ranking
    requests = (
        jnp.zeros((regions * capacity,), jnp.int32)
        .at[slot_index]
        .set(second_station)
    )
    own = jnp.pad(requests.reshape(-1, 128), ((0, (-(regions * capacity // 128)) % 8), (0, 0)))
    plane = exchange(jnp.broadcast_to(own[None], (slabs,) + own.shape), "slab", 2)
    plane_requests = plane[:, : regions * capacity // 128].reshape(slabs, regions, capacity)
    outgoing = jnp.transpose(plane_requests, (1, 0, 2)).reshape(regions, -1, 128)
    outgoing = jnp.pad(outgoing, ((0, 0), (0, (-outgoing.shape[1]) % 8), (0, 0)))
    asked = exchange(outgoing, "region", 1)[:, : slabs * capacity // 128].reshape(-1)

    firsts = lax.all_gather(first_station, "slab", axis=0, tiled=False)
    first_parts = pick_rows(records, firsts.reshape(-1)).reshape(slabs, pair_count, width)
    first_arrived = exchange(first_parts, "slab", 0)
    table = dft_table()
    taper = taper_table(slabs // SEG, width)
    first_white = white_rows(first_arrived, table, taper)

    served = pick_rows(records, asked)
    served = served.reshape(regions * slabs, capacity, width)
    arrived = lax.all_to_all(served, ("region", "slab"), split_axis=0, concat_axis=0, tiled=True)
    arrived, first_white = lax.optimization_barrier((arrived, first_white))
    return cross_rows(arrived.reshape(regions, slabs, capacity, width), slot_index, first_white, table, taper)

def solution(mesh):
    placed = (
        P("region", "slab"),
        P(("region", "slab")),
        P(("region", "slab"), None),
        P(("region", "slab")),
    )
    return jax.shard_map(
        local, mesh=mesh, in_specs=placed, out_specs=P(("region", "slab"), None), check_vma=False
    )
```

```python
import functools
import math

import jax
import jax.numpy as jnp
from jax import lax
from jax.experimental import pallas as pl
from jax.experimental.pallas import tpu as pltpu
from jax.sharding import PartitionSpec as P

NFFT = 2048
BINS = 1024
SEG = 2
HALF = 4


def dft_table():
    low = 64
    high = NFFT // low
    frequency = jnp.arange(BINS, dtype=jnp.int32)[None, :]
    coarse = jnp.arange(high, dtype=jnp.int32)[:, None]
    fine = jnp.arange(low, dtype=jnp.int32)[:, None]
    angle_a = ((coarse * frequency) % high).astype(jnp.float32) * (2.0 * math.pi / high)
    angle_b = ((fine * frequency) % NFFT).astype(jnp.float32) * (2.0 * math.pi / NFFT)
    ca, sa = jnp.cos(angle_a)[:, None, :], jnp.sin(angle_a)[:, None, :]
    cb, sb = jnp.cos(angle_b)[None, :, :], jnp.sin(angle_b)[None, :, :]
    cos_part = (ca * cb - sa * sb).reshape(NFFT, BINS)
    sin_part = (sa * cb + ca * sb).reshape(NFFT, BINS)
    return jnp.concatenate([cos_part, -sin_part], axis=1).astype(jnp.bfloat16)


def whitened(traces):
    count = traces.shape[0]
    signal = traces.astype(jnp.float32).reshape(count * SEG, NFFT)
    signal = signal - jnp.mean(signal, axis=1, keepdims=True)
    position = jnp.arange(NFFT, dtype=jnp.int32).astype(jnp.float32)
    taper = 0.5 - 0.5 * jnp.cos(position * (2.0 * math.pi / NFFT))
    tapered = (signal * taper[None, :]).astype(jnp.bfloat16)
    spectrum = jnp.dot(tapered, dft_table(), preferred_element_type=jnp.float32)
    real_part = spectrum[:, :BINS]
    imag_part = spectrum[:, BINS:]
    amplitude = jnp.sqrt(real_part * real_part + imag_part * imag_part + 1e-06)
    padded = jnp.pad(amplitude, ((0, 0), (HALF, HALF)))
    smooth = jnp.zeros_like(amplitude)
    for offset in range(2 * HALF + 1):
        smooth = smooth + padded[:, offset : offset + BINS]
    smooth = smooth / (2 * HALF + 1)
    level = jnp.mean(amplitude, axis=1, keepdims=True)
    divisor = smooth + level + 1e-06
    white = spectrum / jnp.concatenate([divisor, divisor], axis=1)
    return white.astype(jnp.bfloat16).reshape(count, SEG * NFFT)


def cross(first_rows, second_rows):
    left = first_rows.astype(jnp.float32).reshape(first_rows.shape[:-1] + (SEG, 2, BINS))
    right = second_rows.astype(jnp.float32).reshape(second_rows.shape[:-1] + (SEG, 2, BINS))
    real_sum = jnp.mean(
        left[..., 0, :] * right[..., 0, :] + left[..., 1, :] * right[..., 1, :], axis=-2
    )
    imag_sum = jnp.mean(
        left[..., 0, :] * right[..., 1, :] - left[..., 1, :] * right[..., 0, :], axis=-2
    )
    return jnp.concatenate([real_sum, imag_sum], axis=-1).astype(jnp.bfloat16)


def _pick_kernel(ids_ref, table_ref, out_ref):
    ids = ids_ref[...]
    rows = table_ref.shape[0]
    onehot = (lax.broadcasted_iota(jnp.int32, (ids.shape[0], rows), 1) == ids).astype(table_ref.dtype)
    out_ref[...] = jnp.dot(onehot, table_ref[...], preferred_element_type=jnp.float32).astype(out_ref.dtype)


def pick_rows(table, ids, block=1024):
    rows, width = table.shape
    count = ids.shape[0]
    block = min(block, count)
    return pl.pallas_call(
        _pick_kernel,
        out_shape=jax.ShapeDtypeStruct((count, width), table.dtype),
        grid=(count // block,),
        in_specs=[
            pl.BlockSpec((block, 1), lambda i: (i, 0)),
            pl.BlockSpec((rows, width), lambda i: (0, 0)),
        ],
        out_specs=pl.BlockSpec((block, width), lambda i: (i, 0)),
        cost_estimate=pl.CostEstimate(
            flops=2 * count * rows * width, transcendentals=0, bytes_accessed=2 * (rows + count) * width
        ),
    )(ids.reshape(count, 1), table)


def _compact_kernel(ids_ref, table_ref, out_ref):
    buckets, slabs, capacity, width = table_ref.shape
    for s in range(slabs):
        ids = ids_ref[s]
        table = table_ref[:, s].reshape(buckets * capacity, width)
        onehot = (lax.broadcasted_iota(jnp.int32, (ids.shape[0], buckets * capacity), 1) == ids).astype(table.dtype)
        out_ref[s] = jnp.dot(onehot, table, preferred_element_type=jnp.float32).astype(out_ref.dtype)


def compact_rows(arrived, slots):
    buckets, slabs, capacity, width = arrived.shape
    pairs = slots.shape[1]
    return pl.pallas_call(
        _compact_kernel,
        out_shape=jax.ShapeDtypeStruct((slabs, pairs, width), arrived.dtype),
        cost_estimate=pl.CostEstimate(
            flops=2 * slabs * pairs * buckets * capacity * width,
            transcendentals=0,
            bytes_accessed=2 * (buckets * capacity + pairs) * slabs * width,
        ),
    )(slots.reshape(slabs, pairs, 1), arrived)


def _white_block(slices, table, taper):
    per_segment = len(slices) // SEG
    tapered = []
    for segment in range(SEG):
        part = [piece.astype(jnp.float32) for piece in slices[segment * per_segment : (segment + 1) * per_segment]]
        total = jnp.sum(part[0], axis=1, keepdims=True)
        for piece in part[1:]:
            total = total + jnp.sum(piece, axis=1, keepdims=True)
        mean = total / NFFT
        pieces = [((part[i] - mean) * taper[i : i + 1, :]).astype(jnp.bfloat16) for i in range(per_segment)]
        tapered.append(jnp.concatenate(pieces, axis=1))
    spectrum = jnp.dot(jnp.concatenate(tapered, axis=0), table, preferred_element_type=jnp.float32)
    real_part = spectrum[:, :BINS]
    imag_part = spectrum[:, BINS:]
    amplitude = jnp.sqrt(real_part * real_part + imag_part * imag_part + 1e-06)
    lane = lax.broadcasted_iota(jnp.int32, amplitude.shape, 1)
    smooth = jnp.zeros_like(amplitude)
    for offset in range(-HALF, HALF + 1):
        moved = amplitude if offset == 0 else pltpu.roll(amplitude, (-offset) % BINS, 1)
        inside = (lane + offset >= 0) & (lane + offset < BINS)
        smooth = smooth + jnp.where(inside, moved, 0.0)
    smooth = smooth / (2 * HALF + 1)
    level = jnp.sum(amplitude, axis=1, keepdims=True) / BINS
    divisor = smooth + level + 1e-06
    white_real = (real_part / divisor).astype(jnp.bfloat16)
    white_imag = (imag_part / divisor).astype(jnp.bfloat16)
    return white_real, white_imag


def _white_kernel(x_ref, table_ref, taper_ref, out_ref):
    rows = x_ref.shape[1]
    slices = [x_ref[i] for i in range(x_ref.shape[0])]
    white_real, white_imag = _white_block(slices, table_ref[...], taper_ref[...])
    for segment in range(SEG):
        out_ref[2 * segment] = white_real[segment * rows : (segment + 1) * rows]
        out_ref[2 * segment + 1] = white_imag[segment * rows : (segment + 1) * rows]


def _cross_kernel(ids_ref, arrived_ref, first_ref, table_ref, taper_ref, out_ref):
    buckets, slabs, capacity, width = arrived_ref.shape
    ids = ids_ref[...]
    rows = ids.shape[0]
    onehot = (lax.broadcasted_iota(jnp.int32, (rows, buckets * capacity), 1) == ids).astype(arrived_ref.dtype)
    slices = [
        jnp.dot(onehot, arrived_ref[:, s].reshape(buckets * capacity, width), preferred_element_type=jnp.float32).astype(
            arrived_ref.dtype
        )
        for s in range(slabs)
    ]
    white_real, white_imag = _white_block(slices, table_ref[...], taper_ref[...])
    real_sum = None
    imag_sum = None
    for segment in range(SEG):
        left_real = first_ref[2 * segment].astype(jnp.float32)
        left_imag = first_ref[2 * segment + 1].astype(jnp.float32)
        right_real = white_real[segment * rows : (segment + 1) * rows].astype(jnp.float32)
        right_imag = white_imag[segment * rows : (segment + 1) * rows].astype(jnp.float32)
        real_term = left_real * right_real + left_imag * right_imag
        imag_term = left_real * right_imag - left_imag * right_real
        real_sum = real_term if real_sum is None else real_sum + real_term
        imag_sum = imag_term if imag_sum is None else imag_sum + imag_term
    out_ref[:, :BINS] = (real_sum / SEG).astype(out_ref.dtype)
    out_ref[:, BINS:] = (imag_sum / SEG).astype(out_ref.dtype)


def taper_table(slabs_per_segment, width):
    position = jnp.arange(NFFT, dtype=jnp.int32).astype(jnp.float32)
    taper = 0.5 - 0.5 * jnp.cos(position * (2.0 * math.pi / NFFT))
    return taper.reshape(slabs_per_segment, width)


def _white_specs(slabs, block, width, per_segment):
    return [
        pl.BlockSpec((slabs, block, width), lambda i: (0, i, 0)),
        pl.BlockSpec((NFFT, 2 * BINS), lambda i: (0, 0), pipeline_mode=pl.Buffered(1)),
        pl.BlockSpec((per_segment, width), lambda i: (0, 0)),
    ]


def white_rows(parts, table, taper, block=128):
    slabs, rows, width = parts.shape
    specs = _white_specs(slabs, block, width, slabs // SEG)
    return pl.pallas_call(
        _white_kernel,
        out_shape=jax.ShapeDtypeStruct((2 * SEG, rows, BINS), jnp.bfloat16),
        grid=(rows // block,),
        in_specs=specs,
        out_specs=pl.BlockSpec((2 * SEG, block, BINS), lambda i: (0, i, 0)),
        compiler_params=pltpu.CompilerParams(vmem_limit_bytes=48 * 1024 * 1024),
        cost_estimate=pl.CostEstimate(
            flops=2 * SEG * rows * NFFT * 2 * BINS, transcendentals=SEG * rows * BINS,
            bytes_accessed=NFFT * 2 * BINS * 2 + 4 * slabs * rows * width,
        ),
    )(parts, table, taper)


def cross_rows(arrived, slots, first_white, table, taper, block=128):
    buckets, slabs, capacity, width = arrived.shape
    rows = slots.shape[0]
    return pl.pallas_call(
        _cross_kernel,
        out_shape=jax.ShapeDtypeStruct((rows, 2 * BINS), jnp.bfloat16),
        grid=(rows // block,),
        in_specs=[
            pl.BlockSpec((block, 1), lambda i: (i, 0)),
            pl.BlockSpec(arrived.shape, lambda i: (0, 0, 0, 0), pipeline_mode=pl.Buffered(1)),
            pl.BlockSpec((2 * SEG, block, BINS), lambda i: (0, i, 0)),
            pl.BlockSpec((NFFT, 2 * BINS), lambda i: (0, 0), pipeline_mode=pl.Buffered(1)),
            pl.BlockSpec((slabs // SEG, width), lambda i: (0, 0)),
        ],
        out_specs=pl.BlockSpec((block, 2 * BINS), lambda i: (i, 0)),
        compiler_params=pltpu.CompilerParams(vmem_limit_bytes=48 * 1024 * 1024),
        cost_estimate=pl.CostEstimate(
            flops=2 * SEG * rows * NFFT * 2 * BINS, transcendentals=SEG * rows * BINS,
            bytes_accessed=NFFT * 2 * BINS * 2 + 2 * arrived.size,
        ),
    )(slots.reshape(rows, 1), arrived, first_white, table, taper)


def _exchange_kernel(axis, x_ref, out_ref, landed, send_sems, recv_sems):
    count = x_ref.shape[0]
    me = lax.axis_index(axis)

    def peer_id(peer):
        return {axis: peer}

    barrier = pltpu.get_barrier_semaphore()
    for step in range(1, count):
        pl.semaphore_signal(
            barrier, inc=1, device_id=peer_id(lax.rem(me + step, count)), device_id_type=pl.DeviceIdType.MESH
        )
    pl.semaphore_wait(barrier, count - 1)
    copies = []
    for step in range(1, count):
        peer = lax.rem(me + step, count)
        copy = pltpu.make_async_remote_copy(
            src_ref=x_ref.at[peer],
            dst_ref=landed.at[me],
            send_sem=send_sems.at[step],
            recv_sem=recv_sems.at[step],
            device_id=peer_id(peer),
            device_id_type=pl.DeviceIdType.MESH,
        )
        copy.start()
        copies.append(copy)
    landed[me] = x_ref[me]
    for copy in copies:
        copy.wait_send()
        copy.wait_recv()
    out_ref[...] = landed[...]


def exchange(parts, axis, collective):
    count = parts.shape[0]
    return pl.pallas_call(
        functools.partial(_exchange_kernel, axis),
        out_shape=jax.ShapeDtypeStruct(parts.shape, parts.dtype),
        scratch_shapes=[
            pltpu.VMEM(parts.shape, parts.dtype),
            pltpu.SemaphoreType.DMA((count,)),
            pltpu.SemaphoreType.DMA((count,)),
        ],
        compiler_params=pltpu.CompilerParams(collective_id=collective, has_side_effects=True),
        cost_estimate=pl.CostEstimate(flops=0, transcendentals=0, bytes_accessed=4 * parts.size),
    )(parts)


def to_rows(parts):
    slabs, rows, width = parts.shape
    return jnp.transpose(parts, (1, 0, 2)).reshape(rows, slabs * width)


def local(records, first_station, second_region, second_station):
    regions = lax.axis_size("region")
    slabs = lax.axis_size("slab")
    pair_count = first_station.shape[0]
    width = records.shape[1]
    capacity = max(2, pair_count // regions + pair_count // 16)

    target = second_region[:, 0]
    onehot = (target[:, None] == jnp.arange(regions, dtype=jnp.int32)[None, :]).astype(jnp.int32)
    ranking = jnp.sum((jnp.cumsum(onehot, axis=0) - onehot) * onehot, axis=1)
    slot_index = target * capacity + ranking
    requests = (
        jnp.zeros((regions * capacity,), jnp.int32)
        .at[slot_index]
        .set(second_station)
    )
    own = jnp.pad(requests.reshape(-1, 128), ((0, (-(regions * capacity // 128)) % 8), (0, 0)))
    plane = exchange(jnp.broadcast_to(own[None], (slabs,) + own.shape), "slab", 2)
    plane_requests = plane[:, : regions * capacity // 128].reshape(slabs, regions, capacity)
    outgoing = jnp.transpose(plane_requests, (1, 0, 2)).reshape(regions, -1, 128)
    outgoing = jnp.pad(outgoing, ((0, 0), (0, (-outgoing.shape[1]) % 8), (0, 0)))
    asked = exchange(outgoing, "region", 1)[:, : slabs * capacity // 128].reshape(-1)

    firsts = lax.all_gather(first_station, "slab", axis=0, tiled=False)
    first_parts = pick_rows(records, firsts.reshape(-1)).reshape(slabs, pair_count, width)
    first_arrived = exchange(first_parts, "slab", 0)
    table = dft_table()
    taper = taper_table(slabs // SEG, width)
    first_white = white_rows(first_arrived, table, taper)

    served = pick_rows(records, asked)
    served = served.reshape(regions * slabs, capacity, width)
    arrived = lax.all_to_all(served, ("region", "slab"), split_axis=0, concat_axis=0, tiled=True)
    arrived, first_white = lax.optimization_barrier((arrived, first_white))
    return cross_rows(arrived.reshape(regions, slabs, capacity, width), slot_index, first_white, table, taper)

def solution(mesh):
    placed = (
        P("region", "slab"),
        P(("region", "slab")),
        P(("region", "slab"), None),
        P(("region", "slab")),
    )
    return jax.shard_map(
        local, mesh=mesh, in_specs=placed, out_specs=P(("region", "slab"), None), check_vma=False
    )
```

```python
import functools
import math

import jax
import jax.numpy as jnp
from jax import lax
from jax.experimental import pallas as pl
from jax.experimental.pallas import tpu as pltpu
from jax.sharding import PartitionSpec as P

NFFT = 2048
BINS = 1024
SEG = 2
HALF = 4


def dft_table():
    low = 64
    high = NFFT // low
    frequency = jnp.arange(BINS, dtype=jnp.int32)[None, :]
    coarse = jnp.arange(high, dtype=jnp.int32)[:, None]
    fine = jnp.arange(low, dtype=jnp.int32)[:, None]
    angle_a = ((coarse * frequency) % high).astype(jnp.float32) * (2.0 * math.pi / high)
    angle_b = ((fine * frequency) % NFFT).astype(jnp.float32) * (2.0 * math.pi / NFFT)
    ca, sa = jnp.cos(angle_a)[:, None, :], jnp.sin(angle_a)[:, None, :]
    cb, sb = jnp.cos(angle_b)[None, :, :], jnp.sin(angle_b)[None, :, :]
    cos_part = (ca * cb - sa * sb).reshape(NFFT, BINS)
    sin_part = (sa * cb + ca * sb).reshape(NFFT, BINS)
    return jnp.concatenate([cos_part, -sin_part], axis=1).astype(jnp.bfloat16)


def whitened(traces):
    count = traces.shape[0]
    signal = traces.astype(jnp.float32).reshape(count * SEG, NFFT)
    signal = signal - jnp.mean(signal, axis=1, keepdims=True)
    position = jnp.arange(NFFT, dtype=jnp.int32).astype(jnp.float32)
    taper = 0.5 - 0.5 * jnp.cos(position * (2.0 * math.pi / NFFT))
    tapered = (signal * taper[None, :]).astype(jnp.bfloat16)
    spectrum = jnp.dot(tapered, dft_table(), preferred_element_type=jnp.float32)
    real_part = spectrum[:, :BINS]
    imag_part = spectrum[:, BINS:]
    amplitude = jnp.sqrt(real_part * real_part + imag_part * imag_part + 1e-06)
    padded = jnp.pad(amplitude, ((0, 0), (HALF, HALF)))
    smooth = jnp.zeros_like(amplitude)
    for offset in range(2 * HALF + 1):
        smooth = smooth + padded[:, offset : offset + BINS]
    smooth = smooth / (2 * HALF + 1)
    level = jnp.mean(amplitude, axis=1, keepdims=True)
    divisor = smooth + level + 1e-06
    white = spectrum / jnp.concatenate([divisor, divisor], axis=1)
    return white.astype(jnp.bfloat16).reshape(count, SEG * NFFT)


def cross(first_rows, second_rows):
    left = first_rows.astype(jnp.float32).reshape(first_rows.shape[:-1] + (SEG, 2, BINS))
    right = second_rows.astype(jnp.float32).reshape(second_rows.shape[:-1] + (SEG, 2, BINS))
    real_sum = jnp.mean(
        left[..., 0, :] * right[..., 0, :] + left[..., 1, :] * right[..., 1, :], axis=-2
    )
    imag_sum = jnp.mean(
        left[..., 0, :] * right[..., 1, :] - left[..., 1, :] * right[..., 0, :], axis=-2
    )
    return jnp.concatenate([real_sum, imag_sum], axis=-1).astype(jnp.bfloat16)


def _pick_kernel(ids_ref, table_ref, out_ref):
    ids = ids_ref[...]
    rows = table_ref.shape[0]
    onehot = (lax.broadcasted_iota(jnp.int32, (ids.shape[0], rows), 1) == ids).astype(table_ref.dtype)
    out_ref[...] = jnp.dot(onehot, table_ref[...], preferred_element_type=jnp.float32).astype(out_ref.dtype)


def pick_rows(table, ids, block=2048):
    rows, width = table.shape
    count = ids.shape[0]
    block = min(block, count)
    return pl.pallas_call(
        _pick_kernel,
        out_shape=jax.ShapeDtypeStruct((count, width), table.dtype),
        grid=(count // block,),
        in_specs=[
            pl.BlockSpec((block, 1), lambda i: (i, 0)),
            pl.BlockSpec((rows, width), lambda i: (0, 0)),
        ],
        out_specs=pl.BlockSpec((block, width), lambda i: (i, 0)),
        cost_estimate=pl.CostEstimate(
            flops=2 * count * rows * width, transcendentals=0, bytes_accessed=2 * (rows + count) * width
        ),
    )(ids.reshape(count, 1), table)


def _compact_kernel(ids_ref, table_ref, out_ref):
    buckets, slabs, capacity, width = table_ref.shape
    for s in range(slabs):
        ids = ids_ref[s]
        table = table_ref[:, s].reshape(buckets * capacity, width)
        onehot = (lax.broadcasted_iota(jnp.int32, (ids.shape[0], buckets * capacity), 1) == ids).astype(table.dtype)
        out_ref[s] = jnp.dot(onehot, table, preferred_element_type=jnp.float32).astype(out_ref.dtype)


def compact_rows(arrived, slots):
    buckets, slabs, capacity, width = arrived.shape
    pairs = slots.shape[1]
    return pl.pallas_call(
        _compact_kernel,
        out_shape=jax.ShapeDtypeStruct((slabs, pairs, width), arrived.dtype),
        cost_estimate=pl.CostEstimate(
            flops=2 * slabs * pairs * buckets * capacity * width,
            transcendentals=0,
            bytes_accessed=2 * (buckets * capacity + pairs) * slabs * width,
        ),
    )(slots.reshape(slabs, pairs, 1), arrived)


def _white_block(slices, table, taper):
    per_segment = len(slices) // SEG
    tapered = []
    for segment in range(SEG):
        part = [piece.astype(jnp.float32) for piece in slices[segment * per_segment : (segment + 1) * per_segment]]
        total = jnp.sum(part[0], axis=1, keepdims=True)
        for piece in part[1:]:
            total = total + jnp.sum(piece, axis=1, keepdims=True)
        mean = total / NFFT
        pieces = [((part[i] - mean) * taper[i : i + 1, :]).astype(jnp.bfloat16) for i in range(per_segment)]
        tapered.append(jnp.concatenate(pieces, axis=1))
    spectrum = jnp.dot(jnp.concatenate(tapered, axis=0), table, preferred_element_type=jnp.float32)
    real_part = spectrum[:, :BINS]
    imag_part = spectrum[:, BINS:]
    amplitude = jnp.sqrt(real_part * real_part + imag_part * imag_part + 1e-06)
    lane = lax.broadcasted_iota(jnp.int32, amplitude.shape, 1)
    smooth = jnp.zeros_like(amplitude)
    for offset in range(-HALF, HALF + 1):
        moved = amplitude if offset == 0 else pltpu.roll(amplitude, (-offset) % BINS, 1)
        inside = (lane + offset >= 0) & (lane + offset < BINS)
        smooth = smooth + jnp.where(inside, moved, 0.0)
    smooth = smooth / (2 * HALF + 1)
    level = jnp.sum(amplitude, axis=1, keepdims=True) / BINS
    divisor = smooth + level + 1e-06
    white_real = (real_part / divisor).astype(jnp.bfloat16)
    white_imag = (imag_part / divisor).astype(jnp.bfloat16)
    return white_real, white_imag


def _white_kernel(x_ref, table_ref, taper_ref, out_ref):
    rows = x_ref.shape[1]
    slices = [x_ref[i] for i in range(x_ref.shape[0])]
    white_real, white_imag = _white_block(slices, table_ref[...], taper_ref[...])
    for segment in range(SEG):
        out_ref[2 * segment] = white_real[segment * rows : (segment + 1) * rows]
        out_ref[2 * segment + 1] = white_imag[segment * rows : (segment + 1) * rows]


def _cross_kernel(ids_ref, arrived_ref, first_ref, table_ref, taper_ref, out_ref):
    buckets, slabs, capacity, width = arrived_ref.shape
    ids = ids_ref[...]
    rows = ids.shape[0]
    onehot = (lax.broadcasted_iota(jnp.int32, (rows, buckets * capacity), 1) == ids).astype(arrived_ref.dtype)
    slices = [
        jnp.dot(onehot, arrived_ref[:, s].reshape(buckets * capacity, width), preferred_element_type=jnp.float32).astype(
            arrived_ref.dtype
        )
        for s in range(slabs)
    ]
    white_real, white_imag = _white_block(slices, table_ref[...], taper_ref[...])
    real_sum = None
    imag_sum = None
    for segment in range(SEG):
        left_real = first_ref[2 * segment].astype(jnp.float32)
        left_imag = first_ref[2 * segment + 1].astype(jnp.float32)
        right_real = white_real[segment * rows : (segment + 1) * rows].astype(jnp.float32)
        right_imag = white_imag[segment * rows : (segment + 1) * rows].astype(jnp.float32)
        real_term = left_real * right_real + left_imag * right_imag
        imag_term = left_real * right_imag - left_imag * right_real
        real_sum = real_term if real_sum is None else real_sum + real_term
        imag_sum = imag_term if imag_sum is None else imag_sum + imag_term
    out_ref[:, :BINS] = (real_sum / SEG).astype(out_ref.dtype)
    out_ref[:, BINS:] = (imag_sum / SEG).astype(out_ref.dtype)


def taper_table(slabs_per_segment, width):
    position = jnp.arange(NFFT, dtype=jnp.int32).astype(jnp.float32)
    taper = 0.5 - 0.5 * jnp.cos(position * (2.0 * math.pi / NFFT))
    return taper.reshape(slabs_per_segment, width)


def _white_specs(slabs, block, width, per_segment):
    return [
        pl.BlockSpec((slabs, block, width), lambda i: (0, i, 0)),
        pl.BlockSpec((NFFT, 2 * BINS), lambda i: (0, 0), pipeline_mode=pl.Buffered(1)),
        pl.BlockSpec((per_segment, width), lambda i: (0, 0)),
    ]


def white_rows(parts, table, taper, block=128):
    slabs, rows, width = parts.shape
    specs = _white_specs(slabs, block, width, slabs // SEG)
    return pl.pallas_call(
        _white_kernel,
        out_shape=jax.ShapeDtypeStruct((2 * SEG, rows, BINS), jnp.bfloat16),
        grid=(rows // block,),
        in_specs=specs,
        out_specs=pl.BlockSpec((2 * SEG, block, BINS), lambda i: (0, i, 0)),
        compiler_params=pltpu.CompilerParams(vmem_limit_bytes=48 * 1024 * 1024),
        cost_estimate=pl.CostEstimate(
            flops=2 * SEG * rows * NFFT * 2 * BINS, transcendentals=SEG * rows * BINS,
            bytes_accessed=NFFT * 2 * BINS * 2 + 4 * slabs * rows * width,
        ),
    )(parts, table, taper)


def cross_rows(arrived, slots, first_white, table, taper, block=128):
    buckets, slabs, capacity, width = arrived.shape
    rows = slots.shape[0]
    return pl.pallas_call(
        _cross_kernel,
        out_shape=jax.ShapeDtypeStruct((rows, 2 * BINS), jnp.bfloat16),
        grid=(rows // block,),
        in_specs=[
            pl.BlockSpec((block, 1), lambda i: (i, 0)),
            pl.BlockSpec(arrived.shape, lambda i: (0, 0, 0, 0), pipeline_mode=pl.Buffered(1)),
            pl.BlockSpec((2 * SEG, block, BINS), lambda i: (0, i, 0)),
            pl.BlockSpec((NFFT, 2 * BINS), lambda i: (0, 0), pipeline_mode=pl.Buffered(1)),
            pl.BlockSpec((slabs // SEG, width), lambda i: (0, 0)),
        ],
        out_specs=pl.BlockSpec((block, 2 * BINS), lambda i: (i, 0)),
        compiler_params=pltpu.CompilerParams(vmem_limit_bytes=48 * 1024 * 1024),
        cost_estimate=pl.CostEstimate(
            flops=2 * SEG * rows * NFFT * 2 * BINS, transcendentals=SEG * rows * BINS,
            bytes_accessed=NFFT * 2 * BINS * 2 + 2 * arrived.size,
        ),
    )(slots.reshape(rows, 1), arrived, first_white, table, taper)


def _exchange_kernel(axis, x_ref, out_ref, landed, send_sems, recv_sems):
    count = x_ref.shape[0]
    me = lax.axis_index(axis)

    def peer_id(peer):
        return {axis: peer}

    barrier = pltpu.get_barrier_semaphore()
    for step in range(1, count):
        pl.semaphore_signal(
            barrier, inc=1, device_id=peer_id(lax.rem(me + step, count)), device_id_type=pl.DeviceIdType.MESH
        )
    pl.semaphore_wait(barrier, count - 1)
    copies = []
    for step in range(1, count):
        peer = lax.rem(me + step, count)
        copy = pltpu.make_async_remote_copy(
            src_ref=x_ref.at[peer],
            dst_ref=landed.at[me],
            send_sem=send_sems.at[step],
            recv_sem=recv_sems.at[step],
            device_id=peer_id(peer),
            device_id_type=pl.DeviceIdType.MESH,
        )
        copy.start()
        copies.append(copy)
    landed[me] = x_ref[me]
    for copy in copies:
        copy.wait_send()
        copy.wait_recv()
    out_ref[...] = landed[...]


def exchange(parts, axis, collective):
    count = parts.shape[0]
    return pl.pallas_call(
        functools.partial(_exchange_kernel, axis),
        out_shape=jax.ShapeDtypeStruct(parts.shape, parts.dtype),
        scratch_shapes=[
            pltpu.VMEM(parts.shape, parts.dtype),
            pltpu.SemaphoreType.DMA((count,)),
            pltpu.SemaphoreType.DMA((count,)),
        ],
        compiler_params=pltpu.CompilerParams(collective_id=collective, has_side_effects=True),
        cost_estimate=pl.CostEstimate(flops=0, transcendentals=0, bytes_accessed=4 * parts.size),
    )(parts)


def to_rows(parts):
    slabs, rows, width = parts.shape
    return jnp.transpose(parts, (1, 0, 2)).reshape(rows, slabs * width)


def local(records, first_station, second_region, second_station):
    regions = lax.axis_size("region")
    slabs = lax.axis_size("slab")
    pair_count = first_station.shape[0]
    width = records.shape[1]
    capacity = max(2, pair_count // regions + pair_count // 16)

    target = second_region[:, 0]
    onehot = (target[:, None] == jnp.arange(regions, dtype=jnp.int32)[None, :]).astype(jnp.int32)
    ranking = jnp.sum((jnp.cumsum(onehot, axis=0) - onehot) * onehot, axis=1)
    slot_index = target * capacity + ranking
    requests = (
        jnp.zeros((regions * capacity,), jnp.int32)
        .at[slot_index]
        .set(second_station)
    )
    own = jnp.pad(requests.reshape(-1, 128), ((0, (-(regions * capacity // 128)) % 8), (0, 0)))
    plane = exchange(jnp.broadcast_to(own[None], (slabs,) + own.shape), "slab", 2)
    plane_requests = plane[:, : regions * capacity // 128].reshape(slabs, regions, capacity)
    outgoing = jnp.transpose(plane_requests, (1, 0, 2)).reshape(regions, -1, 128)
    outgoing = jnp.pad(outgoing, ((0, 0), (0, (-outgoing.shape[1]) % 8), (0, 0)))
    asked = exchange(outgoing, "region", 1)[:, : slabs * capacity // 128].reshape(-1)

    firsts = lax.all_gather(first_station, "slab", axis=0, tiled=False)
    first_parts = pick_rows(records, firsts.reshape(-1)).reshape(slabs, pair_count, width)
    first_arrived = exchange(first_parts, "slab", 0)
    table = dft_table()
    taper = taper_table(slabs // SEG, width)
    first_white = white_rows(first_arrived, table, taper)

    served = pick_rows(records, asked)
    served = served.reshape(regions * slabs, capacity, width)
    arrived = lax.all_to_all(served, ("region", "slab"), split_axis=0, concat_axis=0, tiled=True)
    arrived, first_white = lax.optimization_barrier((arrived, first_white))
    return cross_rows(arrived.reshape(regions, slabs, capacity, width), slot_index, first_white, table, taper)

def solution(mesh):
    placed = (
        P("region", "slab"),
        P(("region", "slab")),
        P(("region", "slab"), None),
        P(("region", "slab")),
    )
    return jax.shard_map(
        local, mesh=mesh, in_specs=placed, out_specs=P(("region", "slab"), None), check_vma=False
    )
```

```python
import functools
import math

import jax
import jax.numpy as jnp
from jax import lax
from jax.experimental import pallas as pl
from jax.experimental.pallas import tpu as pltpu
from jax.sharding import PartitionSpec as P

NFFT = 2048
BINS = 1024
SEG = 2
HALF = 4


def dft_table():
    low = 64
    high = NFFT // low
    frequency = jnp.arange(BINS, dtype=jnp.int32)[None, :]
    coarse = jnp.arange(high, dtype=jnp.int32)[:, None]
    fine = jnp.arange(low, dtype=jnp.int32)[:, None]
    angle_a = ((coarse * frequency) % high).astype(jnp.float32) * (2.0 * math.pi / high)
    angle_b = ((fine * frequency) % NFFT).astype(jnp.float32) * (2.0 * math.pi / NFFT)
    ca, sa = jnp.cos(angle_a)[:, None, :], jnp.sin(angle_a)[:, None, :]
    cb, sb = jnp.cos(angle_b)[None, :, :], jnp.sin(angle_b)[None, :, :]
    cos_part = (ca * cb - sa * sb).reshape(NFFT, BINS)
    sin_part = (sa * cb + ca * sb).reshape(NFFT, BINS)
    return jnp.concatenate([cos_part, -sin_part], axis=1).astype(jnp.bfloat16)


def whitened(traces):
    count = traces.shape[0]
    signal = traces.astype(jnp.float32).reshape(count * SEG, NFFT)
    signal = signal - jnp.mean(signal, axis=1, keepdims=True)
    position = jnp.arange(NFFT, dtype=jnp.int32).astype(jnp.float32)
    taper = 0.5 - 0.5 * jnp.cos(position * (2.0 * math.pi / NFFT))
    tapered = (signal * taper[None, :]).astype(jnp.bfloat16)
    spectrum = jnp.dot(tapered, dft_table(), preferred_element_type=jnp.float32)
    real_part = spectrum[:, :BINS]
    imag_part = spectrum[:, BINS:]
    amplitude = jnp.sqrt(real_part * real_part + imag_part * imag_part + 1e-06)
    padded = jnp.pad(amplitude, ((0, 0), (HALF, HALF)))
    smooth = jnp.zeros_like(amplitude)
    for offset in range(2 * HALF + 1):
        smooth = smooth + padded[:, offset : offset + BINS]
    smooth = smooth / (2 * HALF + 1)
    level = jnp.mean(amplitude, axis=1, keepdims=True)
    divisor = smooth + level + 1e-06
    white = spectrum / jnp.concatenate([divisor, divisor], axis=1)
    return white.astype(jnp.bfloat16).reshape(count, SEG * NFFT)


def cross(first_rows, second_rows):
    left = first_rows.astype(jnp.float32).reshape(first_rows.shape[:-1] + (SEG, 2, BINS))
    right = second_rows.astype(jnp.float32).reshape(second_rows.shape[:-1] + (SEG, 2, BINS))
    real_sum = jnp.mean(
        left[..., 0, :] * right[..., 0, :] + left[..., 1, :] * right[..., 1, :], axis=-2
    )
    imag_sum = jnp.mean(
        left[..., 0, :] * right[..., 1, :] - left[..., 1, :] * right[..., 0, :], axis=-2
    )
    return jnp.concatenate([real_sum, imag_sum], axis=-1).astype(jnp.bfloat16)


def _pick_kernel(ids_ref, table_ref, out_ref):
    ids = ids_ref[...]
    rows = table_ref.shape[0]
    onehot = (lax.broadcasted_iota(jnp.int32, (ids.shape[0], rows), 1) == ids).astype(table_ref.dtype)
    out_ref[...] = jnp.dot(onehot, table_ref[...], preferred_element_type=jnp.float32).astype(out_ref.dtype)


def pick_rows(table, ids, block=2048):
    rows, width = table.shape
    count = ids.shape[0]
    block = min(block, count)
    return pl.pallas_call(
        _pick_kernel,
        out_shape=jax.ShapeDtypeStruct((count, width), table.dtype),
        grid=(count // block,),
        in_specs=[
            pl.BlockSpec((block, 1), lambda i: (i, 0)),
            pl.BlockSpec((rows, width), lambda i: (0, 0)),
        ],
        out_specs=pl.BlockSpec((block, width), lambda i: (i, 0)),
        cost_estimate=pl.CostEstimate(
            flops=2 * count * rows * width, transcendentals=0, bytes_accessed=2 * (rows + count) * width
        ),
    )(ids.reshape(count, 1), table)


def _compact_kernel(ids_ref, table_ref, out_ref):
    buckets, slabs, capacity, width = table_ref.shape
    for s in range(slabs):
        ids = ids_ref[s]
        table = table_ref[:, s].reshape(buckets * capacity, width)
        onehot = (lax.broadcasted_iota(jnp.int32, (ids.shape[0], buckets * capacity), 1) == ids).astype(table.dtype)
        out_ref[s] = jnp.dot(onehot, table, preferred_element_type=jnp.float32).astype(out_ref.dtype)


def compact_rows(arrived, slots):
    buckets, slabs, capacity, width = arrived.shape
    pairs = slots.shape[1]
    return pl.pallas_call(
        _compact_kernel,
        out_shape=jax.ShapeDtypeStruct((slabs, pairs, width), arrived.dtype),
        cost_estimate=pl.CostEstimate(
            flops=2 * slabs * pairs * buckets * capacity * width,
            transcendentals=0,
            bytes_accessed=2 * (buckets * capacity + pairs) * slabs * width,
        ),
    )(slots.reshape(slabs, pairs, 1), arrived)


def _white_block(slices, table, taper):
    per_segment = len(slices) // SEG
    tapered = []
    for segment in range(SEG):
        part = [piece.astype(jnp.float32) for piece in slices[segment * per_segment : (segment + 1) * per_segment]]
        total = jnp.sum(part[0], axis=1, keepdims=True)
        for piece in part[1:]:
            total = total + jnp.sum(piece, axis=1, keepdims=True)
        mean = total / NFFT
        pieces = [((part[i] - mean) * taper[i : i + 1, :]).astype(jnp.bfloat16) for i in range(per_segment)]
        tapered.append(jnp.concatenate(pieces, axis=1))
    spectrum = jnp.dot(jnp.concatenate(tapered, axis=0), table, preferred_element_type=jnp.float32)
    real_part = spectrum[:, :BINS]
    imag_part = spectrum[:, BINS:]
    amplitude = jnp.sqrt(real_part * real_part + imag_part * imag_part + 1e-06)
    lane = lax.broadcasted_iota(jnp.int32, amplitude.shape, 1)
    smooth = jnp.zeros_like(amplitude)
    for offset in range(-HALF, HALF + 1):
        moved = amplitude if offset == 0 else pltpu.roll(amplitude, (-offset) % BINS, 1)
        inside = (lane + offset >= 0) & (lane + offset < BINS)
        smooth = smooth + jnp.where(inside, moved, 0.0)
    smooth = smooth / (2 * HALF + 1)
    level = jnp.sum(amplitude, axis=1, keepdims=True) / BINS
    divisor = smooth + level + 1e-06
    white_real = (real_part / divisor).astype(jnp.bfloat16)
    white_imag = (imag_part / divisor).astype(jnp.bfloat16)
    return white_real, white_imag


def _white_kernel(x_ref, table_ref, taper_ref, out_ref):
    rows = x_ref.shape[1]
    slices = [x_ref[i] for i in range(x_ref.shape[0])]
    white_real, white_imag = _white_block(slices, table_ref[...], taper_ref[...])
    for segment in range(SEG):
        out_ref[2 * segment] = white_real[segment * rows : (segment + 1) * rows]
        out_ref[2 * segment + 1] = white_imag[segment * rows : (segment + 1) * rows]


def _cross_kernel(ids_ref, arrived_hbm, first_ref, table_hbm, taper_ref, out_ref, arrived_ref, table_ref, sems):
    arrived_copy = pltpu.make_async_copy(arrived_hbm, arrived_ref, sems.at[0])
    table_copy = pltpu.make_async_copy(table_hbm, table_ref, sems.at[1])
    arrived_copy.start()
    table_copy.start()
    buckets, slabs, capacity, width = arrived_ref.shape
    ids = ids_ref[...]
    rows = ids.shape[0]
    onehot = (lax.broadcasted_iota(jnp.int32, (rows, buckets * capacity), 1) == ids).astype(arrived_ref.dtype)
    arrived_copy.wait()
    slices = [
        jnp.dot(onehot, arrived_ref[:, s].reshape(buckets * capacity, width), preferred_element_type=jnp.float32).astype(
            arrived_ref.dtype
        )
        for s in range(slabs)
    ]
    table_copy.wait()
    white_real, white_imag = _white_block(slices, table_ref[...], taper_ref[...])
    real_sum = None
    imag_sum = None
    for segment in range(SEG):
        left_real = first_ref[2 * segment].astype(jnp.float32)
        left_imag = first_ref[2 * segment + 1].astype(jnp.float32)
        right_real = white_real[segment * rows : (segment + 1) * rows].astype(jnp.float32)
        right_imag = white_imag[segment * rows : (segment + 1) * rows].astype(jnp.float32)
        real_term = left_real * right_real + left_imag * right_imag
        imag_term = left_real * right_imag - left_imag * right_real
        real_sum = real_term if real_sum is None else real_sum + real_term
        imag_sum = imag_term if imag_sum is None else imag_sum + imag_term
    out_ref[:, :BINS] = (real_sum / SEG).astype(out_ref.dtype)
    out_ref[:, BINS:] = (imag_sum / SEG).astype(out_ref.dtype)


def taper_table(slabs_per_segment, width):
    position = jnp.arange(NFFT, dtype=jnp.int32).astype(jnp.float32)
    taper = 0.5 - 0.5 * jnp.cos(position * (2.0 * math.pi / NFFT))
    return taper.reshape(slabs_per_segment, width)


def _white_specs(slabs, block, width, per_segment):
    return [
        pl.BlockSpec((slabs, block, width), lambda i: (0, i, 0)),
        pl.BlockSpec((NFFT, 2 * BINS), lambda i: (0, 0), pipeline_mode=pl.Buffered(1)),
        pl.BlockSpec((per_segment, width), lambda i: (0, 0)),
    ]


def white_rows(parts, table, taper, block=128):
    slabs, rows, width = parts.shape
    specs = _white_specs(slabs, block, width, slabs // SEG)
    return pl.pallas_call(
        _white_kernel,
        out_shape=jax.ShapeDtypeStruct((2 * SEG, rows, BINS), jnp.bfloat16),
        grid=(rows // block,),
        in_specs=specs,
        out_specs=pl.BlockSpec((2 * SEG, block, BINS), lambda i: (0, i, 0)),
        compiler_params=pltpu.CompilerParams(vmem_limit_bytes=48 * 1024 * 1024),
        cost_estimate=pl.CostEstimate(
            flops=2 * SEG * rows * NFFT * 2 * BINS, transcendentals=SEG * rows * BINS,
            bytes_accessed=NFFT * 2 * BINS * 2 + 4 * slabs * rows * width,
        ),
    )(parts, table, taper)


def cross_rows(arrived, slots, first_white, table, taper):
    buckets, slabs, capacity, width = arrived.shape
    rows = slots.shape[0]
    vmem = pltpu.MemorySpace.VMEM
    return pl.pallas_call(
        _cross_kernel,
        out_shape=jax.ShapeDtypeStruct((rows, 2 * BINS), jnp.bfloat16),
        in_specs=[
            pl.BlockSpec(memory_space=vmem),
            pl.BlockSpec(memory_space=pl.ANY),
            pl.BlockSpec(memory_space=vmem),
            pl.BlockSpec(memory_space=pl.ANY),
            pl.BlockSpec(memory_space=vmem),
        ],
        out_specs=pl.BlockSpec(memory_space=vmem),
        scratch_shapes=[
            pltpu.VMEM(arrived.shape, arrived.dtype),
            pltpu.VMEM(table.shape, table.dtype),
            pltpu.SemaphoreType.DMA((2,)),
        ],
        compiler_params=pltpu.CompilerParams(vmem_limit_bytes=48 * 1024 * 1024),
        cost_estimate=pl.CostEstimate(
            flops=2 * SEG * rows * NFFT * 2 * BINS, transcendentals=SEG * rows * BINS,
            bytes_accessed=NFFT * 2 * BINS * 2 + 2 * arrived.size,
        ),
    )(slots.reshape(rows, 1), arrived, first_white, table, taper)


def _exchange_kernel(axis, x_ref, out_ref, landed, send_sems, recv_sems):
    count = x_ref.shape[0]
    me = lax.axis_index(axis)

    def peer_id(peer):
        return {axis: peer}

    barrier = pltpu.get_barrier_semaphore()
    for step in range(1, count):
        pl.semaphore_signal(
            barrier, inc=1, device_id=peer_id(lax.rem(me + step, count)), device_id_type=pl.DeviceIdType.MESH
        )
    pl.semaphore_wait(barrier, count - 1)
    copies = []
    for step in range(1, count):
        peer = lax.rem(me + step, count)
        copy = pltpu.make_async_remote_copy(
            src_ref=x_ref.at[peer],
            dst_ref=landed.at[me],
            send_sem=send_sems.at[step],
            recv_sem=recv_sems.at[step],
            device_id=peer_id(peer),
            device_id_type=pl.DeviceIdType.MESH,
        )
        copy.start()
        copies.append(copy)
    landed[me] = x_ref[me]
    for copy in copies:
        copy.wait_send()
        copy.wait_recv()
    out_ref[...] = landed[...]


def exchange(parts, axis, collective):
    count = parts.shape[0]
    return pl.pallas_call(
        functools.partial(_exchange_kernel, axis),
        out_shape=jax.ShapeDtypeStruct(parts.shape, parts.dtype),
        scratch_shapes=[
            pltpu.VMEM(parts.shape, parts.dtype),
            pltpu.SemaphoreType.DMA((count,)),
            pltpu.SemaphoreType.DMA((count,)),
        ],
        compiler_params=pltpu.CompilerParams(collective_id=collective, has_side_effects=True),
        cost_estimate=pl.CostEstimate(flops=0, transcendentals=0, bytes_accessed=4 * parts.size),
    )(parts)


def to_rows(parts):
    slabs, rows, width = parts.shape
    return jnp.transpose(parts, (1, 0, 2)).reshape(rows, slabs * width)


def local(records, first_station, second_region, second_station):
    regions = lax.axis_size("region")
    slabs = lax.axis_size("slab")
    pair_count = first_station.shape[0]
    width = records.shape[1]
    capacity = max(2, pair_count // regions + pair_count // 16)

    target = second_region[:, 0]
    onehot = (target[:, None] == jnp.arange(regions, dtype=jnp.int32)[None, :]).astype(jnp.int32)
    ranking = jnp.sum((jnp.cumsum(onehot, axis=0) - onehot) * onehot, axis=1)
    slot_index = target * capacity + ranking
    requests = (
        jnp.zeros((regions * capacity,), jnp.int32)
        .at[slot_index]
        .set(second_station)
    )
    own = jnp.pad(requests.reshape(-1, 128), ((0, (-(regions * capacity // 128)) % 8), (0, 0)))
    plane = exchange(jnp.broadcast_to(own[None], (slabs,) + own.shape), "slab", 2)
    plane_requests = plane[:, : regions * capacity // 128].reshape(slabs, regions, capacity)
    outgoing = jnp.transpose(plane_requests, (1, 0, 2)).reshape(regions, -1, 128)
    outgoing = jnp.pad(outgoing, ((0, 0), (0, (-outgoing.shape[1]) % 8), (0, 0)))
    asked = exchange(outgoing, "region", 1)[:, : slabs * capacity // 128].reshape(-1)

    firsts = lax.all_gather(first_station, "slab", axis=0, tiled=False)
    first_parts = pick_rows(records, firsts.reshape(-1)).reshape(slabs, pair_count, width)
    first_arrived = exchange(first_parts, "slab", 0)
    table = dft_table()
    taper = taper_table(slabs // SEG, width)
    first_white = white_rows(first_arrived, table, taper)

    served = pick_rows(records, asked)
    served = served.reshape(regions * slabs, capacity, width)
    arrived = lax.all_to_all(served, ("region", "slab"), split_axis=0, concat_axis=0, tiled=True)
    arrived, first_white = lax.optimization_barrier((arrived, first_white))
    return cross_rows(arrived.reshape(regions, slabs, capacity, width), slot_index, first_white, table, taper)

def solution(mesh):
    placed = (
        P("region", "slab"),
        P(("region", "slab")),
        P(("region", "slab"), None),
        P(("region", "slab")),
    )
    return jax.shard_map(
        local, mesh=mesh, in_specs=placed, out_specs=P(("region", "slab"), None), check_vma=False
    )
```

```python
import functools
import math

import jax
import jax.numpy as jnp
from jax import lax
from jax.experimental import pallas as pl
from jax.experimental.pallas import tpu as pltpu
from jax.sharding import PartitionSpec as P

NFFT = 2048
BINS = 1024
SEG = 2
HALF = 4


def dft_table():
    low = 64
    high = NFFT // low
    frequency = jnp.arange(BINS, dtype=jnp.int32)[None, :]
    coarse = jnp.arange(high, dtype=jnp.int32)[:, None]
    fine = jnp.arange(low, dtype=jnp.int32)[:, None]
    angle_a = ((coarse * frequency) % high).astype(jnp.float32) * (2.0 * math.pi / high)
    angle_b = ((fine * frequency) % NFFT).astype(jnp.float32) * (2.0 * math.pi / NFFT)
    ca, sa = jnp.cos(angle_a)[:, None, :], jnp.sin(angle_a)[:, None, :]
    cb, sb = jnp.cos(angle_b)[None, :, :], jnp.sin(angle_b)[None, :, :]
    cos_part = (ca * cb - sa * sb).reshape(NFFT, BINS)
    sin_part = (sa * cb + ca * sb).reshape(NFFT, BINS)
    return jnp.concatenate([cos_part, -sin_part], axis=1).astype(jnp.bfloat16)


def whitened(traces):
    count = traces.shape[0]
    signal = traces.astype(jnp.float32).reshape(count * SEG, NFFT)
    signal = signal - jnp.mean(signal, axis=1, keepdims=True)
    position = jnp.arange(NFFT, dtype=jnp.int32).astype(jnp.float32)
    taper = 0.5 - 0.5 * jnp.cos(position * (2.0 * math.pi / NFFT))
    tapered = (signal * taper[None, :]).astype(jnp.bfloat16)
    spectrum = jnp.dot(tapered, dft_table(), preferred_element_type=jnp.float32)
    real_part = spectrum[:, :BINS]
    imag_part = spectrum[:, BINS:]
    amplitude = jnp.sqrt(real_part * real_part + imag_part * imag_part + 1e-06)
    padded = jnp.pad(amplitude, ((0, 0), (HALF, HALF)))
    smooth = jnp.zeros_like(amplitude)
    for offset in range(2 * HALF + 1):
        smooth = smooth + padded[:, offset : offset + BINS]
    smooth = smooth / (2 * HALF + 1)
    level = jnp.mean(amplitude, axis=1, keepdims=True)
    divisor = smooth + level + 1e-06
    white = spectrum / jnp.concatenate([divisor, divisor], axis=1)
    return white.astype(jnp.bfloat16).reshape(count, SEG * NFFT)


def cross(first_rows, second_rows):
    left = first_rows.astype(jnp.float32).reshape(first_rows.shape[:-1] + (SEG, 2, BINS))
    right = second_rows.astype(jnp.float32).reshape(second_rows.shape[:-1] + (SEG, 2, BINS))
    real_sum = jnp.mean(
        left[..., 0, :] * right[..., 0, :] + left[..., 1, :] * right[..., 1, :], axis=-2
    )
    imag_sum = jnp.mean(
        left[..., 0, :] * right[..., 1, :] - left[..., 1, :] * right[..., 0, :], axis=-2
    )
    return jnp.concatenate([real_sum, imag_sum], axis=-1).astype(jnp.bfloat16)


def _pick_kernel(ids_ref, table_ref, out_ref):
    ids = ids_ref[...]
    rows = table_ref.shape[0]
    onehot = (lax.broadcasted_iota(jnp.int32, (ids.shape[0], rows), 1) == ids).astype(table_ref.dtype)
    out_ref[...] = jnp.dot(onehot, table_ref[...], preferred_element_type=jnp.float32).astype(out_ref.dtype)


def pick_rows(table, ids, block=2048):
    rows, width = table.shape
    count = ids.shape[0]
    block = min(block, count)
    return pl.pallas_call(
        _pick_kernel,
        out_shape=jax.ShapeDtypeStruct((count, width), table.dtype),
        grid=(count // block,),
        in_specs=[
            pl.BlockSpec((block, 1), lambda i: (i, 0)),
            pl.BlockSpec((rows, width), lambda i: (0, 0)),
        ],
        out_specs=pl.BlockSpec((block, width), lambda i: (i, 0)),
        cost_estimate=pl.CostEstimate(
            flops=2 * count * rows * width, transcendentals=0, bytes_accessed=2 * (rows + count) * width
        ),
    )(ids.reshape(count, 1), table)


def _compact_kernel(ids_ref, table_ref, out_ref):
    buckets, slabs, capacity, width = table_ref.shape
    for s in range(slabs):
        ids = ids_ref[s]
        table = table_ref[:, s].reshape(buckets * capacity, width)
        onehot = (lax.broadcasted_iota(jnp.int32, (ids.shape[0], buckets * capacity), 1) == ids).astype(table.dtype)
        out_ref[s] = jnp.dot(onehot, table, preferred_element_type=jnp.float32).astype(out_ref.dtype)


def compact_rows(arrived, slots):
    buckets, slabs, capacity, width = arrived.shape
    pairs = slots.shape[1]
    return pl.pallas_call(
        _compact_kernel,
        out_shape=jax.ShapeDtypeStruct((slabs, pairs, width), arrived.dtype),
        cost_estimate=pl.CostEstimate(
            flops=2 * slabs * pairs * buckets * capacity * width,
            transcendentals=0,
            bytes_accessed=2 * (buckets * capacity + pairs) * slabs * width,
        ),
    )(slots.reshape(slabs, pairs, 1), arrived)


def _white_block(slices, table, taper):
    per_segment = len(slices) // SEG
    tapered = []
    for segment in range(SEG):
        part = [piece.astype(jnp.float32) for piece in slices[segment * per_segment : (segment + 1) * per_segment]]
        total = jnp.sum(part[0], axis=1, keepdims=True)
        for piece in part[1:]:
            total = total + jnp.sum(piece, axis=1, keepdims=True)
        mean = total / NFFT
        pieces = [((part[i] - mean) * taper[i : i + 1, :]).astype(jnp.bfloat16) for i in range(per_segment)]
        tapered.append(jnp.concatenate(pieces, axis=1))
    spectrum = jnp.dot(jnp.concatenate(tapered, axis=0), table, preferred_element_type=jnp.float32)
    real_part = spectrum[:, :BINS]
    imag_part = spectrum[:, BINS:]
    amplitude = jnp.sqrt(real_part * real_part + imag_part * imag_part + 1e-06)
    lane = lax.broadcasted_iota(jnp.int32, amplitude.shape, 1)
    smooth = jnp.zeros_like(amplitude)
    for offset in range(-HALF, HALF + 1):
        moved = amplitude if offset == 0 else pltpu.roll(amplitude, (-offset) % BINS, 1)
        inside = (lane + offset >= 0) & (lane + offset < BINS)
        smooth = smooth + jnp.where(inside, moved, 0.0)
    smooth = smooth / (2 * HALF + 1)
    level = jnp.sum(amplitude, axis=1, keepdims=True) / BINS
    divisor = smooth + level + 1e-06
    white_real = (real_part / divisor).astype(jnp.bfloat16)
    white_imag = (imag_part / divisor).astype(jnp.bfloat16)
    return white_real, white_imag


def _white_kernel(x_ref, table_ref, taper_ref, out_ref):
    rows = x_ref.shape[1]
    slices = [x_ref[i] for i in range(x_ref.shape[0])]
    white_real, white_imag = _white_block(slices, table_ref[...], taper_ref[...])
    for segment in range(SEG):
        out_ref[2 * segment] = white_real[segment * rows : (segment + 1) * rows]
        out_ref[2 * segment + 1] = white_imag[segment * rows : (segment + 1) * rows]


def _cross_kernel(ids_ref, arrived_hbm, first_hbm, table_hbm, taper_ref, out_ref, arrived_ref, first_ref, table_ref, sems):
    arrived_copy = pltpu.make_async_copy(arrived_hbm, arrived_ref, sems.at[0])
    table_copy = pltpu.make_async_copy(table_hbm, table_ref, sems.at[1])
    first_copy = pltpu.make_async_copy(first_hbm, first_ref, sems.at[2])
    arrived_copy.start()
    first_copy.start()
    table_copy.start()
    buckets, slabs, capacity, width = arrived_ref.shape
    ids = ids_ref[...]
    rows = ids.shape[0]
    onehot = (lax.broadcasted_iota(jnp.int32, (rows, buckets * capacity), 1) == ids).astype(arrived_ref.dtype)
    arrived_copy.wait()
    slices = [
        jnp.dot(onehot, arrived_ref[:, s].reshape(buckets * capacity, width), preferred_element_type=jnp.float32).astype(
            arrived_ref.dtype
        )
        for s in range(slabs)
    ]
    table_copy.wait()
    white_real, white_imag = _white_block(slices, table_ref[...], taper_ref[...])
    first_copy.wait()
    real_sum = None
    imag_sum = None
    for segment in range(SEG):
        left_real = first_ref[2 * segment].astype(jnp.float32)
        left_imag = first_ref[2 * segment + 1].astype(jnp.float32)
        right_real = white_real[segment * rows : (segment + 1) * rows].astype(jnp.float32)
        right_imag = white_imag[segment * rows : (segment + 1) * rows].astype(jnp.float32)
        real_term = left_real * right_real + left_imag * right_imag
        imag_term = left_real * right_imag - left_imag * right_real
        real_sum = real_term if real_sum is None else real_sum + real_term
        imag_sum = imag_term if imag_sum is None else imag_sum + imag_term
    out_ref[:, :BINS] = (real_sum / SEG).astype(out_ref.dtype)
    out_ref[:, BINS:] = (imag_sum / SEG).astype(out_ref.dtype)


def taper_table(slabs_per_segment, width):
    position = jnp.arange(NFFT, dtype=jnp.int32).astype(jnp.float32)
    taper = 0.5 - 0.5 * jnp.cos(position * (2.0 * math.pi / NFFT))
    return taper.reshape(slabs_per_segment, width)


def _white_specs(slabs, block, width, per_segment):
    return [
        pl.BlockSpec((slabs, block, width), lambda i: (0, i, 0)),
        pl.BlockSpec((NFFT, 2 * BINS), lambda i: (0, 0), pipeline_mode=pl.Buffered(1)),
        pl.BlockSpec((per_segment, width), lambda i: (0, 0)),
    ]


def white_rows(parts, table, taper, block=128):
    slabs, rows, width = parts.shape
    specs = _white_specs(slabs, block, width, slabs // SEG)
    return pl.pallas_call(
        _white_kernel,
        out_shape=jax.ShapeDtypeStruct((2 * SEG, rows, BINS), jnp.bfloat16),
        grid=(rows // block,),
        in_specs=specs,
        out_specs=pl.BlockSpec((2 * SEG, block, BINS), lambda i: (0, i, 0)),
        compiler_params=pltpu.CompilerParams(vmem_limit_bytes=48 * 1024 * 1024),
        cost_estimate=pl.CostEstimate(
            flops=2 * SEG * rows * NFFT * 2 * BINS, transcendentals=SEG * rows * BINS,
            bytes_accessed=NFFT * 2 * BINS * 2 + 4 * slabs * rows * width,
        ),
    )(parts, table, taper)


def cross_rows(arrived, slots, first_white, table, taper):
    buckets, slabs, capacity, width = arrived.shape
    rows = slots.shape[0]
    vmem = pltpu.MemorySpace.VMEM
    return pl.pallas_call(
        _cross_kernel,
        out_shape=jax.ShapeDtypeStruct((rows, 2 * BINS), jnp.bfloat16),
        in_specs=[
            pl.BlockSpec(memory_space=vmem),
            pl.BlockSpec(memory_space=pl.ANY),
            pl.BlockSpec(memory_space=pltpu.MemorySpace.HBM),
            pl.BlockSpec(memory_space=pl.ANY),
            pl.BlockSpec(memory_space=vmem),
        ],
        out_specs=pl.BlockSpec(memory_space=vmem),
        scratch_shapes=[
            pltpu.VMEM(arrived.shape, arrived.dtype),
            pltpu.VMEM(first_white.shape, first_white.dtype),
            pltpu.VMEM(table.shape, table.dtype),
            pltpu.SemaphoreType.DMA((3,)),
        ],
        compiler_params=pltpu.CompilerParams(vmem_limit_bytes=48 * 1024 * 1024),
        cost_estimate=pl.CostEstimate(
            flops=2 * SEG * rows * NFFT * 2 * BINS, transcendentals=SEG * rows * BINS,
            bytes_accessed=NFFT * 2 * BINS * 2 + 2 * arrived.size,
        ),
    )(slots.reshape(rows, 1), arrived, first_white, table, taper)


def _exchange_kernel(axis, x_ref, out_ref, landed, send_sems, recv_sems):
    count = x_ref.shape[0]
    me = lax.axis_index(axis)

    def peer_id(peer):
        return {axis: peer}

    barrier = pltpu.get_barrier_semaphore()
    for step in range(1, count):
        pl.semaphore_signal(
            barrier, inc=1, device_id=peer_id(lax.rem(me + step, count)), device_id_type=pl.DeviceIdType.MESH
        )
    pl.semaphore_wait(barrier, count - 1)
    copies = []
    for step in range(1, count):
        peer = lax.rem(me + step, count)
        copy = pltpu.make_async_remote_copy(
            src_ref=x_ref.at[peer],
            dst_ref=landed.at[me],
            send_sem=send_sems.at[step],
            recv_sem=recv_sems.at[step],
            device_id=peer_id(peer),
            device_id_type=pl.DeviceIdType.MESH,
        )
        copy.start()
        copies.append(copy)
    landed[me] = x_ref[me]
    for copy in copies:
        copy.wait_send()
        copy.wait_recv()
    out_ref[...] = landed[...]


def exchange(parts, axis, collective):
    count = parts.shape[0]
    return pl.pallas_call(
        functools.partial(_exchange_kernel, axis),
        out_shape=jax.ShapeDtypeStruct(parts.shape, parts.dtype),
        scratch_shapes=[
            pltpu.VMEM(parts.shape, parts.dtype),
            pltpu.SemaphoreType.DMA((count,)),
            pltpu.SemaphoreType.DMA((count,)),
        ],
        compiler_params=pltpu.CompilerParams(collective_id=collective, has_side_effects=True),
        cost_estimate=pl.CostEstimate(flops=0, transcendentals=0, bytes_accessed=4 * parts.size),
    )(parts)


def to_rows(parts):
    slabs, rows, width = parts.shape
    return jnp.transpose(parts, (1, 0, 2)).reshape(rows, slabs * width)


def local(records, first_station, second_region, second_station):
    regions = lax.axis_size("region")
    slabs = lax.axis_size("slab")
    pair_count = first_station.shape[0]
    width = records.shape[1]
    capacity = max(2, pair_count // regions + pair_count // 16)

    target = second_region[:, 0]
    onehot = (target[:, None] == jnp.arange(regions, dtype=jnp.int32)[None, :]).astype(jnp.int32)
    ranking = jnp.sum((jnp.cumsum(onehot, axis=0) - onehot) * onehot, axis=1)
    slot_index = target * capacity + ranking
    requests = (
        jnp.zeros((regions * capacity,), jnp.int32)
        .at[slot_index]
        .set(second_station)
    )
    own = jnp.pad(requests.reshape(-1, 128), ((0, (-(regions * capacity // 128)) % 8), (0, 0)))
    plane = exchange(jnp.broadcast_to(own[None], (slabs,) + own.shape), "slab", 2)
    plane_requests = plane[:, : regions * capacity // 128].reshape(slabs, regions, capacity)
    outgoing = jnp.transpose(plane_requests, (1, 0, 2)).reshape(regions, -1, 128)
    outgoing = jnp.pad(outgoing, ((0, 0), (0, (-outgoing.shape[1]) % 8), (0, 0)))
    asked = exchange(outgoing, "region", 1)[:, : slabs * capacity // 128].reshape(-1)

    firsts = lax.all_gather(first_station, "slab", axis=0, tiled=False)
    first_parts = pick_rows(records, firsts.reshape(-1)).reshape(slabs, pair_count, width)
    first_arrived = exchange(first_parts, "slab", 0)
    table = dft_table()
    taper = taper_table(slabs // SEG, width)
    first_white = white_rows(first_arrived, table, taper)

    served = pick_rows(records, asked)
    served = served.reshape(regions * slabs, capacity, width)
    arrived = lax.all_to_all(served, ("region", "slab"), split_axis=0, concat_axis=0, tiled=True)
    arrived, _ = lax.optimization_barrier((arrived, first_white[0, :8, :128]))
    first_white = pltpu.with_memory_space_constraint(first_white, pltpu.MemorySpace.HBM)
    return cross_rows(arrived.reshape(regions, slabs, capacity, width), slot_index, first_white, table, taper)

def solution(mesh):
    placed = (
        P("region", "slab"),
        P(("region", "slab")),
        P(("region", "slab"), None),
        P(("region", "slab")),
    )
    return jax.shard_map(
        local, mesh=mesh, in_specs=placed, out_specs=P(("region", "slab"), None), check_vma=False
    )
```

```python
import functools
import math

import jax
import jax.numpy as jnp
from jax import lax
from jax.experimental import pallas as pl
from jax.experimental.pallas import tpu as pltpu
from jax.sharding import PartitionSpec as P

NFFT = 2048
BINS = 1024
SEG = 2
HALF = 4


def dft_table():
    low = 64
    high = NFFT // low
    frequency = jnp.arange(BINS, dtype=jnp.int32)[None, :]
    coarse = jnp.arange(high, dtype=jnp.int32)[:, None]
    fine = jnp.arange(low, dtype=jnp.int32)[:, None]
    angle_a = ((coarse * frequency) % high).astype(jnp.float32) * (2.0 * math.pi / high)
    angle_b = ((fine * frequency) % NFFT).astype(jnp.float32) * (2.0 * math.pi / NFFT)
    ca, sa = jnp.cos(angle_a)[:, None, :], jnp.sin(angle_a)[:, None, :]
    cb, sb = jnp.cos(angle_b)[None, :, :], jnp.sin(angle_b)[None, :, :]
    cos_part = (ca * cb - sa * sb).reshape(NFFT, BINS)
    sin_part = (sa * cb + ca * sb).reshape(NFFT, BINS)
    return jnp.concatenate([cos_part, -sin_part], axis=1).astype(jnp.bfloat16)


def whitened(traces):
    count = traces.shape[0]
    signal = traces.astype(jnp.float32).reshape(count * SEG, NFFT)
    signal = signal - jnp.mean(signal, axis=1, keepdims=True)
    position = jnp.arange(NFFT, dtype=jnp.int32).astype(jnp.float32)
    taper = 0.5 - 0.5 * jnp.cos(position * (2.0 * math.pi / NFFT))
    tapered = (signal * taper[None, :]).astype(jnp.bfloat16)
    spectrum = jnp.dot(tapered, dft_table(), preferred_element_type=jnp.float32)
    real_part = spectrum[:, :BINS]
    imag_part = spectrum[:, BINS:]
    amplitude = jnp.sqrt(real_part * real_part + imag_part * imag_part + 1e-06)
    padded = jnp.pad(amplitude, ((0, 0), (HALF, HALF)))
    smooth = jnp.zeros_like(amplitude)
    for offset in range(2 * HALF + 1):
        smooth = smooth + padded[:, offset : offset + BINS]
    smooth = smooth / (2 * HALF + 1)
    level = jnp.mean(amplitude, axis=1, keepdims=True)
    divisor = smooth + level + 1e-06
    white = spectrum / jnp.concatenate([divisor, divisor], axis=1)
    return white.astype(jnp.bfloat16).reshape(count, SEG * NFFT)


def cross(first_rows, second_rows):
    left = first_rows.astype(jnp.float32).reshape(first_rows.shape[:-1] + (SEG, 2, BINS))
    right = second_rows.astype(jnp.float32).reshape(second_rows.shape[:-1] + (SEG, 2, BINS))
    real_sum = jnp.mean(
        left[..., 0, :] * right[..., 0, :] + left[..., 1, :] * right[..., 1, :], axis=-2
    )
    imag_sum = jnp.mean(
        left[..., 0, :] * right[..., 1, :] - left[..., 1, :] * right[..., 0, :], axis=-2
    )
    return jnp.concatenate([real_sum, imag_sum], axis=-1).astype(jnp.bfloat16)


def _pick_kernel(ids_ref, table_ref, out_ref):
    ids = jnp.transpose(ids_ref[...])[:, :1]
    rows = table_ref.shape[0]
    onehot = (lax.broadcasted_iota(jnp.int32, (ids.shape[0], rows), 1) == ids).astype(table_ref.dtype)
    out_ref[...] = jnp.dot(onehot, table_ref[...], preferred_element_type=jnp.float32).astype(out_ref.dtype)


def pick_rows(table, ids, block=2048):
    rows, width = table.shape
    count = ids.shape[0]
    block = min(block, count)
    return pl.pallas_call(
        _pick_kernel,
        out_shape=jax.ShapeDtypeStruct((count, width), table.dtype),
        grid=(count // block,),
        in_specs=[
            pl.BlockSpec((8, block), lambda i: (0, i)),
            pl.BlockSpec((rows, width), lambda i: (0, 0)),
        ],
        out_specs=pl.BlockSpec((block, width), lambda i: (i, 0)),
        cost_estimate=pl.CostEstimate(
            flops=2 * count * rows * width, transcendentals=0, bytes_accessed=2 * (rows + count) * width
        ),
    )(jnp.broadcast_to(ids[None, :], (8, count)), table)


def _compact_kernel(ids_ref, table_ref, out_ref):
    buckets, slabs, capacity, width = table_ref.shape
    for s in range(slabs):
        ids = ids_ref[s]
        table = table_ref[:, s].reshape(buckets * capacity, width)
        onehot = (lax.broadcasted_iota(jnp.int32, (ids.shape[0], buckets * capacity), 1) == ids).astype(table.dtype)
        out_ref[s] = jnp.dot(onehot, table, preferred_element_type=jnp.float32).astype(out_ref.dtype)


def compact_rows(arrived, slots):
    buckets, slabs, capacity, width = arrived.shape
    pairs = slots.shape[1]
    return pl.pallas_call(
        _compact_kernel,
        out_shape=jax.ShapeDtypeStruct((slabs, pairs, width), arrived.dtype),
        cost_estimate=pl.CostEstimate(
            flops=2 * slabs * pairs * buckets * capacity * width,
            transcendentals=0,
            bytes_accessed=2 * (buckets * capacity + pairs) * slabs * width,
        ),
    )(slots.reshape(slabs, pairs, 1), arrived)


def _white_block(slices, table, taper):
    per_segment = len(slices) // SEG
    tapered = []
    for segment in range(SEG):
        part = [piece.astype(jnp.float32) for piece in slices[segment * per_segment : (segment + 1) * per_segment]]
        total = jnp.sum(part[0], axis=1, keepdims=True)
        for piece in part[1:]:
            total = total + jnp.sum(piece, axis=1, keepdims=True)
        mean = total / NFFT
        pieces = [((part[i] - mean) * taper[i : i + 1, :]).astype(jnp.bfloat16) for i in range(per_segment)]
        tapered.append(jnp.concatenate(pieces, axis=1))
    spectrum = jnp.dot(jnp.concatenate(tapered, axis=0), table, preferred_element_type=jnp.float32)
    real_part = spectrum[:, :BINS]
    imag_part = spectrum[:, BINS:]
    amplitude = jnp.sqrt(real_part * real_part + imag_part * imag_part + 1e-06)
    lane = lax.broadcasted_iota(jnp.int32, amplitude.shape, 1)
    smooth = jnp.zeros_like(amplitude)
    for offset in range(-HALF, HALF + 1):
        moved = amplitude if offset == 0 else pltpu.roll(amplitude, (-offset) % BINS, 1)
        inside = (lane + offset >= 0) & (lane + offset < BINS)
        smooth = smooth + jnp.where(inside, moved, 0.0)
    smooth = smooth / (2 * HALF + 1)
    level = jnp.sum(amplitude, axis=1, keepdims=True) / BINS
    divisor = smooth + level + 1e-06
    white_real = (real_part / divisor).astype(jnp.bfloat16)
    white_imag = (imag_part / divisor).astype(jnp.bfloat16)
    return white_real, white_imag


def _white_kernel(x_ref, table_ref, taper_ref, out_ref):
    rows = x_ref.shape[1]
    slices = [x_ref[i] for i in range(x_ref.shape[0])]
    white_real, white_imag = _white_block(slices, table_ref[...], taper_ref[...])
    for segment in range(SEG):
        out_ref[2 * segment] = white_real[segment * rows : (segment + 1) * rows]
        out_ref[2 * segment + 1] = white_imag[segment * rows : (segment + 1) * rows]


def _cross_kernel(ids_ref, arrived_hbm, first_hbm, table_hbm, taper_ref, out_ref, arrived_ref, first_ref, table_ref, sems):
    arrived_copy = pltpu.make_async_copy(arrived_hbm, arrived_ref, sems.at[0])
    table_copy = pltpu.make_async_copy(table_hbm, table_ref, sems.at[1])
    first_copy = pltpu.make_async_copy(first_hbm, first_ref, sems.at[2])
    arrived_copy.start()
    first_copy.start()
    table_copy.start()
    buckets, slabs, capacity, width = arrived_ref.shape
    ids = ids_ref[...]
    rows = ids.shape[0]
    onehot = (lax.broadcasted_iota(jnp.int32, (rows, buckets * capacity), 1) == ids).astype(arrived_ref.dtype)
    arrived_copy.wait()
    slices = [
        jnp.dot(onehot, arrived_ref[:, s].reshape(buckets * capacity, width), preferred_element_type=jnp.float32).astype(
            arrived_ref.dtype
        )
        for s in range(slabs)
    ]
    table_copy.wait()
    white_real, white_imag = _white_block(slices, table_ref[...], taper_ref[...])
    first_copy.wait()
    real_sum = None
    imag_sum = None
    for segment in range(SEG):
        left_real = first_ref[2 * segment].astype(jnp.float32)
        left_imag = first_ref[2 * segment + 1].astype(jnp.float32)
        right_real = white_real[segment * rows : (segment + 1) * rows].astype(jnp.float32)
        right_imag = white_imag[segment * rows : (segment + 1) * rows].astype(jnp.float32)
        real_term = left_real * right_real + left_imag * right_imag
        imag_term = left_real * right_imag - left_imag * right_real
        real_sum = real_term if real_sum is None else real_sum + real_term
        imag_sum = imag_term if imag_sum is None else imag_sum + imag_term
    out_ref[:, :BINS] = (real_sum / SEG).astype(out_ref.dtype)
    out_ref[:, BINS:] = (imag_sum / SEG).astype(out_ref.dtype)


def taper_table(slabs_per_segment, width):
    position = jnp.arange(NFFT, dtype=jnp.int32).astype(jnp.float32)
    taper = 0.5 - 0.5 * jnp.cos(position * (2.0 * math.pi / NFFT))
    return taper.reshape(slabs_per_segment, width)


def _white_specs(slabs, block, width, per_segment):
    return [
        pl.BlockSpec((slabs, block, width), lambda i: (0, i, 0)),
        pl.BlockSpec((NFFT, 2 * BINS), lambda i: (0, 0), pipeline_mode=pl.Buffered(1)),
        pl.BlockSpec((per_segment, width), lambda i: (0, 0)),
    ]


def white_rows(parts, table, taper, block=128):
    slabs, rows, width = parts.shape
    specs = _white_specs(slabs, block, width, slabs // SEG)
    return pl.pallas_call(
        _white_kernel,
        out_shape=jax.ShapeDtypeStruct((2 * SEG, rows, BINS), jnp.bfloat16),
        grid=(rows // block,),
        in_specs=specs,
        out_specs=pl.BlockSpec((2 * SEG, block, BINS), lambda i: (0, i, 0)),
        compiler_params=pltpu.CompilerParams(vmem_limit_bytes=48 * 1024 * 1024),
        cost_estimate=pl.CostEstimate(
            flops=2 * SEG * rows * NFFT * 2 * BINS, transcendentals=SEG * rows * BINS,
            bytes_accessed=NFFT * 2 * BINS * 2 + 4 * slabs * rows * width,
        ),
    )(parts, table, taper)


def cross_rows(arrived, slots, first_white, table, taper):
    buckets, slabs, capacity, width = arrived.shape
    rows = slots.shape[0]
    vmem = pltpu.MemorySpace.VMEM
    return pl.pallas_call(
        _cross_kernel,
        out_shape=jax.ShapeDtypeStruct((rows, 2 * BINS), jnp.bfloat16),
        in_specs=[
            pl.BlockSpec(memory_space=vmem),
            pl.BlockSpec(memory_space=pl.ANY),
            pl.BlockSpec(memory_space=pltpu.MemorySpace.HBM),
            pl.BlockSpec(memory_space=pl.ANY),
            pl.BlockSpec(memory_space=vmem),
        ],
        out_specs=pl.BlockSpec(memory_space=vmem),
        scratch_shapes=[
            pltpu.VMEM(arrived.shape, arrived.dtype),
            pltpu.VMEM(first_white.shape, first_white.dtype),
            pltpu.VMEM(table.shape, table.dtype),
            pltpu.SemaphoreType.DMA((3,)),
        ],
        compiler_params=pltpu.CompilerParams(vmem_limit_bytes=48 * 1024 * 1024),
        cost_estimate=pl.CostEstimate(
            flops=2 * SEG * rows * NFFT * 2 * BINS, transcendentals=SEG * rows * BINS,
            bytes_accessed=NFFT * 2 * BINS * 2 + 2 * arrived.size,
        ),
    )(slots.reshape(rows, 1), arrived, first_white, table, taper)


def _exchange_kernel(axis, x_ref, out_ref, landed, send_sems, recv_sems):
    count = x_ref.shape[0]
    me = lax.axis_index(axis)

    def peer_id(peer):
        return {axis: peer}

    barrier = pltpu.get_barrier_semaphore()
    for step in range(1, count):
        pl.semaphore_signal(
            barrier, inc=1, device_id=peer_id(lax.rem(me + step, count)), device_id_type=pl.DeviceIdType.MESH
        )
    pl.semaphore_wait(barrier, count - 1)
    copies = []
    for step in range(1, count):
        peer = lax.rem(me + step, count)
        copy = pltpu.make_async_remote_copy(
            src_ref=x_ref.at[peer],
            dst_ref=landed.at[me],
            send_sem=send_sems.at[step],
            recv_sem=recv_sems.at[step],
            device_id=peer_id(peer),
            device_id_type=pl.DeviceIdType.MESH,
        )
        copy.start()
        copies.append(copy)
    landed[me] = x_ref[me]
    for copy in copies:
        copy.wait_send()
        copy.wait_recv()
    out_ref[...] = landed[...]


def exchange(parts, axis, collective):
    count = parts.shape[0]
    return pl.pallas_call(
        functools.partial(_exchange_kernel, axis),
        out_shape=jax.ShapeDtypeStruct(parts.shape, parts.dtype),
        scratch_shapes=[
            pltpu.VMEM(parts.shape, parts.dtype),
            pltpu.SemaphoreType.DMA((count,)),
            pltpu.SemaphoreType.DMA((count,)),
        ],
        compiler_params=pltpu.CompilerParams(collective_id=collective, has_side_effects=True),
        cost_estimate=pl.CostEstimate(flops=0, transcendentals=0, bytes_accessed=4 * parts.size),
    )(parts)


def to_rows(parts):
    slabs, rows, width = parts.shape
    return jnp.transpose(parts, (1, 0, 2)).reshape(rows, slabs * width)


def local(records, first_station, second_region, second_station):
    regions = lax.axis_size("region")
    slabs = lax.axis_size("slab")
    pair_count = first_station.shape[0]
    width = records.shape[1]
    capacity = max(2, pair_count // regions + pair_count // 16)

    target = second_region[:, 0]
    onehot = (target[:, None] == jnp.arange(regions, dtype=jnp.int32)[None, :]).astype(jnp.int32)
    ranking = jnp.sum((jnp.cumsum(onehot, axis=0) - onehot) * onehot, axis=1)
    slot_index = target * capacity + ranking
    requests = (
        jnp.zeros((regions * capacity,), jnp.int32)
        .at[slot_index]
        .set(second_station)
    )
    own = jnp.pad(requests.reshape(-1, 128), ((0, (-(regions * capacity // 128)) % 8), (0, 0)))
    plane = exchange(jnp.broadcast_to(own[None], (slabs,) + own.shape), "slab", 2)
    plane_requests = plane[:, : regions * capacity // 128].reshape(slabs, regions, capacity)
    outgoing = jnp.transpose(plane_requests, (1, 0, 2)).reshape(regions, -1, 128)
    outgoing = jnp.pad(outgoing, ((0, 0), (0, (-outgoing.shape[1]) % 8), (0, 0)))
    asked = exchange(outgoing, "region", 1)[:, : slabs * capacity // 128].reshape(-1)

    firsts = lax.all_gather(first_station, "slab", axis=0, tiled=False)
    first_parts = pick_rows(records, firsts.reshape(-1)).reshape(slabs, pair_count, width)
    first_arrived = exchange(first_parts, "slab", 0)
    table = dft_table()
    taper = taper_table(slabs // SEG, width)
    first_white = white_rows(first_arrived, table, taper)

    served = pick_rows(records, asked)
    served = served.reshape(regions * slabs, capacity, width)
    arrived = lax.all_to_all(served, ("region", "slab"), split_axis=0, concat_axis=0, tiled=True)
    arrived, _ = lax.optimization_barrier((arrived, first_white[0, :8, :128]))
    first_white = pltpu.with_memory_space_constraint(first_white, pltpu.MemorySpace.HBM)
    return cross_rows(arrived.reshape(regions, slabs, capacity, width), slot_index, first_white, table, taper)

def solution(mesh):
    placed = (
        P("region", "slab"),
        P(("region", "slab")),
        P(("region", "slab"), None),
        P(("region", "slab")),
    )
    return jax.shard_map(
        local, mesh=mesh, in_specs=placed, out_specs=P(("region", "slab"), None), check_vma=False
    )
```

```python
import functools
import math

import jax
import jax.numpy as jnp
from jax import lax
from jax.experimental import pallas as pl
from jax.experimental.pallas import tpu as pltpu
from jax.sharding import PartitionSpec as P

NFFT = 2048
BINS = 1024
SEG = 2
HALF = 4


def dft_table():
    low = 64
    high = NFFT // low
    frequency = jnp.arange(BINS, dtype=jnp.int32)[None, :]
    coarse = jnp.arange(high, dtype=jnp.int32)[:, None]
    fine = jnp.arange(low, dtype=jnp.int32)[:, None]
    angle_a = ((coarse * frequency) % high).astype(jnp.float32) * (2.0 * math.pi / high)
    angle_b = ((fine * frequency) % NFFT).astype(jnp.float32) * (2.0 * math.pi / NFFT)
    ca, sa = jnp.cos(angle_a)[:, None, :], jnp.sin(angle_a)[:, None, :]
    cb, sb = jnp.cos(angle_b)[None, :, :], jnp.sin(angle_b)[None, :, :]
    cos_part = (ca * cb - sa * sb).reshape(NFFT, BINS)
    sin_part = (sa * cb + ca * sb).reshape(NFFT, BINS)
    return jnp.concatenate([cos_part, -sin_part], axis=1).astype(jnp.bfloat16)


def whitened(traces):
    count = traces.shape[0]
    signal = traces.astype(jnp.float32).reshape(count * SEG, NFFT)
    signal = signal - jnp.mean(signal, axis=1, keepdims=True)
    position = jnp.arange(NFFT, dtype=jnp.int32).astype(jnp.float32)
    taper = 0.5 - 0.5 * jnp.cos(position * (2.0 * math.pi / NFFT))
    tapered = (signal * taper[None, :]).astype(jnp.bfloat16)
    spectrum = jnp.dot(tapered, dft_table(), preferred_element_type=jnp.float32)
    real_part = spectrum[:, :BINS]
    imag_part = spectrum[:, BINS:]
    amplitude = jnp.sqrt(real_part * real_part + imag_part * imag_part + 1e-06)
    padded = jnp.pad(amplitude, ((0, 0), (HALF, HALF)))
    smooth = jnp.zeros_like(amplitude)
    for offset in range(2 * HALF + 1):
        smooth = smooth + padded[:, offset : offset + BINS]
    smooth = smooth / (2 * HALF + 1)
    level = jnp.mean(amplitude, axis=1, keepdims=True)
    divisor = smooth + level + 1e-06
    white = spectrum / jnp.concatenate([divisor, divisor], axis=1)
    return white.astype(jnp.bfloat16).reshape(count, SEG * NFFT)


def cross(first_rows, second_rows):
    left = first_rows.astype(jnp.float32).reshape(first_rows.shape[:-1] + (SEG, 2, BINS))
    right = second_rows.astype(jnp.float32).reshape(second_rows.shape[:-1] + (SEG, 2, BINS))
    real_sum = jnp.mean(
        left[..., 0, :] * right[..., 0, :] + left[..., 1, :] * right[..., 1, :], axis=-2
    )
    imag_sum = jnp.mean(
        left[..., 0, :] * right[..., 1, :] - left[..., 1, :] * right[..., 0, :], axis=-2
    )
    return jnp.concatenate([real_sum, imag_sum], axis=-1).astype(jnp.bfloat16)


def _pick_kernel(ids_ref, table_ref, out_ref):
    ids = ids_ref[...]
    rows = table_ref.shape[0]
    onehot = (lax.broadcasted_iota(jnp.int32, (ids.shape[0], rows), 1) == ids).astype(table_ref.dtype)
    out_ref[...] = jnp.dot(onehot, table_ref[...], preferred_element_type=jnp.float32).astype(out_ref.dtype)


def pick_rows(table, ids, block=2048):
    rows, width = table.shape
    count = ids.shape[0]
    block = min(block, count)
    return pl.pallas_call(
        _pick_kernel,
        out_shape=jax.ShapeDtypeStruct((count, width), table.dtype),
        grid=(count // block,),
        in_specs=[
            pl.BlockSpec((block, 1), lambda i: (i, 0)),
            pl.BlockSpec((rows, width), lambda i: (0, 0)),
        ],
        out_specs=pl.BlockSpec((block, width), lambda i: (i, 0)),
        cost_estimate=pl.CostEstimate(
            flops=2 * count * rows * width, transcendentals=0, bytes_accessed=2 * (rows + count) * width
        ),
    )(ids.reshape(count, 1), table)


def _compact_kernel(ids_ref, table_ref, out_ref):
    buckets, slabs, capacity, width = table_ref.shape
    for s in range(slabs):
        ids = ids_ref[s]
        table = table_ref[:, s].reshape(buckets * capacity, width)
        onehot = (lax.broadcasted_iota(jnp.int32, (ids.shape[0], buckets * capacity), 1) == ids).astype(table.dtype)
        out_ref[s] = jnp.dot(onehot, table, preferred_element_type=jnp.float32).astype(out_ref.dtype)


def compact_rows(arrived, slots):
    buckets, slabs, capacity, width = arrived.shape
    pairs = slots.shape[1]
    return pl.pallas_call(
        _compact_kernel,
        out_shape=jax.ShapeDtypeStruct((slabs, pairs, width), arrived.dtype),
        cost_estimate=pl.CostEstimate(
            flops=2 * slabs * pairs * buckets * capacity * width,
            transcendentals=0,
            bytes_accessed=2 * (buckets * capacity + pairs) * slabs * width,
        ),
    )(slots.reshape(slabs, pairs, 1), arrived)


def _white_block(slices, table, taper):
    per_segment = len(slices) // SEG
    tapered = []
    for segment in range(SEG):
        part = [piece.astype(jnp.float32) for piece in slices[segment * per_segment : (segment + 1) * per_segment]]
        total = jnp.sum(part[0], axis=1, keepdims=True)
        for piece in part[1:]:
            total = total + jnp.sum(piece, axis=1, keepdims=True)
        mean = total / NFFT
        pieces = [((part[i] - mean) * taper[i : i + 1, :]).astype(jnp.bfloat16) for i in range(per_segment)]
        tapered.append(jnp.concatenate(pieces, axis=1))
    spectrum = jnp.dot(jnp.concatenate(tapered, axis=0), table, preferred_element_type=jnp.float32)
    real_part = spectrum[:, :BINS]
    imag_part = spectrum[:, BINS:]
    amplitude = jnp.sqrt(real_part * real_part + imag_part * imag_part + 1e-06)
    lane = lax.broadcasted_iota(jnp.int32, amplitude.shape, 1)
    smooth = jnp.zeros_like(amplitude)
    for offset in range(-HALF, HALF + 1):
        moved = amplitude if offset == 0 else pltpu.roll(amplitude, (-offset) % BINS, 1)
        inside = (lane + offset >= 0) & (lane + offset < BINS)
        smooth = smooth + jnp.where(inside, moved, 0.0)
    smooth = smooth / (2 * HALF + 1)
    level = jnp.sum(amplitude, axis=1, keepdims=True) / BINS
    divisor = smooth + level + 1e-06
    inverse = 1.0 / divisor
    white_real = (real_part * inverse).astype(jnp.bfloat16)
    white_imag = (imag_part * inverse).astype(jnp.bfloat16)
    return white_real, white_imag


def _white_kernel(x_ref, table_ref, taper_ref, out_ref):
    rows = x_ref.shape[1]
    slices = [x_ref[i] for i in range(x_ref.shape[0])]
    white_real, white_imag = _white_block(slices, table_ref[...], taper_ref[...])
    for segment in range(SEG):
        out_ref[2 * segment] = white_real[segment * rows : (segment + 1) * rows]
        out_ref[2 * segment + 1] = white_imag[segment * rows : (segment + 1) * rows]


def _cross_kernel(ids_ref, arrived_hbm, first_hbm, table_hbm, taper_ref, out_ref, arrived_ref, first_ref, table_ref, sems):
    arrived_copy = pltpu.make_async_copy(arrived_hbm, arrived_ref, sems.at[0])
    table_copy = pltpu.make_async_copy(table_hbm, table_ref, sems.at[1])
    first_copy = pltpu.make_async_copy(first_hbm, first_ref, sems.at[2])
    arrived_copy.start()
    first_copy.start()
    table_copy.start()
    buckets, slabs, capacity, width = arrived_ref.shape
    ids = ids_ref[...]
    rows = ids.shape[0]
    onehot = (lax.broadcasted_iota(jnp.int32, (rows, buckets * capacity), 1) == ids).astype(arrived_ref.dtype)
    arrived_copy.wait()
    slices = [
        jnp.dot(onehot, arrived_ref[:, s].reshape(buckets * capacity, width), preferred_element_type=jnp.float32).astype(
            arrived_ref.dtype
        )
        for s in range(slabs)
    ]
    table_copy.wait()
    white_real, white_imag = _white_block(slices, table_ref[...], taper_ref[...])
    first_copy.wait()
    real_sum = None
    imag_sum = None
    for segment in range(SEG):
        left_real = first_ref[2 * segment].astype(jnp.float32)
        left_imag = first_ref[2 * segment + 1].astype(jnp.float32)
        right_real = white_real[segment * rows : (segment + 1) * rows].astype(jnp.float32)
        right_imag = white_imag[segment * rows : (segment + 1) * rows].astype(jnp.float32)
        real_term = left_real * right_real + left_imag * right_imag
        imag_term = left_real * right_imag - left_imag * right_real
        real_sum = real_term if real_sum is None else real_sum + real_term
        imag_sum = imag_term if imag_sum is None else imag_sum + imag_term
    out_ref[:, :BINS] = (real_sum / SEG).astype(out_ref.dtype)
    out_ref[:, BINS:] = (imag_sum / SEG).astype(out_ref.dtype)


def taper_table(slabs_per_segment, width):
    position = jnp.arange(NFFT, dtype=jnp.int32).astype(jnp.float32)
    taper = 0.5 - 0.5 * jnp.cos(position * (2.0 * math.pi / NFFT))
    return taper.reshape(slabs_per_segment, width)


def _white_specs(slabs, block, width, per_segment):
    return [
        pl.BlockSpec((slabs, block, width), lambda i: (0, i, 0)),
        pl.BlockSpec((NFFT, 2 * BINS), lambda i: (0, 0), pipeline_mode=pl.Buffered(1)),
        pl.BlockSpec((per_segment, width), lambda i: (0, 0)),
    ]


def white_rows(parts, table, taper, block=128):
    slabs, rows, width = parts.shape
    specs = _white_specs(slabs, block, width, slabs // SEG)
    return pl.pallas_call(
        _white_kernel,
        out_shape=jax.ShapeDtypeStruct((2 * SEG, rows, BINS), jnp.bfloat16),
        grid=(rows // block,),
        in_specs=specs,
        out_specs=pl.BlockSpec((2 * SEG, block, BINS), lambda i: (0, i, 0)),
        compiler_params=pltpu.CompilerParams(vmem_limit_bytes=48 * 1024 * 1024),
        cost_estimate=pl.CostEstimate(
            flops=2 * SEG * rows * NFFT * 2 * BINS, transcendentals=SEG * rows * BINS,
            bytes_accessed=NFFT * 2 * BINS * 2 + 4 * slabs * rows * width,
        ),
    )(parts, table, taper)


def cross_rows(arrived, slots, first_white, table, taper):
    buckets, slabs, capacity, width = arrived.shape
    rows = slots.shape[0]
    vmem = pltpu.MemorySpace.VMEM
    return pl.pallas_call(
        _cross_kernel,
        out_shape=jax.ShapeDtypeStruct((rows, 2 * BINS), jnp.bfloat16),
        in_specs=[
            pl.BlockSpec(memory_space=vmem),
            pl.BlockSpec(memory_space=pl.ANY),
            pl.BlockSpec(memory_space=pltpu.MemorySpace.HBM),
            pl.BlockSpec(memory_space=pl.ANY),
            pl.BlockSpec(memory_space=vmem),
        ],
        out_specs=pl.BlockSpec(memory_space=vmem),
        scratch_shapes=[
            pltpu.VMEM(arrived.shape, arrived.dtype),
            pltpu.VMEM(first_white.shape, first_white.dtype),
            pltpu.VMEM(table.shape, table.dtype),
            pltpu.SemaphoreType.DMA((3,)),
        ],
        compiler_params=pltpu.CompilerParams(vmem_limit_bytes=48 * 1024 * 1024),
        cost_estimate=pl.CostEstimate(
            flops=2 * SEG * rows * NFFT * 2 * BINS, transcendentals=SEG * rows * BINS,
            bytes_accessed=NFFT * 2 * BINS * 2 + 2 * arrived.size,
        ),
    )(slots.reshape(rows, 1), arrived, first_white, table, taper)


def _exchange_kernel(axis, x_ref, out_ref, landed, send_sems, recv_sems):
    count = x_ref.shape[0]
    me = lax.axis_index(axis)

    def peer_id(peer):
        return {axis: peer}

    barrier = pltpu.get_barrier_semaphore()
    for step in range(1, count):
        pl.semaphore_signal(
            barrier, inc=1, device_id=peer_id(lax.rem(me + step, count)), device_id_type=pl.DeviceIdType.MESH
        )
    pl.semaphore_wait(barrier, count - 1)
    copies = []
    for step in range(1, count):
        peer = lax.rem(me + step, count)
        copy = pltpu.make_async_remote_copy(
            src_ref=x_ref.at[peer],
            dst_ref=landed.at[me],
            send_sem=send_sems.at[step],
            recv_sem=recv_sems.at[step],
            device_id=peer_id(peer),
            device_id_type=pl.DeviceIdType.MESH,
        )
        copy.start()
        copies.append(copy)
    landed[me] = x_ref[me]
    for copy in copies:
        copy.wait_send()
        copy.wait_recv()
    out_ref[...] = landed[...]


def exchange(parts, axis, collective):
    count = parts.shape[0]
    return pl.pallas_call(
        functools.partial(_exchange_kernel, axis),
        out_shape=jax.ShapeDtypeStruct(parts.shape, parts.dtype),
        scratch_shapes=[
            pltpu.VMEM(parts.shape, parts.dtype),
            pltpu.SemaphoreType.DMA((count,)),
            pltpu.SemaphoreType.DMA((count,)),
        ],
        compiler_params=pltpu.CompilerParams(collective_id=collective, has_side_effects=True),
        cost_estimate=pl.CostEstimate(flops=0, transcendentals=0, bytes_accessed=4 * parts.size),
    )(parts)


def to_rows(parts):
    slabs, rows, width = parts.shape
    return jnp.transpose(parts, (1, 0, 2)).reshape(rows, slabs * width)


def local(records, first_station, second_region, second_station):
    regions = lax.axis_size("region")
    slabs = lax.axis_size("slab")
    pair_count = first_station.shape[0]
    width = records.shape[1]
    capacity = max(2, pair_count // regions + pair_count // 16)

    target = second_region[:, 0]
    onehot = (target[:, None] == jnp.arange(regions, dtype=jnp.int32)[None, :]).astype(jnp.int32)
    ranking = jnp.sum((jnp.cumsum(onehot, axis=0) - onehot) * onehot, axis=1)
    slot_index = target * capacity + ranking
    requests = (
        jnp.zeros((regions * capacity,), jnp.int32)
        .at[slot_index]
        .set(second_station)
    )
    own = jnp.pad(requests.reshape(-1, 128), ((0, (-(regions * capacity // 128)) % 8), (0, 0)))
    plane = exchange(jnp.broadcast_to(own[None], (slabs,) + own.shape), "slab", 2)
    plane_requests = plane[:, : regions * capacity // 128].reshape(slabs, regions, capacity)
    outgoing = jnp.transpose(plane_requests, (1, 0, 2)).reshape(regions, -1, 128)
    outgoing = jnp.pad(outgoing, ((0, 0), (0, (-outgoing.shape[1]) % 8), (0, 0)))
    asked = exchange(outgoing, "region", 1)[:, : slabs * capacity // 128].reshape(-1)

    firsts = lax.all_gather(first_station, "slab", axis=0, tiled=False)
    first_parts = pick_rows(records, firsts.reshape(-1)).reshape(slabs, pair_count, width)
    first_arrived = exchange(first_parts, "slab", 0)
    table = dft_table()
    taper = taper_table(slabs // SEG, width)
    first_white = white_rows(first_arrived, table, taper)

    served = pick_rows(records, asked)
    served = served.reshape(regions * slabs, capacity, width)
    arrived = lax.all_to_all(served, ("region", "slab"), split_axis=0, concat_axis=0, tiled=True)
    arrived, _ = lax.optimization_barrier((arrived, first_white[0, :8, :128]))
    first_white = pltpu.with_memory_space_constraint(first_white, pltpu.MemorySpace.HBM)
    return cross_rows(arrived.reshape(regions, slabs, capacity, width), slot_index, first_white, table, taper)

def solution(mesh):
    placed = (
        P("region", "slab"),
        P(("region", "slab")),
        P(("region", "slab"), None),
        P(("region", "slab")),
    )
    return jax.shard_map(
        local, mesh=mesh, in_specs=placed, out_specs=P(("region", "slab"), None), check_vma=False
    )
```

```python
import functools
import math

import jax
import jax.numpy as jnp
from jax import lax
from jax.experimental import pallas as pl
from jax.experimental.pallas import tpu as pltpu
from jax.sharding import PartitionSpec as P

NFFT = 2048
BINS = 1024
SEG = 2
HALF = 4


def dft_table():
    low = 64
    high = NFFT // low
    frequency = jnp.arange(BINS, dtype=jnp.int32)[None, :]
    coarse = jnp.arange(high, dtype=jnp.int32)[:, None]
    fine = jnp.arange(low, dtype=jnp.int32)[:, None]
    angle_a = ((coarse * frequency) % high).astype(jnp.float32) * (2.0 * math.pi / high)
    angle_b = ((fine * frequency) % NFFT).astype(jnp.float32) * (2.0 * math.pi / NFFT)
    ca, sa = jnp.cos(angle_a)[:, None, :], jnp.sin(angle_a)[:, None, :]
    cb, sb = jnp.cos(angle_b)[None, :, :], jnp.sin(angle_b)[None, :, :]
    cos_part = (ca * cb - sa * sb).reshape(NFFT, BINS)
    sin_part = (sa * cb + ca * sb).reshape(NFFT, BINS)
    return jnp.concatenate([cos_part, -sin_part], axis=1).astype(jnp.bfloat16)


def whitened(traces):
    count = traces.shape[0]
    signal = traces.astype(jnp.float32).reshape(count * SEG, NFFT)
    signal = signal - jnp.mean(signal, axis=1, keepdims=True)
    position = jnp.arange(NFFT, dtype=jnp.int32).astype(jnp.float32)
    taper = 0.5 - 0.5 * jnp.cos(position * (2.0 * math.pi / NFFT))
    tapered = (signal * taper[None, :]).astype(jnp.bfloat16)
    spectrum = jnp.dot(tapered, dft_table(), preferred_element_type=jnp.float32)
    real_part = spectrum[:, :BINS]
    imag_part = spectrum[:, BINS:]
    amplitude = jnp.sqrt(real_part * real_part + imag_part * imag_part + 1e-06)
    padded = jnp.pad(amplitude, ((0, 0), (HALF, HALF)))
    smooth = jnp.zeros_like(amplitude)
    for offset in range(2 * HALF + 1):
        smooth = smooth + padded[:, offset : offset + BINS]
    smooth = smooth / (2 * HALF + 1)
    level = jnp.mean(amplitude, axis=1, keepdims=True)
    divisor = smooth + level + 1e-06
    white = spectrum / jnp.concatenate([divisor, divisor], axis=1)
    return white.astype(jnp.bfloat16).reshape(count, SEG * NFFT)


def cross(first_rows, second_rows):
    left = first_rows.astype(jnp.float32).reshape(first_rows.shape[:-1] + (SEG, 2, BINS))
    right = second_rows.astype(jnp.float32).reshape(second_rows.shape[:-1] + (SEG, 2, BINS))
    real_sum = jnp.mean(
        left[..., 0, :] * right[..., 0, :] + left[..., 1, :] * right[..., 1, :], axis=-2
    )
    imag_sum = jnp.mean(
        left[..., 0, :] * right[..., 1, :] - left[..., 1, :] * right[..., 0, :], axis=-2
    )
    return jnp.concatenate([real_sum, imag_sum], axis=-1).astype(jnp.bfloat16)


def _pick_kernel(ids_ref, table_ref, out_ref):
    ids = ids_ref[...]
    rows = table_ref.shape[0]
    onehot = (lax.broadcasted_iota(jnp.int32, (ids.shape[0], rows), 1) == ids).astype(table_ref.dtype)
    out_ref[...] = jnp.dot(onehot, table_ref[...], preferred_element_type=jnp.float32).astype(out_ref.dtype)


def pick_rows(table, ids, block=2048):
    rows, width = table.shape
    count = ids.shape[0]
    block = min(block, count)
    return pl.pallas_call(
        _pick_kernel,
        out_shape=jax.ShapeDtypeStruct((count, width), table.dtype),
        grid=(count // block,),
        in_specs=[
            pl.BlockSpec((block, 1), lambda i: (i, 0)),
            pl.BlockSpec((rows, width), lambda i: (0, 0)),
        ],
        out_specs=pl.BlockSpec((block, width), lambda i: (i, 0)),
        cost_estimate=pl.CostEstimate(
            flops=2 * count * rows * width, transcendentals=0, bytes_accessed=2 * (rows + count) * width
        ),
    )(ids.reshape(count, 1), table)


def _compact_kernel(ids_ref, table_ref, out_ref):
    buckets, slabs, capacity, width = table_ref.shape
    for s in range(slabs):
        ids = ids_ref[s]
        table = table_ref[:, s].reshape(buckets * capacity, width)
        onehot = (lax.broadcasted_iota(jnp.int32, (ids.shape[0], buckets * capacity), 1) == ids).astype(table.dtype)
        out_ref[s] = jnp.dot(onehot, table, preferred_element_type=jnp.float32).astype(out_ref.dtype)


def compact_rows(arrived, slots):
    buckets, slabs, capacity, width = arrived.shape
    pairs = slots.shape[1]
    return pl.pallas_call(
        _compact_kernel,
        out_shape=jax.ShapeDtypeStruct((slabs, pairs, width), arrived.dtype),
        cost_estimate=pl.CostEstimate(
            flops=2 * slabs * pairs * buckets * capacity * width,
            transcendentals=0,
            bytes_accessed=2 * (buckets * capacity + pairs) * slabs * width,
        ),
    )(slots.reshape(slabs, pairs, 1), arrived)


def _white_block(slices, table, taper):
    per_segment = len(slices) // SEG
    tapered = []
    for segment in range(SEG):
        part = [piece.astype(jnp.float32) for piece in slices[segment * per_segment : (segment + 1) * per_segment]]
        total = jnp.sum(part[0], axis=1, keepdims=True)
        for piece in part[1:]:
            total = total + jnp.sum(piece, axis=1, keepdims=True)
        mean = total / NFFT
        pieces = [((part[i] - mean) * taper[i : i + 1, :]).astype(jnp.bfloat16) for i in range(per_segment)]
        tapered.append(jnp.concatenate(pieces, axis=1))
    spectrum = jnp.dot(jnp.concatenate(tapered, axis=0), table, preferred_element_type=jnp.float32)
    real_part = spectrum[:, :BINS]
    imag_part = spectrum[:, BINS:]
    amplitude = jnp.sqrt(real_part * real_part + imag_part * imag_part + 1e-06)
    lane = lax.broadcasted_iota(jnp.int32, amplitude.shape, 1)
    smooth = jnp.zeros_like(amplitude)
    for offset in range(-HALF, HALF + 1):
        moved = amplitude if offset == 0 else pltpu.roll(amplitude, (-offset) % BINS, 1)
        inside = (lane + offset >= 0) & (lane + offset < BINS)
        smooth = smooth + jnp.where(inside, moved, 0.0)
    smooth = smooth / (2 * HALF + 1)
    level = jnp.sum(amplitude, axis=1, keepdims=True) / BINS
    divisor = smooth + level + 1e-06
    white_real = (real_part / divisor).astype(jnp.bfloat16)
    white_imag = (imag_part / divisor).astype(jnp.bfloat16)
    return white_real, white_imag


def _white_kernel(x_ref, table_ref, taper_ref, out_ref):
    rows = x_ref.shape[1]
    slices = [x_ref[i] for i in range(x_ref.shape[0])]
    white_real, white_imag = _white_block(slices, table_ref[...], taper_ref[...])
    for segment in range(SEG):
        out_ref[2 * segment] = white_real[segment * rows : (segment + 1) * rows]
        out_ref[2 * segment + 1] = white_imag[segment * rows : (segment + 1) * rows]


def _cross_kernel(ids_ref, arrived_hbm, first_hbm, table_hbm, taper_ref, out_ref, arrived_ref, first_ref, table_ref, sems):
    arrived_copy = pltpu.make_async_copy(arrived_hbm, arrived_ref, sems.at[0])
    table_copy = pltpu.make_async_copy(table_hbm, table_ref, sems.at[1])
    first_copy = pltpu.make_async_copy(first_hbm, first_ref, sems.at[2])
    arrived_copy.start()
    first_copy.start()
    table_copy.start()
    buckets, slabs, capacity, width = arrived_ref.shape
    ids = ids_ref[...]
    rows = ids.shape[0]
    onehot = (lax.broadcasted_iota(jnp.int32, (rows, buckets * capacity), 1) == ids).astype(arrived_ref.dtype)
    arrived_copy.wait()
    slices = [
        jnp.dot(onehot, arrived_ref[:, s].reshape(buckets * capacity, width), preferred_element_type=jnp.float32).astype(
            arrived_ref.dtype
        )
        for s in range(slabs)
    ]
    table_copy.wait()
    white_real, white_imag = _white_block(slices, table_ref[...], taper_ref[...])
    first_copy.wait()
    real_sum = None
    imag_sum = None
    for segment in range(SEG):
        left_real = first_ref[2 * segment].astype(jnp.float32)
        left_imag = first_ref[2 * segment + 1].astype(jnp.float32)
        right_real = white_real[segment * rows : (segment + 1) * rows].astype(jnp.float32)
        right_imag = white_imag[segment * rows : (segment + 1) * rows].astype(jnp.float32)
        real_term = left_real * right_real + left_imag * right_imag
        imag_term = left_real * right_imag - left_imag * right_real
        real_sum = real_term if real_sum is None else real_sum + real_term
        imag_sum = imag_term if imag_sum is None else imag_sum + imag_term
    out_ref[:, :BINS] = (real_sum / SEG).astype(out_ref.dtype)
    out_ref[:, BINS:] = (imag_sum / SEG).astype(out_ref.dtype)


def taper_table(slabs_per_segment, width):
    position = jnp.arange(NFFT, dtype=jnp.int32).astype(jnp.float32)
    taper = 0.5 - 0.5 * jnp.cos(position * (2.0 * math.pi / NFFT))
    return taper.reshape(slabs_per_segment, width)


def _white_specs(slabs, block, width, per_segment):
    return [
        pl.BlockSpec((slabs, block, width), lambda i: (0, i, 0)),
        pl.BlockSpec((NFFT, 2 * BINS), lambda i: (0, 0), pipeline_mode=pl.Buffered(1)),
        pl.BlockSpec((per_segment, width), lambda i: (0, 0)),
    ]


def white_rows(parts, table, taper, block=128):
    slabs, rows, width = parts.shape
    specs = _white_specs(slabs, block, width, slabs // SEG)
    return pl.pallas_call(
        _white_kernel,
        out_shape=jax.ShapeDtypeStruct((2 * SEG, rows, BINS), jnp.bfloat16),
        grid=(rows // block,),
        in_specs=specs,
        out_specs=pl.BlockSpec((2 * SEG, block, BINS), lambda i: (0, i, 0)),
        compiler_params=pltpu.CompilerParams(vmem_limit_bytes=48 * 1024 * 1024),
        cost_estimate=pl.CostEstimate(
            flops=2 * SEG * rows * NFFT * 2 * BINS, transcendentals=SEG * rows * BINS,
            bytes_accessed=NFFT * 2 * BINS * 2 + 4 * slabs * rows * width,
        ),
    )(parts, table, taper)


def cross_rows(arrived, slots, first_white, table, taper):
    buckets, slabs, capacity, width = arrived.shape
    rows = slots.shape[0]
    vmem = pltpu.MemorySpace.VMEM
    return pl.pallas_call(
        _cross_kernel,
        out_shape=jax.ShapeDtypeStruct((rows, 2 * BINS), jnp.bfloat16),
        in_specs=[
            pl.BlockSpec(memory_space=vmem),
            pl.BlockSpec(memory_space=pl.ANY),
            pl.BlockSpec(memory_space=pltpu.MemorySpace.HBM),
            pl.BlockSpec(memory_space=pl.ANY),
            pl.BlockSpec(memory_space=vmem),
        ],
        out_specs=pl.BlockSpec(memory_space=vmem),
        scratch_shapes=[
            pltpu.VMEM(arrived.shape, arrived.dtype),
            pltpu.VMEM(first_white.shape, first_white.dtype),
            pltpu.VMEM(table.shape, table.dtype),
            pltpu.SemaphoreType.DMA((3,)),
        ],
        compiler_params=pltpu.CompilerParams(vmem_limit_bytes=48 * 1024 * 1024),
        cost_estimate=pl.CostEstimate(
            flops=2 * SEG * rows * NFFT * 2 * BINS, transcendentals=SEG * rows * BINS,
            bytes_accessed=NFFT * 2 * BINS * 2 + 2 * arrived.size,
        ),
    )(slots.reshape(rows, 1), arrived, first_white, table, taper)


def _exchange_kernel(axis, x_ref, out_ref, landed, send_sems, recv_sems):
    count = x_ref.shape[0]
    me = lax.axis_index(axis)

    def peer_id(peer):
        return {axis: peer}

    barrier = pltpu.get_barrier_semaphore()
    for step in range(1, count):
        pl.semaphore_signal(
            barrier, inc=1, device_id=peer_id(lax.rem(me + step, count)), device_id_type=pl.DeviceIdType.MESH
        )
    pl.semaphore_wait(barrier, count - 1)
    copies = []
    for step in range(1, count):
        peer = lax.rem(me + step, count)
        copy = pltpu.make_async_remote_copy(
            src_ref=x_ref.at[peer],
            dst_ref=landed.at[me],
            send_sem=send_sems.at[step],
            recv_sem=recv_sems.at[step],
            device_id=peer_id(peer),
            device_id_type=pl.DeviceIdType.MESH,
        )
        copy.start()
        copies.append(copy)
    landed[me] = x_ref[me]
    for copy in copies:
        copy.wait_send()
        copy.wait_recv()
    out_ref[...] = landed[...]


def exchange(parts, axis, collective):
    count = parts.shape[0]
    return pl.pallas_call(
        functools.partial(_exchange_kernel, axis),
        out_shape=jax.ShapeDtypeStruct(parts.shape, parts.dtype),
        scratch_shapes=[
            pltpu.VMEM(parts.shape, parts.dtype),
            pltpu.SemaphoreType.DMA((count,)),
            pltpu.SemaphoreType.DMA((count,)),
        ],
        compiler_params=pltpu.CompilerParams(collective_id=collective, has_side_effects=True),
        cost_estimate=pl.CostEstimate(flops=0, transcendentals=0, bytes_accessed=4 * parts.size),
    )(parts)


def to_rows(parts):
    slabs, rows, width = parts.shape
    return jnp.transpose(parts, (1, 0, 2)).reshape(rows, slabs * width)


def local(records, first_station, second_region, second_station):
    regions = lax.axis_size("region")
    slabs = lax.axis_size("slab")
    pair_count = first_station.shape[0]
    width = records.shape[1]
    capacity = max(2, pair_count // regions + pair_count // 16)

    target = second_region[:, 0]
    onehot = (target[:, None] == jnp.arange(regions, dtype=jnp.int32)[None, :]).astype(jnp.int32)
    ranking = jnp.sum((jnp.cumsum(onehot, axis=0) - onehot) * onehot, axis=1)
    slot_index = target * capacity + ranking
    requests = (
        jnp.zeros((regions * capacity,), jnp.int32)
        .at[slot_index]
        .set(second_station)
    )
    own = jnp.pad(requests.reshape(-1, 128), ((0, (-(regions * capacity // 128)) % 8), (0, 0)))
    plane = exchange(jnp.broadcast_to(own[None], (slabs,) + own.shape), "slab", 2)
    plane_requests = plane[:, : regions * capacity // 128].reshape(slabs, regions, capacity)
    outgoing = jnp.transpose(plane_requests, (1, 0, 2)).reshape(regions, -1, 128)
    outgoing = jnp.pad(outgoing, ((0, 0), (0, (-outgoing.shape[1]) % 8), (0, 0)))
    asked = exchange(outgoing, "region", 1)[:, : slabs * capacity // 128].reshape(-1)

    own_firsts = jnp.pad(first_station.reshape(-1, 128), ((0, (-(pair_count // 128)) % 8), (0, 0)))
    firsts = exchange(jnp.broadcast_to(own_firsts[None], (slabs,) + own_firsts.shape), "slab", 3)
    firsts = firsts[:, : pair_count // 128].reshape(slabs, pair_count)
    first_parts = pick_rows(records, firsts.reshape(-1)).reshape(slabs, pair_count, width)
    first_arrived = exchange(first_parts, "slab", 0)
    table = dft_table()
    taper = taper_table(slabs // SEG, width)
    first_white = white_rows(first_arrived, table, taper)

    served = pick_rows(records, asked)
    served = served.reshape(regions * slabs, capacity, width)
    arrived = lax.all_to_all(served, ("region", "slab"), split_axis=0, concat_axis=0, tiled=True)
    arrived, _ = lax.optimization_barrier((arrived, first_white[0, :8, :128]))
    first_white = pltpu.with_memory_space_constraint(first_white, pltpu.MemorySpace.HBM)
    return cross_rows(arrived.reshape(regions, slabs, capacity, width), slot_index, first_white, table, taper)

def solution(mesh):
    placed = (
        P("region", "slab"),
        P(("region", "slab")),
        P(("region", "slab"), None),
        P(("region", "slab")),
    )
    return jax.shard_map(
        local, mesh=mesh, in_specs=placed, out_specs=P(("region", "slab"), None), check_vma=False
    )
```

```python
import functools
import math

import jax
import jax.numpy as jnp
from jax import lax
from jax.experimental import pallas as pl
from jax.experimental.pallas import tpu as pltpu
from jax.sharding import PartitionSpec as P

NFFT = 2048
BINS = 1024
SEG = 2
HALF = 4


def dft_table():
    low = 64
    high = NFFT // low
    frequency = jnp.arange(BINS, dtype=jnp.int32)[None, :]
    coarse = jnp.arange(high, dtype=jnp.int32)[:, None]
    fine = jnp.arange(low, dtype=jnp.int32)[:, None]
    angle_a = ((coarse * frequency) % high).astype(jnp.float32) * (2.0 * math.pi / high)
    angle_b = ((fine * frequency) % NFFT).astype(jnp.float32) * (2.0 * math.pi / NFFT)
    ca, sa = jnp.cos(angle_a)[:, None, :], jnp.sin(angle_a)[:, None, :]
    cb, sb = jnp.cos(angle_b)[None, :, :], jnp.sin(angle_b)[None, :, :]
    cos_part = (ca * cb - sa * sb).reshape(NFFT, BINS)
    sin_part = (sa * cb + ca * sb).reshape(NFFT, BINS)
    return jnp.concatenate([cos_part, -sin_part], axis=1).astype(jnp.bfloat16)


def whitened(traces):
    count = traces.shape[0]
    signal = traces.astype(jnp.float32).reshape(count * SEG, NFFT)
    signal = signal - jnp.mean(signal, axis=1, keepdims=True)
    position = jnp.arange(NFFT, dtype=jnp.int32).astype(jnp.float32)
    taper = 0.5 - 0.5 * jnp.cos(position * (2.0 * math.pi / NFFT))
    tapered = (signal * taper[None, :]).astype(jnp.bfloat16)
    spectrum = jnp.dot(tapered, dft_table(), preferred_element_type=jnp.float32)
    real_part = spectrum[:, :BINS]
    imag_part = spectrum[:, BINS:]
    amplitude = jnp.sqrt(real_part * real_part + imag_part * imag_part + 1e-06)
    padded = jnp.pad(amplitude, ((0, 0), (HALF, HALF)))
    smooth = jnp.zeros_like(amplitude)
    for offset in range(2 * HALF + 1):
        smooth = smooth + padded[:, offset : offset + BINS]
    smooth = smooth / (2 * HALF + 1)
    level = jnp.mean(amplitude, axis=1, keepdims=True)
    divisor = smooth + level + 1e-06
    white = spectrum / jnp.concatenate([divisor, divisor], axis=1)
    return white.astype(jnp.bfloat16).reshape(count, SEG * NFFT)


def cross(first_rows, second_rows):
    left = first_rows.astype(jnp.float32).reshape(first_rows.shape[:-1] + (SEG, 2, BINS))
    right = second_rows.astype(jnp.float32).reshape(second_rows.shape[:-1] + (SEG, 2, BINS))
    real_sum = jnp.mean(
        left[..., 0, :] * right[..., 0, :] + left[..., 1, :] * right[..., 1, :], axis=-2
    )
    imag_sum = jnp.mean(
        left[..., 0, :] * right[..., 1, :] - left[..., 1, :] * right[..., 0, :], axis=-2
    )
    return jnp.concatenate([real_sum, imag_sum], axis=-1).astype(jnp.bfloat16)


def _pick_kernel(ids_ref, table_ref, out_ref):
    ids = jnp.transpose(ids_ref[...])[:, :1]
    rows = table_ref.shape[0]
    onehot = (lax.broadcasted_iota(jnp.int32, (ids.shape[0], rows), 1) == ids).astype(table_ref.dtype)
    out_ref[...] = jnp.dot(onehot, table_ref[...], preferred_element_type=jnp.float32).astype(out_ref.dtype)


def pick_rows(table, ids, block=2048):
    rows, width = table.shape
    count = ids.shape[0]
    block = min(block, count)
    return pl.pallas_call(
        _pick_kernel,
        out_shape=jax.ShapeDtypeStruct((count, width), table.dtype),
        grid=(count // block,),
        in_specs=[
            pl.BlockSpec((8, block), lambda i: (0, i)),
            pl.BlockSpec((rows, width), lambda i: (0, 0)),
        ],
        out_specs=pl.BlockSpec((block, width), lambda i: (i, 0)),
        cost_estimate=pl.CostEstimate(
            flops=2 * count * rows * width, transcendentals=0, bytes_accessed=2 * (rows + count) * width
        ),
    )(jnp.broadcast_to(ids[None, :], (8, count)), table)


def _compact_kernel(ids_ref, table_ref, out_ref):
    buckets, slabs, capacity, width = table_ref.shape
    for s in range(slabs):
        ids = ids_ref[s]
        table = table_ref[:, s].reshape(buckets * capacity, width)
        onehot = (lax.broadcasted_iota(jnp.int32, (ids.shape[0], buckets * capacity), 1) == ids).astype(table.dtype)
        out_ref[s] = jnp.dot(onehot, table, preferred_element_type=jnp.float32).astype(out_ref.dtype)


def compact_rows(arrived, slots):
    buckets, slabs, capacity, width = arrived.shape
    pairs = slots.shape[1]
    return pl.pallas_call(
        _compact_kernel,
        out_shape=jax.ShapeDtypeStruct((slabs, pairs, width), arrived.dtype),
        cost_estimate=pl.CostEstimate(
            flops=2 * slabs * pairs * buckets * capacity * width,
            transcendentals=0,
            bytes_accessed=2 * (buckets * capacity + pairs) * slabs * width,
        ),
    )(slots.reshape(slabs, pairs, 1), arrived)


def _white_block(slices, table, taper):
    per_segment = len(slices) // SEG
    tapered = []
    for segment in range(SEG):
        part = [piece.astype(jnp.float32) for piece in slices[segment * per_segment : (segment + 1) * per_segment]]
        total = jnp.sum(part[0], axis=1, keepdims=True)
        for piece in part[1:]:
            total = total + jnp.sum(piece, axis=1, keepdims=True)
        mean = total / NFFT
        pieces = [((part[i] - mean) * taper[i : i + 1, :]).astype(jnp.bfloat16) for i in range(per_segment)]
        tapered.append(jnp.concatenate(pieces, axis=1))
    spectrum = jnp.dot(jnp.concatenate(tapered, axis=0), table, preferred_element_type=jnp.float32)
    real_part = spectrum[:, :BINS]
    imag_part = spectrum[:, BINS:]
    amplitude = jnp.sqrt(real_part * real_part + imag_part * imag_part + 1e-06)
    lane = lax.broadcasted_iota(jnp.int32, amplitude.shape, 1)
    smooth = jnp.zeros_like(amplitude)
    for offset in range(-HALF, HALF + 1):
        moved = amplitude if offset == 0 else pltpu.roll(amplitude, (-offset) % BINS, 1)
        inside = (lane + offset >= 0) & (lane + offset < BINS)
        smooth = smooth + jnp.where(inside, moved, 0.0)
    smooth = smooth / (2 * HALF + 1)
    level = jnp.sum(amplitude, axis=1, keepdims=True) / BINS
    divisor = smooth + level + 1e-06
    white_real = (real_part / divisor).astype(jnp.bfloat16)
    white_imag = (imag_part / divisor).astype(jnp.bfloat16)
    return white_real, white_imag


def _white_kernel(x_ref, table_ref, taper_ref, out_ref):
    rows = x_ref.shape[1]
    slices = [x_ref[i] for i in range(x_ref.shape[0])]
    white_real, white_imag = _white_block(slices, table_ref[...], taper_ref[...])
    for segment in range(SEG):
        out_ref[2 * segment] = white_real[segment * rows : (segment + 1) * rows]
        out_ref[2 * segment + 1] = white_imag[segment * rows : (segment + 1) * rows]


def _cross_kernel(ids_ref, arrived_hbm, first_hbm, table_hbm, taper_ref, out_ref, arrived_ref, first_ref, table_ref, sems):
    arrived_copy = pltpu.make_async_copy(arrived_hbm, arrived_ref, sems.at[0])
    table_copy = pltpu.make_async_copy(table_hbm, table_ref, sems.at[1])
    first_copy = pltpu.make_async_copy(first_hbm, first_ref, sems.at[2])
    arrived_copy.start()
    first_copy.start()
    table_copy.start()
    buckets, slabs, capacity, width = arrived_ref.shape
    ids = ids_ref[...]
    rows = ids.shape[0]
    onehot = (lax.broadcasted_iota(jnp.int32, (rows, buckets * capacity), 1) == ids).astype(arrived_ref.dtype)
    arrived_copy.wait()
    slices = [
        jnp.dot(onehot, arrived_ref[:, s].reshape(buckets * capacity, width), preferred_element_type=jnp.float32).astype(
            arrived_ref.dtype
        )
        for s in range(slabs)
    ]
    table_copy.wait()
    white_real, white_imag = _white_block(slices, table_ref[...], taper_ref[...])
    first_copy.wait()
    real_sum = None
    imag_sum = None
    for segment in range(SEG):
        left_real = first_ref[2 * segment].astype(jnp.float32)
        left_imag = first_ref[2 * segment + 1].astype(jnp.float32)
        right_real = white_real[segment * rows : (segment + 1) * rows].astype(jnp.float32)
        right_imag = white_imag[segment * rows : (segment + 1) * rows].astype(jnp.float32)
        real_term = left_real * right_real + left_imag * right_imag
        imag_term = left_real * right_imag - left_imag * right_real
        real_sum = real_term if real_sum is None else real_sum + real_term
        imag_sum = imag_term if imag_sum is None else imag_sum + imag_term
    out_ref[:, :BINS] = (real_sum / SEG).astype(out_ref.dtype)
    out_ref[:, BINS:] = (imag_sum / SEG).astype(out_ref.dtype)


def taper_table(slabs_per_segment, width):
    position = jnp.arange(NFFT, dtype=jnp.int32).astype(jnp.float32)
    taper = 0.5 - 0.5 * jnp.cos(position * (2.0 * math.pi / NFFT))
    return taper.reshape(slabs_per_segment, width)


def _white_specs(slabs, block, width, per_segment):
    return [
        pl.BlockSpec((slabs, block, width), lambda i: (0, i, 0)),
        pl.BlockSpec((NFFT, 2 * BINS), lambda i: (0, 0), pipeline_mode=pl.Buffered(1)),
        pl.BlockSpec((per_segment, width), lambda i: (0, 0)),
    ]


def white_rows(parts, table, taper, block=128):
    slabs, rows, width = parts.shape
    specs = _white_specs(slabs, block, width, slabs // SEG)
    return pl.pallas_call(
        _white_kernel,
        out_shape=jax.ShapeDtypeStruct((2 * SEG, rows, BINS), jnp.bfloat16),
        grid=(rows // block,),
        in_specs=specs,
        out_specs=pl.BlockSpec((2 * SEG, block, BINS), lambda i: (0, i, 0)),
        compiler_params=pltpu.CompilerParams(vmem_limit_bytes=48 * 1024 * 1024),
        cost_estimate=pl.CostEstimate(
            flops=2 * SEG * rows * NFFT * 2 * BINS, transcendentals=SEG * rows * BINS,
            bytes_accessed=NFFT * 2 * BINS * 2 + 4 * slabs * rows * width,
        ),
    )(parts, table, taper)


def cross_rows(arrived, slots, first_white, table, taper):
    buckets, slabs, capacity, width = arrived.shape
    rows = slots.shape[0]
    vmem = pltpu.MemorySpace.VMEM
    return pl.pallas_call(
        _cross_kernel,
        out_shape=jax.ShapeDtypeStruct((rows, 2 * BINS), jnp.bfloat16),
        in_specs=[
            pl.BlockSpec(memory_space=vmem),
            pl.BlockSpec(memory_space=pl.ANY),
            pl.BlockSpec(memory_space=pltpu.MemorySpace.HBM),
            pl.BlockSpec(memory_space=pl.ANY),
            pl.BlockSpec(memory_space=vmem),
        ],
        out_specs=pl.BlockSpec(memory_space=vmem),
        scratch_shapes=[
            pltpu.VMEM(arrived.shape, arrived.dtype),
            pltpu.VMEM(first_white.shape, first_white.dtype),
            pltpu.VMEM(table.shape, table.dtype),
            pltpu.SemaphoreType.DMA((3,)),
        ],
        compiler_params=pltpu.CompilerParams(vmem_limit_bytes=48 * 1024 * 1024),
        cost_estimate=pl.CostEstimate(
            flops=2 * SEG * rows * NFFT * 2 * BINS, transcendentals=SEG * rows * BINS,
            bytes_accessed=NFFT * 2 * BINS * 2 + 2 * arrived.size,
        ),
    )(slots.reshape(rows, 1), arrived, first_white, table, taper)


def _exchange_kernel(axis, x_ref, out_ref, landed, send_sems, recv_sems):
    count = x_ref.shape[0]
    me = lax.axis_index(axis)

    def peer_id(peer):
        return {axis: peer}

    barrier = pltpu.get_barrier_semaphore()
    for step in range(1, count):
        pl.semaphore_signal(
            barrier, inc=1, device_id=peer_id(lax.rem(me + step, count)), device_id_type=pl.DeviceIdType.MESH
        )
    pl.semaphore_wait(barrier, count - 1)
    copies = []
    for step in range(1, count):
        peer = lax.rem(me + step, count)
        copy = pltpu.make_async_remote_copy(
            src_ref=x_ref.at[peer],
            dst_ref=landed.at[me],
            send_sem=send_sems.at[step],
            recv_sem=recv_sems.at[step],
            device_id=peer_id(peer),
            device_id_type=pl.DeviceIdType.MESH,
        )
        copy.start()
        copies.append(copy)
    landed[me] = x_ref[me]
    for copy in copies:
        copy.wait_send()
        copy.wait_recv()
    out_ref[...] = landed[...]


def exchange(parts, axis, collective):
    count = parts.shape[0]
    return pl.pallas_call(
        functools.partial(_exchange_kernel, axis),
        out_shape=jax.ShapeDtypeStruct(parts.shape, parts.dtype),
        scratch_shapes=[
            pltpu.VMEM(parts.shape, parts.dtype),
            pltpu.SemaphoreType.DMA((count,)),
            pltpu.SemaphoreType.DMA((count,)),
        ],
        compiler_params=pltpu.CompilerParams(collective_id=collective, has_side_effects=True),
        cost_estimate=pl.CostEstimate(flops=0, transcendentals=0, bytes_accessed=4 * parts.size),
    )(parts)


def to_rows(parts):
    slabs, rows, width = parts.shape
    return jnp.transpose(parts, (1, 0, 2)).reshape(rows, slabs * width)


def local(records, first_station, second_region, second_station):
    regions = lax.axis_size("region")
    slabs = lax.axis_size("slab")
    pair_count = first_station.shape[0]
    width = records.shape[1]
    capacity = max(2, pair_count // regions + pair_count // 16)

    target = second_region[:, 0]
    onehot = (target[:, None] == jnp.arange(regions, dtype=jnp.int32)[None, :]).astype(jnp.int32)
    ranking = jnp.sum((jnp.cumsum(onehot, axis=0) - onehot) * onehot, axis=1)
    slot_index = target * capacity + ranking
    requests = (
        jnp.zeros((regions * capacity,), jnp.int32)
        .at[slot_index]
        .set(second_station)
    )
    own = jnp.pad(requests.reshape(-1, 128), ((0, (-(regions * capacity // 128)) % 8), (0, 0)))
    plane = exchange(jnp.broadcast_to(own[None], (slabs,) + own.shape), "slab", 2)
    plane_requests = plane[:, : regions * capacity // 128].reshape(slabs, regions, capacity)
    outgoing = jnp.transpose(plane_requests, (1, 0, 2)).reshape(regions, -1, 128)
    outgoing = jnp.pad(outgoing, ((0, 0), (0, (-outgoing.shape[1]) % 8), (0, 0)))
    asked = exchange(outgoing, "region", 1)[:, : slabs * capacity // 128].reshape(-1)

    own_firsts = jnp.pad(first_station.reshape(-1, 128), ((0, (-(pair_count // 128)) % 8), (0, 0)))
    firsts = exchange(jnp.broadcast_to(own_firsts[None], (slabs,) + own_firsts.shape), "slab", 3)
    firsts = firsts[:, : pair_count // 128].reshape(slabs, pair_count)
    first_parts = pick_rows(records, firsts.reshape(-1)).reshape(slabs, pair_count, width)
    first_arrived = exchange(first_parts, "slab", 0)
    table = dft_table()
    taper = taper_table(slabs // SEG, width)
    first_white = white_rows(first_arrived, table, taper)

    served = pick_rows(records, asked)
    served = served.reshape(regions * slabs, capacity, width)
    arrived = lax.all_to_all(served, ("region", "slab"), split_axis=0, concat_axis=0, tiled=True)
    arrived, _ = lax.optimization_barrier((arrived, first_white[0, :8, :128]))
    first_white = pltpu.with_memory_space_constraint(first_white, pltpu.MemorySpace.HBM)
    return cross_rows(arrived.reshape(regions, slabs, capacity, width), slot_index, first_white, table, taper)

def solution(mesh):
    placed = (
        P("region", "slab"),
        P(("region", "slab")),
        P(("region", "slab"), None),
        P(("region", "slab")),
    )
    return jax.shard_map(
        local, mesh=mesh, in_specs=placed, out_specs=P(("region", "slab"), None), check_vma=False
    )
```

```python
import functools
import math

import jax
import jax.numpy as jnp
from jax import lax
from jax.experimental import pallas as pl
from jax.experimental.pallas import tpu as pltpu
from jax.sharding import PartitionSpec as P

NFFT = 2048
BINS = 1024
SEG = 2
HALF = 4


def dft_table():
    low = 64
    high = NFFT // low
    frequency = jnp.arange(BINS, dtype=jnp.int32)[None, :]
    coarse = jnp.arange(high, dtype=jnp.int32)[:, None]
    fine = jnp.arange(low, dtype=jnp.int32)[:, None]
    angle_a = ((coarse * frequency) % high).astype(jnp.float32) * (2.0 * math.pi / high)
    angle_b = ((fine * frequency) % NFFT).astype(jnp.float32) * (2.0 * math.pi / NFFT)
    ca, sa = jnp.cos(angle_a)[:, None, :], jnp.sin(angle_a)[:, None, :]
    cb, sb = jnp.cos(angle_b)[None, :, :], jnp.sin(angle_b)[None, :, :]
    cos_part = (ca * cb - sa * sb).reshape(NFFT, BINS)
    sin_part = (sa * cb + ca * sb).reshape(NFFT, BINS)
    return jnp.concatenate([cos_part, -sin_part], axis=1).astype(jnp.bfloat16)


def whitened(traces):
    count = traces.shape[0]
    signal = traces.astype(jnp.float32).reshape(count * SEG, NFFT)
    signal = signal - jnp.mean(signal, axis=1, keepdims=True)
    position = jnp.arange(NFFT, dtype=jnp.int32).astype(jnp.float32)
    taper = 0.5 - 0.5 * jnp.cos(position * (2.0 * math.pi / NFFT))
    tapered = (signal * taper[None, :]).astype(jnp.bfloat16)
    spectrum = jnp.dot(tapered, dft_table(), preferred_element_type=jnp.float32)
    real_part = spectrum[:, :BINS]
    imag_part = spectrum[:, BINS:]
    amplitude = jnp.sqrt(real_part * real_part + imag_part * imag_part + 1e-06)
    padded = jnp.pad(amplitude, ((0, 0), (HALF, HALF)))
    smooth = jnp.zeros_like(amplitude)
    for offset in range(2 * HALF + 1):
        smooth = smooth + padded[:, offset : offset + BINS]
    smooth = smooth / (2 * HALF + 1)
    level = jnp.mean(amplitude, axis=1, keepdims=True)
    divisor = smooth + level + 1e-06
    white = spectrum / jnp.concatenate([divisor, divisor], axis=1)
    return white.astype(jnp.bfloat16).reshape(count, SEG * NFFT)


def cross(first_rows, second_rows):
    left = first_rows.astype(jnp.float32).reshape(first_rows.shape[:-1] + (SEG, 2, BINS))
    right = second_rows.astype(jnp.float32).reshape(second_rows.shape[:-1] + (SEG, 2, BINS))
    real_sum = jnp.mean(
        left[..., 0, :] * right[..., 0, :] + left[..., 1, :] * right[..., 1, :], axis=-2
    )
    imag_sum = jnp.mean(
        left[..., 0, :] * right[..., 1, :] - left[..., 1, :] * right[..., 0, :], axis=-2
    )
    return jnp.concatenate([real_sum, imag_sum], axis=-1).astype(jnp.bfloat16)


def _pick_kernel(ids_ref, table_ref, out_ref):
    ids = ids_ref[...]
    rows = table_ref.shape[0]
    onehot = (lax.broadcasted_iota(jnp.int32, (ids.shape[0], rows), 1) == ids).astype(table_ref.dtype)
    out_ref[...] = jnp.dot(onehot, table_ref[...], preferred_element_type=jnp.float32).astype(out_ref.dtype)


def pick_rows(table, ids, block=4096):
    rows, width = table.shape
    count = ids.shape[0]
    block = min(block, count)
    return pl.pallas_call(
        _pick_kernel,
        out_shape=jax.ShapeDtypeStruct((count, width), table.dtype),
        grid=(count // block,),
        in_specs=[
            pl.BlockSpec((block, 1), lambda i: (i, 0)),
            pl.BlockSpec((rows, width), lambda i: (0, 0)),
        ],
        out_specs=pl.BlockSpec((block, width), lambda i: (i, 0)),
        cost_estimate=pl.CostEstimate(
            flops=2 * count * rows * width, transcendentals=0, bytes_accessed=2 * (rows + count) * width
        ),
    )(ids.reshape(count, 1), table)


def _compact_kernel(ids_ref, table_ref, out_ref):
    buckets, slabs, capacity, width = table_ref.shape
    for s in range(slabs):
        ids = ids_ref[s]
        table = table_ref[:, s].reshape(buckets * capacity, width)
        onehot = (lax.broadcasted_iota(jnp.int32, (ids.shape[0], buckets * capacity), 1) == ids).astype(table.dtype)
        out_ref[s] = jnp.dot(onehot, table, preferred_element_type=jnp.float32).astype(out_ref.dtype)


def compact_rows(arrived, slots):
    buckets, slabs, capacity, width = arrived.shape
    pairs = slots.shape[1]
    return pl.pallas_call(
        _compact_kernel,
        out_shape=jax.ShapeDtypeStruct((slabs, pairs, width), arrived.dtype),
        cost_estimate=pl.CostEstimate(
            flops=2 * slabs * pairs * buckets * capacity * width,
            transcendentals=0,
            bytes_accessed=2 * (buckets * capacity + pairs) * slabs * width,
        ),
    )(slots.reshape(slabs, pairs, 1), arrived)


def _white_block(slices, table, taper):
    per_segment = len(slices) // SEG
    tapered = []
    for segment in range(SEG):
        part = [piece.astype(jnp.float32) for piece in slices[segment * per_segment : (segment + 1) * per_segment]]
        total = jnp.sum(part[0], axis=1, keepdims=True)
        for piece in part[1:]:
            total = total + jnp.sum(piece, axis=1, keepdims=True)
        mean = total / NFFT
        pieces = [((part[i] - mean) * taper[i : i + 1, :]).astype(jnp.bfloat16) for i in range(per_segment)]
        tapered.append(jnp.concatenate(pieces, axis=1))
    spectrum = jnp.dot(jnp.concatenate(tapered, axis=0), table, preferred_element_type=jnp.float32)
    real_part = spectrum[:, :BINS]
    imag_part = spectrum[:, BINS:]
    amplitude = jnp.sqrt(real_part * real_part + imag_part * imag_part + 1e-06)
    lane = lax.broadcasted_iota(jnp.int32, amplitude.shape, 1)
    smooth = jnp.zeros_like(amplitude)
    for offset in range(-HALF, HALF + 1):
        moved = amplitude if offset == 0 else pltpu.roll(amplitude, (-offset) % BINS, 1)
        inside = (lane + offset >= 0) & (lane + offset < BINS)
        smooth = smooth + jnp.where(inside, moved, 0.0)
    smooth = smooth / (2 * HALF + 1)
    level = jnp.sum(amplitude, axis=1, keepdims=True) / BINS
    divisor = smooth + level + 1e-06
    white_real = (real_part / divisor).astype(jnp.bfloat16)
    white_imag = (imag_part / divisor).astype(jnp.bfloat16)
    return white_real, white_imag


def _white_kernel(x_ref, table_ref, taper_ref, out_ref):
    rows = x_ref.shape[1]
    slices = [x_ref[i] for i in range(x_ref.shape[0])]
    white_real, white_imag = _white_block(slices, table_ref[...], taper_ref[...])
    for segment in range(SEG):
        out_ref[2 * segment] = white_real[segment * rows : (segment + 1) * rows]
        out_ref[2 * segment + 1] = white_imag[segment * rows : (segment + 1) * rows]


def _cross_kernel(ids_ref, arrived_hbm, first_hbm, table_hbm, taper_ref, out_ref, arrived_ref, first_ref, table_ref, sems):
    arrived_copy = pltpu.make_async_copy(arrived_hbm, arrived_ref, sems.at[0])
    table_copy = pltpu.make_async_copy(table_hbm, table_ref, sems.at[1])
    first_copy = pltpu.make_async_copy(first_hbm, first_ref, sems.at[2])
    arrived_copy.start()
    first_copy.start()
    table_copy.start()
    buckets, slabs, capacity, width = arrived_ref.shape
    ids = ids_ref[...]
    rows = ids.shape[0]
    onehot = (lax.broadcasted_iota(jnp.int32, (rows, buckets * capacity), 1) == ids).astype(arrived_ref.dtype)
    arrived_copy.wait()
    slices = [
        jnp.dot(onehot, arrived_ref[:, s].reshape(buckets * capacity, width), preferred_element_type=jnp.float32).astype(
            arrived_ref.dtype
        )
        for s in range(slabs)
    ]
    table_copy.wait()
    white_real, white_imag = _white_block(slices, table_ref[...], taper_ref[...])
    first_copy.wait()
    real_sum = None
    imag_sum = None
    for segment in range(SEG):
        left_real = first_ref[2 * segment].astype(jnp.float32)
        left_imag = first_ref[2 * segment + 1].astype(jnp.float32)
        right_real = white_real[segment * rows : (segment + 1) * rows].astype(jnp.float32)
        right_imag = white_imag[segment * rows : (segment + 1) * rows].astype(jnp.float32)
        real_term = left_real * right_real + left_imag * right_imag
        imag_term = left_real * right_imag - left_imag * right_real
        real_sum = real_term if real_sum is None else real_sum + real_term
        imag_sum = imag_term if imag_sum is None else imag_sum + imag_term
    out_ref[:, :BINS] = (real_sum / SEG).astype(out_ref.dtype)
    out_ref[:, BINS:] = (imag_sum / SEG).astype(out_ref.dtype)


def taper_table(slabs_per_segment, width):
    position = jnp.arange(NFFT, dtype=jnp.int32).astype(jnp.float32)
    taper = 0.5 - 0.5 * jnp.cos(position * (2.0 * math.pi / NFFT))
    return taper.reshape(slabs_per_segment, width)


def _white_specs(slabs, block, width, per_segment):
    return [
        pl.BlockSpec((slabs, block, width), lambda i: (0, i, 0)),
        pl.BlockSpec((NFFT, 2 * BINS), lambda i: (0, 0), pipeline_mode=pl.Buffered(1)),
        pl.BlockSpec((per_segment, width), lambda i: (0, 0)),
    ]


def white_rows(parts, table, taper, block=128):
    slabs, rows, width = parts.shape
    specs = _white_specs(slabs, block, width, slabs // SEG)
    return pl.pallas_call(
        _white_kernel,
        out_shape=jax.ShapeDtypeStruct((2 * SEG, rows, BINS), jnp.bfloat16),
        grid=(rows // block,),
        in_specs=specs,
        out_specs=pl.BlockSpec((2 * SEG, block, BINS), lambda i: (0, i, 0)),
        compiler_params=pltpu.CompilerParams(vmem_limit_bytes=48 * 1024 * 1024),
        cost_estimate=pl.CostEstimate(
            flops=2 * SEG * rows * NFFT * 2 * BINS, transcendentals=SEG * rows * BINS,
            bytes_accessed=NFFT * 2 * BINS * 2 + 4 * slabs * rows * width,
        ),
    )(parts, table, taper)


def cross_rows(arrived, slots, first_white, table, taper):
    buckets, slabs, capacity, width = arrived.shape
    rows = slots.shape[0]
    vmem = pltpu.MemorySpace.VMEM
    return pl.pallas_call(
        _cross_kernel,
        out_shape=jax.ShapeDtypeStruct((rows, 2 * BINS), jnp.bfloat16),
        in_specs=[
            pl.BlockSpec(memory_space=vmem),
            pl.BlockSpec(memory_space=pl.ANY),
            pl.BlockSpec(memory_space=pltpu.MemorySpace.HBM),
            pl.BlockSpec(memory_space=pl.ANY),
            pl.BlockSpec(memory_space=vmem),
        ],
        out_specs=pl.BlockSpec(memory_space=vmem),
        scratch_shapes=[
            pltpu.VMEM(arrived.shape, arrived.dtype),
            pltpu.VMEM(first_white.shape, first_white.dtype),
            pltpu.VMEM(table.shape, table.dtype),
            pltpu.SemaphoreType.DMA((3,)),
        ],
        compiler_params=pltpu.CompilerParams(vmem_limit_bytes=48 * 1024 * 1024),
        cost_estimate=pl.CostEstimate(
            flops=2 * SEG * rows * NFFT * 2 * BINS, transcendentals=SEG * rows * BINS,
            bytes_accessed=NFFT * 2 * BINS * 2 + 2 * arrived.size,
        ),
    )(slots.reshape(rows, 1), arrived, first_white, table, taper)


def _exchange_kernel(axis, x_ref, out_ref, landed, send_sems, recv_sems):
    count = x_ref.shape[0]
    me = lax.axis_index(axis)

    def peer_id(peer):
        return {axis: peer}

    barrier = pltpu.get_barrier_semaphore()
    for step in range(1, count):
        pl.semaphore_signal(
            barrier, inc=1, device_id=peer_id(lax.rem(me + step, count)), device_id_type=pl.DeviceIdType.MESH
        )
    pl.semaphore_wait(barrier, count - 1)
    copies = []
    for step in range(1, count):
        peer = lax.rem(me + step, count)
        copy = pltpu.make_async_remote_copy(
            src_ref=x_ref.at[peer],
            dst_ref=landed.at[me],
            send_sem=send_sems.at[step],
            recv_sem=recv_sems.at[step],
            device_id=peer_id(peer),
            device_id_type=pl.DeviceIdType.MESH,
        )
        copy.start()
        copies.append(copy)
    landed[me] = x_ref[me]
    for copy in copies:
        copy.wait_send()
        copy.wait_recv()
    out_ref[...] = landed[...]


def exchange(parts, axis, collective):
    count = parts.shape[0]
    return pl.pallas_call(
        functools.partial(_exchange_kernel, axis),
        out_shape=jax.ShapeDtypeStruct(parts.shape, parts.dtype),
        scratch_shapes=[
            pltpu.VMEM(parts.shape, parts.dtype),
            pltpu.SemaphoreType.DMA((count,)),
            pltpu.SemaphoreType.DMA((count,)),
        ],
        compiler_params=pltpu.CompilerParams(collective_id=collective, has_side_effects=True),
        cost_estimate=pl.CostEstimate(flops=0, transcendentals=0, bytes_accessed=4 * parts.size),
    )(parts)


def to_rows(parts):
    slabs, rows, width = parts.shape
    return jnp.transpose(parts, (1, 0, 2)).reshape(rows, slabs * width)


def local(records, first_station, second_region, second_station):
    regions = lax.axis_size("region")
    slabs = lax.axis_size("slab")
    pair_count = first_station.shape[0]
    width = records.shape[1]
    capacity = max(2, pair_count // regions + pair_count // 16)

    target = second_region[:, 0]
    onehot = (target[:, None] == jnp.arange(regions, dtype=jnp.int32)[None, :]).astype(jnp.int32)
    ranking = jnp.sum((jnp.cumsum(onehot, axis=0) - onehot) * onehot, axis=1)
    slot_index = target * capacity + ranking
    requests = (
        jnp.zeros((regions * capacity,), jnp.int32)
        .at[slot_index]
        .set(second_station)
    )
    own = jnp.pad(requests.reshape(-1, 128), ((0, (-(regions * capacity // 128)) % 8), (0, 0)))
    plane = exchange(jnp.broadcast_to(own[None], (slabs,) + own.shape), "slab", 2)
    plane_requests = plane[:, : regions * capacity // 128].reshape(slabs, regions, capacity)
    outgoing = jnp.transpose(plane_requests, (1, 0, 2)).reshape(regions, -1, 128)
    outgoing = jnp.pad(outgoing, ((0, 0), (0, (-outgoing.shape[1]) % 8), (0, 0)))
    asked = exchange(outgoing, "region", 1)[:, : slabs * capacity // 128].reshape(-1)

    firsts = lax.all_gather(first_station, "slab", axis=0, tiled=False)
    first_parts = pick_rows(records, firsts.reshape(-1)).reshape(slabs, pair_count, width)
    first_arrived = exchange(first_parts, "slab", 0)
    table = dft_table()
    taper = taper_table(slabs // SEG, width)
    first_white = white_rows(first_arrived, table, taper)

    served = pick_rows(records, asked)
    served = served.reshape(regions * slabs, capacity, width)
    arrived = lax.all_to_all(served, ("region", "slab"), split_axis=0, concat_axis=0, tiled=True)
    arrived, _ = lax.optimization_barrier((arrived, first_white[0, :8, :128]))
    first_white = pltpu.with_memory_space_constraint(first_white, pltpu.MemorySpace.HBM)
    return cross_rows(arrived.reshape(regions, slabs, capacity, width), slot_index, first_white, table, taper)

def solution(mesh):
    placed = (
        P("region", "slab"),
        P(("region", "slab")),
        P(("region", "slab"), None),
        P(("region", "slab")),
    )
    return jax.shard_map(
        local, mesh=mesh, in_specs=placed, out_specs=P(("region", "slab"), None), check_vma=False
    )
```
